32 devices in a mesh: aa: 4 (over y, core), ba: 8 (over z, x).
Axes of the slice: x: 2, y: 2, z: 4, core: 2. Of those that a mesh axis runs over, the one named last changes fastest.
Arguments:
- state: float32 [14, 8, 16, 128], P(None, 'ba', 'aa'), as said below
- labels: int32 [8, 16, 128], P('ba', 'aa'), may hold values from 0 to 2, as said below
Outputs:
- swept: float32 [14, 8, 16, 128], P(None, 'ba', 'aa')
The draws below stay inside these ranges and needn't reach their ends.
Inputs may be any that keep to these rules, and one draw needn't show every extreme that they name: `labels`: void cells lie in a band of low y and in scattered pores; projectile cells form one box inside the band. `state`: density is positive; inverse deformation gradients lie within 0.6 of the identity in every entry.
All inputs are finite; a program needn't handle non-finite values.
Results may differ from the reference program's by a relative error of at most 0.0003.
Values sent between devices are 32-bit elements; how exact they have to be, the bound alone decides.
No kernel may reach another device: no remote copies, remote signals or barrier semaphores. Data moves between devices by JAX's collectives and lax.ppermute only.
A program may use at most 64 MiB of HBM per device.

```python
import jax
import jax.numpy as jnp
from jax import lax

NX = 128
RETURN_ITERS = 2
NY = 16
NZ = 8


GAMMA_TABLE = (3.0, 4.0, 1.4)


STIFF_TABLE = (1.0, 6.0, 0.0)


SHEAR_TABLE = (0.6, 3.0, 0.0)


def layout(key):
    zone = jax.random.fold_in(key, 11)
    keys = jax.random.split(zone, 4)
    depth = jax.random.randint(keys[0], (), NY // 4, NY // 2 + 1)
    tall = max(NY // 8, 2)
    broad = max(NX // 8, 2)
    top = jax.random.randint(keys[1], (), 0, depth - tall + 1)
    start = jax.random.randint(keys[2], (), 0, NX - broad + 1)
    row_index = lax.broadcasted_iota(jnp.int32, (NZ, NY, NX), 1)
    column_index = lax.broadcasted_iota(jnp.int32, (NZ, NY, NX), 2)
    pores = jax.random.randint(keys[3], (NZ, NY, NX), 0, 8) == 0
    inside = (row_index >= top) & (row_index < top + tall) & (column_index >= start) & (column_index < start + broad)
    return jnp.where(inside, 1, jnp.where((row_index < depth) | pores, 2, 0)).astype(jnp.int32)


def draw_labels(key, part):
    return layout(key)


def draw_state(key, part):
    labels = layout(key)
    sandy = labels == 0
    solid = labels == 1
    shape = (NZ, NY, NX)
    keys = jax.random.split(jax.random.fold_in(key, 23), 8)

    def spread(subkey, low, high):
        return jnp.exp(jax.random.uniform(subkey, shape, jnp.float32, jnp.log(low), jnp.log(high)))

    def pick(table):
        return jnp.where(sandy, table[0], jnp.where(solid, table[1], table[2]))
    density = jnp.where(sandy, spread(keys[0], 1.2, 2.4), jnp.where(solid, spread(keys[1], 6.0, 9.0), spread(keys[2], 0.05, 0.3)))
    pressure = spread(keys[3], 0.5, 2.0)
    velocity = 0.2 * jax.random.normal(keys[4], (3,) + shape, jnp.float32)
    faint = (labels == 2) & (jax.random.randint(keys[6], shape, 0, 8) == 0)
    pressure = jnp.where(faint, spread(keys[7], 0.01, 0.08), pressure)
    velocity = velocity.at[1].add(jnp.where(solid, 3.0, 0.0))
    amplitude = jnp.where(labels == 2, 0.02, 0.08)
    noise = jnp.clip(jax.random.normal(keys[5], (9,) + shape, jnp.float32), -6.0, 6.0) * amplitude
    gradient = [[noise[3 * row + col] + (1.0 if row == col else 0.0) for col in range(3)] for row in range(3)]
    metric = [[sum((gradient[row][first] * gradient[row][second] for row in range(3))) for second in range(3)] for first in range(3)]
    third = (metric[0][0] + metric[1][1] + metric[2][2]) / 3.0
    shear = pick(SHEAR_TABLE)
    elastic = 0.25 * shear * sum(((metric[first][second] - (third if first == second else 0.0)) ** 2 for first in range(3) for second in range(3)))
    gamma = pick(GAMMA_TABLE)
    stiff = pick(STIFF_TABLE)
    kinetic = 0.5 * density * (velocity[0] ** 2 + velocity[1] ** 2 + velocity[2] ** 2)
    total = kinetic + elastic + (pressure + gamma * stiff) / (gamma - 1.0)
    fields = [density] + [density * velocity[comp] for comp in range(3)] + [total] + [gradient[row][col] for row in range(3) for col in range(3)]
    return jnp.stack(fields).astype(jnp.float32)


def setup_inputs(seed: int = 0) -> dict:
    streams_of = jax.random.split(jax.random.key(seed), 3)
    return {
        "state": draw_state(jax.random.fold_in(streams_of[2], 71), 0),
        "labels": draw_labels(jax.random.fold_in(streams_of[2], 71), 0),
    }


GAMMA_TABLE = (3.0, 4.0, 1.4)
STIFF_TABLE = (1.0, 6.0, 0.0)
SHEAR_TABLE = (0.6, 3.0, 0.0)
COHESION_TABLE = (0.05, 0.0, 0.0)
FRICTION_TABLE = (0.4, 0.0, 0.0)
DENSITY_FLOOR = 0.2
TRACTION_FLOOR = 0.1
COURANT = 0.4
WENO_EPSILON = 1e-06

def material(label):

    def pick(table):
        return jnp.where(label == 0, table[0], jnp.where(label == 1, table[1], table[2]))
    return (pick(GAMMA_TABLE), pick(STIFF_TABLE), pick(SHEAR_TABLE), pick(COHESION_TABLE), pick(FRICTION_TABLE))

def deviator(gradient, shear):
    metric = [[sum((gradient[row][first] * gradient[row][second] for row in range(3))) for second in range(3)] for first in range(3)]
    third = (metric[0][0] + metric[1][1] + metric[2][2]) / 3.0
    devs = [[metric[first][second] - (third if first == second else 0.0) for second in range(3)] for first in range(3)]
    stress = [[-shear * devs[first][second] for second in range(3)] for first in range(3)]
    energy = 0.25 * shear * sum((devs[first][second] * devs[first][second] for first in range(3) for second in range(3)))
    return (stress, energy)

def primitives(fields, label):
    gamma, stiff, shear, cohesion, friction = material(label)
    density = jnp.maximum(fields[0], DENSITY_FLOOR)
    velocity = [fields[1 + comp] / density for comp in range(3)]
    gradient = [[fields[5 + 3 * row + col] for col in range(3)] for row in range(3)]
    stress, energy = deviator(gradient, shear)
    kinetic = 0.5 * (fields[1] * velocity[0] + fields[2] * velocity[1] + fields[3] * velocity[2])
    pressure = (gamma - 1.0) * (fields[4] - kinetic - energy) - gamma * stiff
    sound = jnp.sqrt((gamma * jnp.maximum(pressure + stiff, TRACTION_FLOOR) + 4.0 / 3.0 * shear) / density)
    return (density, velocity, gradient, stress, pressure, sound)

def weno_face(first, second, centre, fourth, fifth):
    cand_a = (2.0 * first - 7.0 * second + 11.0 * centre) / 6.0
    cand_b = (-second + 5.0 * centre + 2.0 * fourth) / 6.0
    cand_c = (2.0 * centre + 5.0 * fourth - fifth) / 6.0
    rough_a = 13.0 / 12.0 * (first - 2.0 * second + centre) ** 2 + 0.25 * (first - 4.0 * second + 3.0 * centre) ** 2
    rough_b = 13.0 / 12.0 * (second - 2.0 * centre + fourth) ** 2 + 0.25 * (second - fourth) ** 2
    rough_c = 13.0 / 12.0 * (centre - 2.0 * fourth + fifth) ** 2 + 0.25 * (3.0 * centre - 4.0 * fourth + fifth) ** 2
    weight_a = 0.1 / (WENO_EPSILON + rough_a) ** 2
    weight_b = 0.6 / (WENO_EPSILON + rough_b) ** 2
    weight_c = 0.3 / (WENO_EPSILON + rough_c) ** 2
    return (weight_a * cand_a + weight_b * cand_b + weight_c * cand_c) / (weight_a + weight_b + weight_c)

def riemann(left_fields, right_fields, left_label, right_label, direction):
    left = primitives(left_fields, left_label)
    right = primitives(right_fields, right_label)
    left_speed = left[1][direction]
    right_speed = right[1][direction]
    slow = jnp.minimum(left_speed - left[5], right_speed - right[5])
    fast = jnp.maximum(left_speed + left[5], right_speed + right[5])
    left_traction = left[4] - left[3][direction][direction]
    right_traction = right[4] - right[3][direction][direction]
    left_gap = slow - left_speed
    right_gap = fast - right_speed
    contact = (right_traction - left_traction + left[0] * left_speed * left_gap - right[0] * right_speed * right_gap) / (left[0] * left_gap - right[0] * right_gap)
    margin = 0.05 * (fast - slow)
    contact = jnp.clip(contact, slow + margin, fast - margin)

    def conserved(fields, prim):
        return [prim[0], fields[1], fields[2], fields[3], fields[4]]

    def normal_flux(fields, prim, traction):
        speed = prim[1][direction]
        out = [fields[1 + direction]]
        for comp in range(3):
            out.append(fields[1 + comp] * speed + (traction if comp == direction else 0.0))
        out.append((fields[4] + traction) * speed)
        return out

    def star(fields, prim, wave, gap, traction):
        ratio = gap / (wave - contact)
        mass = prim[0] * ratio
        moment = [mass * contact if comp == direction else mass * prim[1][comp] for comp in range(3)]
        energy = ratio * (fields[4] + (contact - prim[1][direction]) * (prim[0] * contact + traction / gap))
        return [mass] + moment + [energy]
    flux_left = normal_flux(left_fields, left, left_traction)
    flux_right = normal_flux(right_fields, right, right_traction)
    state_left = conserved(left_fields, left)
    state_right = conserved(right_fields, right)
    star_left = star(left_fields, left, slow, left_gap, left_traction)
    star_right = star(right_fields, right, fast, right_gap, right_traction)
    result = []
    for comp in range(5):
        through_left = flux_left[comp] + slow * (star_left[comp] - state_left[comp])
        through_right = flux_right[comp] + fast * (star_right[comp] - state_right[comp])
        result.append(jnp.where(slow >= 0, flux_left[comp], jnp.where(contact >= 0, through_left, jnp.where(fast > 0, through_right, flux_right[comp]))))
    for comp in range(3):
        if comp != direction:
            result[1 + comp] = result[1 + comp] - 0.5 * (left[3][comp][direction] + right[3][comp][direction])
            result[4] = result[4] - 0.5 * (left[3][direction][comp] * left[1][comp] + right[3][direction][comp] * right[1][comp])
    for row in range(3):
        flow_left = sum((left[2][row][comp] * left[1][comp] for comp in range(3)))
        flow_right = sum((right[2][row][comp] * right[1][comp] for comp in range(3)))
        jump = right_fields[5 + 3 * row + direction] - left_fields[5 + 3 * row + direction]
        blended = (fast * flow_left - slow * flow_right + slow * fast * jump) / (fast - slow)
        result.append(jnp.where(slow >= 0, flow_left, jnp.where(fast <= 0, flow_right, blended)))
    return result

def plastic(fields, label):
    gamma, stiff, shear, cohesion, friction = material(label)
    prim = primitives(fields, label)
    sandy = label == 0
    radius = jnp.where(sandy, cohesion + friction * jnp.maximum(prim[4], 0.0), 1.0)
    gradient = prim[2]
    for turn in range(RETURN_ITERS):
        stress, unused = deviator(gradient, shear)
        norm = jnp.sqrt(sum((stress[row][col] * stress[row][col] for row in range(3) for col in range(3))))
        factor = jnp.where(sandy, 0.5 * (1.0 + radius / jnp.maximum(norm, radius)), 1.0)
        third = (gradient[0][0] + gradient[1][1] + gradient[2][2]) / 3.0
        gradient = [[factor * gradient[row][col] + ((1.0 - factor) * third if row == col else 0.0) for col in range(3)] for row in range(3)]
    return fields[:5] + [gradient[row][col] for row in range(3) for col in range(3)]

def sweep(padded, label_pad, axis, direction, step_size):
    cells = padded.shape[axis] - 6
    faces = cells + 1

    def part(array, offset, count):
        return lax.slice_in_dim(array, offset, offset + count, axis=axis)
    shifted = [part(padded, offset, faces) for offset in range(6)]
    left_state = weno_face(shifted[0], shifted[1], shifted[2], shifted[3], shifted[4])
    right_state = weno_face(shifted[5], shifted[4], shifted[3], shifted[2], shifted[1])
    left_label = part(label_pad, 2, faces)[0]
    right_label = part(label_pad, 3, faces)[0]
    fluxes = riemann([left_state[comp] for comp in range(14)], [right_state[comp] for comp in range(14)], left_label, right_label, direction)
    centre = part(padded, 3, cells)
    label = part(label_pad, 3, cells)[0]
    fields = [centre[comp] for comp in range(14)]
    changed = [0, 1, 2, 3, 4] + [5 + 3 * row + direction for row in range(3)]
    for slot in range(8):
        flux = fluxes[slot]
        change = lax.slice_in_dim(flux, 1, faces, axis=axis - 1) - lax.slice_in_dim(flux, 0, cells, axis=axis - 1)
        fields[changed[slot]] = fields[changed[slot]] - step_size * change
    return jnp.stack(plastic(fields, label))

def edge_pad(array, axis):
    widths = [(0, 0)] * array.ndim
    widths[axis] = (3, 3)
    return jnp.pad(array, widths, mode='edge')

def peak_speed(state, label):
    prim = primitives([state[comp] for comp in range(14)], label)
    fastest = jnp.maximum(jnp.maximum(jnp.abs(prim[1][0]), jnp.abs(prim[1][1])), jnp.abs(prim[1][2]))
    return jnp.max(fastest + prim[5])

def reference(state, labels):
    step_size = COURANT / peak_speed(state, labels)
    label_block = labels[None]

    def along(current, moved_dim, axis, direction):
        moved = jnp.moveaxis(current, moved_dim, 0)
        moved_labels = jnp.moveaxis(label_block, moved_dim, 0)

        def single(pair):
            slab, label_slab = pair
            return sweep(edge_pad(slab, axis), edge_pad(label_slab, axis), axis, direction, step_size)
        return jnp.moveaxis(lax.map(single, (moved, moved_labels)), 0, moved_dim)
    after_x = along(state, 1, 2, 0)
    after_y = along(after_x, 1, 1, 1)
    return along(after_y, 2, 1, 2)
```

```python
import functools

import jax
import jax.numpy as jnp
from jax import lax
from jax.experimental import pallas as pl
from jax.experimental.pallas import tpu as pltpu
from jax.sharding import PartitionSpec as P

RETURN_ITERS = 2
REACH = 3
FIELDS = 14
DENSITY_FLOOR = 0.2
TRACTION_FLOOR = 0.1
COURANT = 0.4
WENO_EPSILON = 1e-06
SMALL_GROUP = 32
SMALL_AXIS = 8


def pick(label, sand, solid, void):
    return jnp.where(label == 0.0, sand, jnp.where(label == 1.0, solid, void))


def material(label):
    gamma = pick(label, 3.0, 4.0, 1.4)
    stiff = jnp.where(label == 1.0, 6.0, jnp.where(label == 0.0, 1.0, 0.0))
    shear = pick(label, 0.6, 3.0, 0.0)
    return gamma, stiff, shear


def deviator(grad):
    metric = {}
    for i in range(3):
        for j in range(i, 3):
            metric[i, j] = (
                grad[0][i] * grad[0][j] + grad[1][i] * grad[1][j] + grad[2][i] * grad[2][j]
            )
    third = (metric[0, 0] + metric[1, 1] + metric[2, 2]) * (1.0 / 3.0)
    for i in range(3):
        metric[i, i] = metric[i, i] - third
    return metric


def square_sum(dev):
    off = dev[0, 1] * dev[0, 1] + dev[0, 2] * dev[0, 2] + dev[1, 2] * dev[1, 2]
    diag = dev[0, 0] * dev[0, 0] + dev[1, 1] * dev[1, 1] + dev[2, 2] * dev[2, 2]
    return diag + (off + off)


def grad_of(fields):
    return [[fields[5 + 3 * row + col] for col in range(3)] for row in range(3)]


def pressure_of(fields, dev, mats):
    gamma, stiff, shear = mats
    density = jnp.maximum(fields[0], DENSITY_FLOOR)
    inverse = 1.0 / density
    velocity = [fields[1 + comp] * inverse for comp in range(3)]
    kinetic = 0.5 * (
        fields[1] * velocity[0] + fields[2] * velocity[1] + fields[3] * velocity[2]
    )
    energy = (0.25 * shear) * square_sum(dev)
    pressure = (gamma - 1.0) * (fields[4] - kinetic - energy) - gamma * stiff
    return density, inverse, velocity, pressure


def primitives(fields, mats):
    gamma, stiff, shear = mats
    dev = deviator(grad_of(fields))
    density, inverse, velocity, pressure = pressure_of(fields, dev, mats)
    sound = jnp.sqrt(
        (gamma * jnp.maximum(pressure + stiff, TRACTION_FLOOR) + (4.0 / 3.0) * shear) * inverse
    )
    return density, velocity, dev, pressure, sound


def weno_pair(v):
    bend = [v[i] - 2.0 * v[i + 1] + v[i + 2] for i in range(4)]
    bend = [13.0 / 12.0 * (b * b) for b in bend]

    def one(a, b, c, e, f, bend_a, bend_b, bend_c):
        slope_a = a - 4.0 * b + 3.0 * c
        slope_b = b - e
        slope_c = 3.0 * c - 4.0 * e + f
        inv_a = 1.0 / (WENO_EPSILON + (bend_a + 0.25 * (slope_a * slope_a)))
        inv_b = 1.0 / (WENO_EPSILON + (bend_b + 0.25 * (slope_b * slope_b)))
        inv_c = 1.0 / (WENO_EPSILON + (bend_c + 0.25 * (slope_c * slope_c)))
        weight_a = (0.1 / 6.0) * (inv_a * inv_a)
        weight_b = (0.6 / 6.0) * (inv_b * inv_b)
        weight_c = (0.3 / 6.0) * (inv_c * inv_c)
        total = (
            weight_a * (2.0 * a - 7.0 * b + 11.0 * c)
            + weight_b * (5.0 * c - b + 2.0 * e)
            + weight_c * (2.0 * c + 5.0 * e - f)
        )
        return total / (6.0 * (weight_a + weight_b + weight_c))

    left = one(v[0], v[1], v[2], v[3], v[4], bend[0], bend[1], bend[2])
    right = one(v[5], v[4], v[3], v[2], v[1], bend[3], bend[2], bend[1])
    return left, right


def riemann(lf, rf, left_label, right_label, d):
    left_mats, right_mats = material(left_label), material(right_label)
    l_rho, l_vel, l_dev, l_p, l_c = primitives(lf, left_mats)
    r_rho, r_vel, r_dev, r_p, r_c = primitives(rf, right_mats)

    def stress(dev, mats, i, j):
        return -mats[2] * dev[min(i, j), max(i, j)]

    l_s = [stress(l_dev, left_mats, k, d) for k in range(3)]
    r_s = [stress(r_dev, right_mats, k, d) for k in range(3)]
    l_u, r_u = l_vel[d], r_vel[d]
    slow = jnp.minimum(l_u - l_c, r_u - r_c)
    fast = jnp.maximum(l_u + l_c, r_u + r_c)
    l_t, r_t = l_p - l_s[d], r_p - r_s[d]
    l_gap, r_gap = slow - l_u, fast - r_u
    l_push, r_push = l_rho * l_gap, r_rho * r_gap
    contact = (r_t - l_t + l_push * l_u - r_push * r_u) / (l_push - r_push)
    width = fast - slow
    margin = 0.05 * width
    contact = jnp.minimum(jnp.maximum(contact, slow + margin), fast - margin)

    go_left = (slow >= 0.0) | (contact >= 0.0)
    plain = (slow >= 0.0) | (jnp.logical_not(contact >= 0.0) & jnp.logical_not(fast > 0.0))

    def side(a, b):
        return jnp.where(go_left, a, b)

    rho, gap, wave, trac = side(l_rho, r_rho), side(l_gap, r_gap), side(slow, fast), side(l_t, r_t)
    vel = [side(l_vel[k], r_vel[k]) for k in range(3)]
    mom = [side(lf[1 + k], rf[1 + k]) for k in range(3)]
    ener = side(lf[4], rf[4])
    u = vel[d]
    ratio = gap / (wave - contact)
    mass = rho * ratio
    star_e = ratio * (ener + (contact - u) * (rho * contact + trac / gap))
    result = [mom[d] + jnp.where(plain, 0.0, wave * (mass - rho))]
    for k in range(3):
        flux = mom[k] * u + trac if k == d else mom[k] * u
        star = mass * (contact if k == d else vel[k])
        result.append(flux + jnp.where(plain, 0.0, wave * (star - mom[k])))
    result.append((ener + trac) * u + jnp.where(plain, 0.0, wave * (star_e - ener)))
    for k in range(3):
        if k != d:
            result[1 + k] = result[1 + k] - 0.5 * (l_s[k] + r_s[k])
            result[4] = result[4] - 0.5 * (l_s[k] * l_vel[k] + r_s[k] * r_vel[k])
    inverse = 1.0 / width
    for row in range(3):
        base = 5 + 3 * row
        l_flow = lf[base] * l_vel[0] + lf[base + 1] * l_vel[1] + lf[base + 2] * l_vel[2]
        r_flow = rf[base] * r_vel[0] + rf[base + 1] * r_vel[1] + rf[base + 2] * r_vel[2]
        jump = rf[base + d] - lf[base + d]
        blend = (fast * l_flow - slow * r_flow + slow * fast * jump) * inverse
        result.append(jnp.where(slow >= 0.0, l_flow, jnp.where(fast <= 0.0, r_flow, blend)))
    return result


def changed_fields(d):
    return [0, 1, 2, 3, 4] + [5 + 3 * row + d for row in range(3)]


def face_fluxes(window, d):
    left, right = [], []
    for field in range(FIELDS):
        a, b = weno_pair([window(field, k) for k in range(6)])
        left.append(a)
        right.append(b)
    return riemann(left, right, window(FIELDS, 2), window(FIELDS, 3), d)


def plastic(fields, label):
    mats = material(label)
    shear = mats[2]
    sandy = label == 0.0
    grad = grad_of(fields)
    dev = deviator(grad)
    pressure = pressure_of(fields, dev, mats)[3]
    radius = jnp.where(sandy, 0.05 + 0.4 * jnp.maximum(pressure, 0.0), 1.0)
    for turn in range(RETURN_ITERS):
        if turn:
            dev = deviator(grad)
        scaled = {key: shear * value for key, value in dev.items()}
        norm = jnp.sqrt(square_sum(scaled))
        factor = jnp.where(sandy, 0.5 * (1.0 + radius / jnp.maximum(norm, radius)), 1.0)
        third = (1.0 - factor) * ((grad[0][0] + grad[1][1] + grad[2][2]) * (1.0 / 3.0))
        grad = [
            [factor * grad[i][j] + third if i == j else factor * grad[i][j] for j in range(3)]
            for i in range(3)
        ]
    return list(fields[:5]) + [grad[i][j] for i in range(3) for j in range(3)]


def peak_kernel(state_ref, label_ref, peak_ref, packed_ref):
    rows = state_ref.shape[2]
    label = label_ref[0].astype(jnp.float32)
    fields = [state_ref[field, 0] for field in range(FIELDS)]
    for field in range(FIELDS):
        packed_ref[field] = fields[field]
    packed_ref[FIELDS] = label
    density, velocity, dev, pressure, sound = primitives(fields, material(label))
    speed = sound + jnp.maximum(
        jnp.maximum(jnp.abs(velocity[0]), jnp.abs(velocity[1])), jnp.abs(velocity[2])
    )
    best = speed[:, :128]
    for start in range(128, speed.shape[1], 128):
        best = jnp.maximum(best, speed[:, start : start + 128])
    best = jnp.max(best, axis=0, keepdims=True)
    peak_ref[...] = jnp.broadcast_to(best, peak_ref.shape)


def x_kernel(own_ref, low_ref, high_ref, out_ref, flux_ref, line_ref):
    rows, nx = own_ref.shape[1:]
    total = rows + 2 * REACH
    stack = line_ref.shape[1]
    pos, count = lax.axis_index("aa"), lax.axis_size("aa")
    first, last = pos == 0, pos == count - 1
    for field in range(FIELDS + 1):
        own = own_ref[field]
        low = jnp.where(first, own[:1], low_ref[field, rows - REACH :])
        high = jnp.where(last, own[rows - 1 :], high_ref[field, :REACH])
        out_ref[field, :REACH] = low
        out_ref[field, REACH : REACH + rows] = own
        out_ref[field, REACH + rows : total] = high
        out_ref[field, total:] = jnp.zeros((out_ref.shape[1] - total, nx), jnp.float32)
    lane = lax.broadcasted_iota(jnp.int32, (total, nx), 1)
    wide = lax.broadcasted_iota(jnp.int32, (stack, nx), 1)
    for field in range(FIELDS + 1):
        cells = out_ref[field, :total]
        line_ref[field, :total] = cells
        line_ref[field, total : 2 * total] = jnp.where(
            lane == nx - 1, cells, pltpu.roll(cells, nx - 1, 1)
        )
        if stack > 2 * total:
            line_ref[field, 2 * total :] = jnp.zeros((stack - 2 * total, nx), jnp.float32)
    cache = {}

    def window(field, k):
        if (field, k) not in cache:
            if k == 3:
                value = line_ref[field]
            elif k < 3:
                near = window(field, k + 1)
                value = jnp.where(wide == 0, near, pltpu.roll(near, 1, 1))
            else:
                near = window(field, k - 1)
                value = jnp.where(wide == nx - 1, near, pltpu.roll(near, nx - 1, 1))
            cache[field, k] = value
        return cache[field, k]

    for slot, flux in enumerate(face_fluxes(window, 0)):
        line_ref[slot] = flux
    for slot in range(8):
        lower = line_ref[slot, :total]
        upper = line_ref[slot, total : 2 * total]
        flux_ref[slot, :total] = (
            jnp.where(lane == nx - 1, upper, pltpu.roll(lower, nx - 1, 1)) - lower
        )
        flux_ref[slot, total:] = jnp.zeros((flux_ref.shape[1] - total, nx), jnp.float32)


def step_of(peak_ref):
    best = jnp.max(peak_ref[...], axis=0, keepdims=True)
    return COURANT / jnp.max(best, axis=1, keepdims=True)


def y_kernel(peak_ref, cells_ref, change_ref, out_ref, step_ref, line_ref, face_ref):
    copies, _, rows, nx = out_ref.shape
    step = step_of(peak_ref)
    step_ref[...] = jnp.broadcast_to(step, step_ref.shape)
    label = cells_ref[FIELDS]
    fields = [cells_ref[field] for field in range(FIELDS)]
    for slot, field in enumerate(changed_fields(0)):
        fields[field] = fields[field] - step * change_ref[slot]
    fields = plastic(fields, label)
    height = label.shape[0]
    for field in range(FIELDS):
        line_ref[field, :height] = fields[field]
    line_ref[FIELDS, :height] = label
    faces = face_ref.shape[1]
    for field in range(FIELDS + 1):
        if line_ref.shape[1] > height:
            line_ref[field, height:] = jnp.zeros((line_ref.shape[1] - height, nx), jnp.float32)
    fluxes = face_fluxes(lambda field, k: line_ref[field, k : k + faces], 1)
    for slot in range(8):
        face_ref[slot] = fluxes[slot]
    label = line_ref[FIELDS, REACH : REACH + rows]
    fields = [line_ref[field, REACH : REACH + rows] for field in range(FIELDS)]
    for slot, field in enumerate(changed_fields(1)):
        change = face_ref[slot, 1 : rows + 1] - face_ref[slot, :rows]
        fields[field] = fields[field] - step * change
    fields = plastic(fields, label) + [label]
    for copy in range(copies):
        for field in range(FIELDS + 1):
            out_ref[copy, field] = fields[field]


def z_kernel(centred, step_ref, lines_ref, out_ref, line_ref):
    rows = out_ref.shape[2]
    pos, count = lax.axis_index("ba"), lax.axis_size("ba")
    step = step_ref[:rows, :1]
    for k in range(2 * REACH + 1):
        where = jnp.clip(pos + k - REACH, 0, count - 1)
        if centred:
            where = where - pos + REACH
        for field in range(FIELDS + 1):
            line_ref[field, k * rows : (k + 1) * rows] = lines_ref[where, field]
    fluxes = face_fluxes(
        lambda field, k: line_ref[field, k * rows : (k + 2) * rows], 2
    )
    centre = slice(REACH * rows, (REACH + 1) * rows)
    label = line_ref[FIELDS, centre]
    fields = [line_ref[field, centre] for field in range(FIELDS)]
    for slot, field in enumerate(changed_fields(2)):
        fields[field] = fields[field] - step * (fluxes[slot][rows:] - fluxes[slot][:rows])
    fields = plastic(fields, label)
    for field in range(FIELDS):
        out_ref[field, 0] = fields[field]


def up8(size):
    return -(-size // 8) * 8


def call(kernel, outs, scratch, cost, name):
    vmem = pl.BlockSpec(memory_space=pltpu.VMEM)
    shapes = [jax.ShapeDtypeStruct(shape, jnp.float32) for shape in outs]

    def run(*args):
        return pl.pallas_call(
            kernel,
            out_shape=shapes if len(shapes) > 1 else shapes[0],
            in_specs=[vmem] * len(args),
            out_specs=[vmem] * len(shapes) if len(shapes) > 1 else vmem,
            scratch_shapes=[pltpu.VMEM(shape, jnp.float32) for shape in scratch],
            cost_estimate=pl.CostEstimate(flops=cost, bytes_accessed=cost // 4, transcendentals=0),
            name=name,
            compiler_params=pltpu.CompilerParams(vmem_limit_bytes=16 * 1024 * 1024),
        )(*args)

    return run


def shards(state, labels):
    _, depth, rows, nx = state.shape
    assert depth == 1 and rows >= REACH and nx % 128 == 0
    count_a, count_b = lax.axis_size("aa"), lax.axis_size("ba")
    devices = count_a * count_b
    total = rows + 2 * REACH
    tall = up8(total)
    small = devices <= SMALL_GROUP
    peak, packed = call(
        peak_kernel,
        [(devices if small else 8, 128), (FIELDS + 1, rows, nx)],
        [],
        200_000,
        "peak",
    )(state, labels)
    ups = [(i, i + 1) for i in range(count_a - 1)]
    low = lax.ppermute(packed, "aa", ups)
    high = lax.ppermute(packed, "aa", [(j, i) for i, j in ups])
    if small:
        peaks = lax.all_to_all(peak, ("aa", "ba"), 0, 0, tiled=True)
    else:
        peaks = lax.pmax(peak, ("aa", "ba"))
    cells, change = call(
        x_kernel,
        [(FIELDS + 1, tall, nx), (8, tall, nx)],
        [(FIELDS + 1, up8(2 * total), nx)],
        4_000_000,
        "xflux",
    )(packed, low, high)
    exchange = count_b <= SMALL_AXIS
    faces = up8(rows + 1)
    after_y, step = call(
        y_kernel,
        [(count_b if exchange else 1, FIELDS + 1, rows, nx), (8, 128)],
        [(FIELDS + 1, max(tall, up8(2 * REACH - 1 + faces)), nx), (8, faces, nx)],
        4_000_000,
        "ysweep",
    )(peaks, cells, change)
    if exchange:
        lines = lax.all_to_all(after_y, "ba", 0, 0, tiled=True)
    else:
        near = []
        for shift in range(-REACH, REACH + 1):
            pairs = [(i, i - shift) for i in range(count_b) if 0 <= i - shift < count_b]
            near.append(lax.ppermute(after_y, "ba", pairs) if shift else after_y)
        lines = jnp.concatenate(near, axis=0)
    return call(
        functools.partial(z_kernel, not exchange),
        [(FIELDS, 1, rows, nx)],
        [(FIELDS + 1, (2 * REACH + 1) * rows, nx)],
        4_000_000,
        "zsweep",
    )(step, lines)


def solution(mesh):
    return jax.shard_map(
        shards,
        mesh=mesh,
        in_specs=(P(None, "ba", "aa", None), P("ba", "aa", None)),
        out_specs=P(None, "ba", "aa", None),
        check_vma=False,
    )
```

```python
import functools

import jax
import jax.numpy as jnp
from jax import lax
from jax.experimental import pallas as pl
from jax.experimental.pallas import tpu as pltpu
from jax.sharding import PartitionSpec as P

RETURN_ITERS = 2
REACH = 3
FIELDS = 14
DENSITY_FLOOR = 0.2
TRACTION_FLOOR = 0.1
COURANT = 0.4
WENO_EPSILON = 1e-06
SMALL_GROUP = 32
SMALL_AXIS = 8


def pick(label, sand, solid, void):
    return jnp.where(label == 0.0, sand, jnp.where(label == 1.0, solid, void))


def material(label):
    gamma = pick(label, 3.0, 4.0, 1.4)
    stiff = jnp.where(label == 1.0, 6.0, jnp.where(label == 0.0, 1.0, 0.0))
    shear = pick(label, 0.6, 3.0, 0.0)
    return gamma, stiff, shear


def deviator(grad):
    metric = {}
    for i in range(3):
        for j in range(i, 3):
            metric[i, j] = (
                grad[0][i] * grad[0][j] + grad[1][i] * grad[1][j] + grad[2][i] * grad[2][j]
            )
    third = (metric[0, 0] + metric[1, 1] + metric[2, 2]) * (1.0 / 3.0)
    for i in range(3):
        metric[i, i] = metric[i, i] - third
    return metric


def square_sum(dev):
    off = dev[0, 1] * dev[0, 1] + dev[0, 2] * dev[0, 2] + dev[1, 2] * dev[1, 2]
    diag = dev[0, 0] * dev[0, 0] + dev[1, 1] * dev[1, 1] + dev[2, 2] * dev[2, 2]
    return diag + (off + off)


def grad_of(fields):
    return [[fields[5 + 3 * row + col] for col in range(3)] for row in range(3)]


def pressure_of(fields, dev, mats):
    gamma, stiff, shear = mats
    density = jnp.maximum(fields[0], DENSITY_FLOOR)
    inverse = 1.0 / density
    velocity = [fields[1 + comp] * inverse for comp in range(3)]
    kinetic = 0.5 * (
        fields[1] * velocity[0] + fields[2] * velocity[1] + fields[3] * velocity[2]
    )
    energy = (0.25 * shear) * square_sum(dev)
    pressure = (gamma - 1.0) * (fields[4] - kinetic - energy) - gamma * stiff
    return density, inverse, velocity, pressure


def primitives(fields, mats):
    gamma, stiff, shear = mats
    dev = deviator(grad_of(fields))
    density, inverse, velocity, pressure = pressure_of(fields, dev, mats)
    sound = jnp.sqrt(
        (gamma * jnp.maximum(pressure + stiff, TRACTION_FLOOR) + (4.0 / 3.0) * shear) * inverse
    )
    return density, velocity, dev, pressure, sound


def weno_pair(v):
    bend = [v[i] - 2.0 * v[i + 1] + v[i + 2] for i in range(4)]
    bend = [13.0 / 12.0 * (b * b) for b in bend]

    def one(a, b, c, e, f, bend_a, bend_b, bend_c):
        slope_a = a - 4.0 * b + 3.0 * c
        slope_b = b - e
        slope_c = 3.0 * c - 4.0 * e + f
        inv_a = 1.0 / (WENO_EPSILON + (bend_a + 0.25 * (slope_a * slope_a)))
        inv_b = 1.0 / (WENO_EPSILON + (bend_b + 0.25 * (slope_b * slope_b)))
        inv_c = 1.0 / (WENO_EPSILON + (bend_c + 0.25 * (slope_c * slope_c)))
        weight_a = (0.1 / 6.0) * (inv_a * inv_a)
        weight_b = (0.6 / 6.0) * (inv_b * inv_b)
        weight_c = (0.3 / 6.0) * (inv_c * inv_c)
        total = (
            weight_a * (2.0 * a - 7.0 * b + 11.0 * c)
            + weight_b * (5.0 * c - b + 2.0 * e)
            + weight_c * (2.0 * c + 5.0 * e - f)
        )
        return total / (6.0 * (weight_a + weight_b + weight_c))

    left = one(v[0], v[1], v[2], v[3], v[4], bend[0], bend[1], bend[2])
    right = one(v[5], v[4], v[3], v[2], v[1], bend[3], bend[2], bend[1])
    return left, right


def riemann(lf, rf, left_label, right_label, d):
    left_mats, right_mats = material(left_label), material(right_label)
    l_rho, l_vel, l_dev, l_p, l_c = primitives(lf, left_mats)
    r_rho, r_vel, r_dev, r_p, r_c = primitives(rf, right_mats)

    def stress(dev, mats, i, j):
        return -mats[2] * dev[min(i, j), max(i, j)]

    l_s = [stress(l_dev, left_mats, k, d) for k in range(3)]
    r_s = [stress(r_dev, right_mats, k, d) for k in range(3)]
    l_u, r_u = l_vel[d], r_vel[d]
    slow = jnp.minimum(l_u - l_c, r_u - r_c)
    fast = jnp.maximum(l_u + l_c, r_u + r_c)
    l_t, r_t = l_p - l_s[d], r_p - r_s[d]
    l_gap, r_gap = slow - l_u, fast - r_u
    l_push, r_push = l_rho * l_gap, r_rho * r_gap
    contact = (r_t - l_t + l_push * l_u - r_push * r_u) / (l_push - r_push)
    width = fast - slow
    margin = 0.05 * width
    contact = jnp.minimum(jnp.maximum(contact, slow + margin), fast - margin)

    go_left = (slow >= 0.0) | (contact >= 0.0)
    plain = (slow >= 0.0) | (jnp.logical_not(contact >= 0.0) & jnp.logical_not(fast > 0.0))

    def side(a, b):
        return jnp.where(go_left, a, b)

    rho, gap, wave, trac = side(l_rho, r_rho), side(l_gap, r_gap), side(slow, fast), side(l_t, r_t)
    vel = [side(l_vel[k], r_vel[k]) for k in range(3)]
    mom = [side(lf[1 + k], rf[1 + k]) for k in range(3)]
    ener = side(lf[4], rf[4])
    u = vel[d]
    ratio = gap / (wave - contact)
    mass = rho * ratio
    star_e = ratio * (ener + (contact - u) * (rho * contact + trac / gap))
    result = [mom[d] + jnp.where(plain, 0.0, wave * (mass - rho))]
    for k in range(3):
        flux = mom[k] * u + trac if k == d else mom[k] * u
        star = mass * (contact if k == d else vel[k])
        result.append(flux + jnp.where(plain, 0.0, wave * (star - mom[k])))
    result.append((ener + trac) * u + jnp.where(plain, 0.0, wave * (star_e - ener)))
    for k in range(3):
        if k != d:
            result[1 + k] = result[1 + k] - 0.5 * (l_s[k] + r_s[k])
            result[4] = result[4] - 0.5 * (l_s[k] * l_vel[k] + r_s[k] * r_vel[k])
    inverse = 1.0 / width
    for row in range(3):
        base = 5 + 3 * row
        l_flow = lf[base] * l_vel[0] + lf[base + 1] * l_vel[1] + lf[base + 2] * l_vel[2]
        r_flow = rf[base] * r_vel[0] + rf[base + 1] * r_vel[1] + rf[base + 2] * r_vel[2]
        jump = rf[base + d] - lf[base + d]
        blend = (fast * l_flow - slow * r_flow + slow * fast * jump) * inverse
        result.append(jnp.where(slow >= 0.0, l_flow, jnp.where(fast <= 0.0, r_flow, blend)))
    return result


def changed_fields(d):
    return [0, 1, 2, 3, 4] + [5 + 3 * row + d for row in range(3)]


def face_fluxes(window, d):
    left, right = [], []
    for field in range(FIELDS):
        a, b = weno_pair([window(field, k) for k in range(6)])
        left.append(a)
        right.append(b)
    return riemann(left, right, window(FIELDS, 2), window(FIELDS, 3), d)


def plastic(fields, label):
    mats = material(label)
    shear = mats[2]
    sandy = label == 0.0
    grad = grad_of(fields)
    dev = deviator(grad)
    pressure = pressure_of(fields, dev, mats)[3]
    radius = jnp.where(sandy, 0.05 + 0.4 * jnp.maximum(pressure, 0.0), 1.0)
    for turn in range(RETURN_ITERS):
        if turn:
            dev = deviator(grad)
        scaled = {key: shear * value for key, value in dev.items()}
        norm = jnp.sqrt(square_sum(scaled))
        factor = jnp.where(sandy, 0.5 * (1.0 + radius / jnp.maximum(norm, radius)), 1.0)
        third = (1.0 - factor) * ((grad[0][0] + grad[1][1] + grad[2][2]) * (1.0 / 3.0))
        grad = [
            [factor * grad[i][j] + third if i == j else factor * grad[i][j] for j in range(3)]
            for i in range(3)
        ]
    return list(fields[:5]) + [grad[i][j] for i in range(3) for j in range(3)]


def peak_kernel(state_ref, label_ref, peak_ref, packed_ref):
    rows = state_ref.shape[2]
    label = label_ref[0].astype(jnp.float32)
    fields = [state_ref[field, 0] for field in range(FIELDS)]
    for field in range(FIELDS):
        packed_ref[field] = fields[field]
    packed_ref[FIELDS] = label
    density, velocity, dev, pressure, sound = primitives(fields, material(label))
    speed = sound + jnp.maximum(
        jnp.maximum(jnp.abs(velocity[0]), jnp.abs(velocity[1])), jnp.abs(velocity[2])
    )
    best = speed[:, :128]
    for start in range(128, speed.shape[1], 128):
        best = jnp.maximum(best, speed[:, start : start + 128])
    best = jnp.max(best, axis=0, keepdims=True)
    peak_ref[...] = jnp.broadcast_to(best, peak_ref.shape)


def x_kernel(own_ref, low_ref, high_ref, out_ref, flux_ref, line_ref):
    rows, nx = own_ref.shape[1:]
    total = rows + 2 * REACH
    stack = line_ref.shape[1]
    pos, count = lax.axis_index("aa"), lax.axis_size("aa")
    first, last = pos == 0, pos == count - 1
    for field in range(FIELDS + 1):
        own = own_ref[field]
        low = jnp.where(first, own[:1], low_ref[field, rows - REACH :])
        high = jnp.where(last, own[rows - 1 :], high_ref[field, :REACH])
        out_ref[field, :REACH] = low
        out_ref[field, REACH : REACH + rows] = own
        out_ref[field, REACH + rows : total] = high
        out_ref[field, total:] = jnp.zeros((out_ref.shape[1] - total, nx), jnp.float32)
    lane = lax.broadcasted_iota(jnp.int32, (total, nx), 1)
    wide = lax.broadcasted_iota(jnp.int32, (stack, nx), 1)
    for field in range(FIELDS + 1):
        cells = out_ref[field, :total]
        line_ref[field, :total] = cells
        line_ref[field, total : 2 * total] = jnp.where(
            lane == nx - 1, cells, pltpu.roll(cells, nx - 1, 1)
        )
        if stack > 2 * total:
            line_ref[field, 2 * total :] = jnp.zeros((stack - 2 * total, nx), jnp.float32)
    cache = {}

    def window(field, k):
        if (field, k) not in cache:
            if k == 3:
                value = line_ref[field]
            elif k < 3:
                near = window(field, k + 1)
                value = jnp.where(wide == 0, near, pltpu.roll(near, 1, 1))
            else:
                near = window(field, k - 1)
                value = jnp.where(wide == nx - 1, near, pltpu.roll(near, nx - 1, 1))
            cache[field, k] = value
        return cache[field, k]

    for slot, flux in enumerate(face_fluxes(window, 0)):
        line_ref[slot] = flux
    for slot in range(8):
        lower = line_ref[slot, :total]
        upper = line_ref[slot, total : 2 * total]
        flux_ref[slot, :total] = (
            jnp.where(lane == nx - 1, upper, pltpu.roll(lower, nx - 1, 1)) - lower
        )
        flux_ref[slot, total:] = jnp.zeros((flux_ref.shape[1] - total, nx), jnp.float32)


def step_of(peak_ref):
    best = jnp.max(peak_ref[...], axis=0, keepdims=True)
    return COURANT / jnp.max(best, axis=1, keepdims=True)


def y_kernel(peak_ref, cells_ref, change_ref, out_ref, step_ref, line_ref, face_ref):
    copies, _, rows, nx = out_ref.shape
    step = step_of(peak_ref)
    step_ref[...] = jnp.broadcast_to(step, step_ref.shape)
    label = cells_ref[FIELDS]
    fields = [cells_ref[field] for field in range(FIELDS)]
    for slot, field in enumerate(changed_fields(0)):
        fields[field] = fields[field] - step * change_ref[slot]
    fields = plastic(fields, label)
    height = label.shape[0]
    for field in range(FIELDS):
        line_ref[field, :height] = fields[field]
    line_ref[FIELDS, :height] = label
    faces = face_ref.shape[1]
    for field in range(FIELDS + 1):
        if line_ref.shape[1] > height:
            line_ref[field, height:] = jnp.zeros((line_ref.shape[1] - height, nx), jnp.float32)
    fluxes = face_fluxes(lambda field, k: line_ref[field, k : k + faces], 1)
    for slot in range(8):
        face_ref[slot] = fluxes[slot]
    label = line_ref[FIELDS, REACH : REACH + rows]
    fields = [line_ref[field, REACH : REACH + rows] for field in range(FIELDS)]
    for slot, field in enumerate(changed_fields(1)):
        change = face_ref[slot, 1 : rows + 1] - face_ref[slot, :rows]
        fields[field] = fields[field] - step * change
    fields = plastic(fields, label) + [label]
    for copy in range(copies):
        for field in range(FIELDS + 1):
            out_ref[copy, field] = fields[field]


def z_kernel(centred, step_ref, lines_ref, out_ref, line_ref):
    rows = out_ref.shape[2]
    pos, count = lax.axis_index("ba"), lax.axis_size("ba")
    step = step_ref[:rows, :1]
    for k in range(2 * REACH + 1):
        where = jnp.clip(pos + k - REACH, 0, count - 1)
        if centred:
            where = where - pos + REACH
        for field in range(FIELDS + 1):
            line_ref[field, k * rows : (k + 1) * rows] = lines_ref[where, field]
    fluxes = face_fluxes(
        lambda field, k: line_ref[field, k * rows : (k + 2) * rows], 2
    )
    centre = slice(REACH * rows, (REACH + 1) * rows)
    label = line_ref[FIELDS, centre]
    fields = [line_ref[field, centre] for field in range(FIELDS)]
    for slot, field in enumerate(changed_fields(2)):
        fields[field] = fields[field] - step * (fluxes[slot][rows:] - fluxes[slot][:rows])
    fields = plastic(fields, label)
    for field in range(FIELDS):
        out_ref[field, 0] = fields[field]


CHANGED = 8


def columns_kernel(
    state_hbm, label_hbm, out_ref, cells_ref, kind_ref, line_ref, stage_ref, sems
):
    copies = [
        pltpu.make_async_copy(state_hbm, cells_ref, sems.at[0]),
        pltpu.make_async_copy(label_hbm, kind_ref, sems.at[1]),
    ]
    for copy in copies:
        copy.start()
    for copy in copies:
        copy.wait()
    _, _, rows, nx = cells_ref.shape
    label = kind_ref[0].astype(jnp.float32)
    fields = [cells_ref[field, 0] for field in range(FIELDS)]
    lane = lax.broadcasted_iota(jnp.int32, (rows, nx), 1)
    wide = lax.broadcasted_iota(jnp.int32, (2 * rows, nx), 1)
    for field, cells in enumerate(fields + [label]):
        stage_ref[field * rows : (field + 1) * rows] = cells
        line_ref[field, :rows] = cells
        line_ref[field, rows:] = jnp.where(lane == nx - 1, cells, pltpu.roll(cells, nx - 1, 1))
    density, velocity, dev, pressure, sound = primitives(fields, material(label))
    speed = sound + jnp.maximum(
        jnp.maximum(jnp.abs(velocity[0]), jnp.abs(velocity[1])), jnp.abs(velocity[2])
    )
    used = (FIELDS + 1 + CHANGED) * rows
    stage_ref[used:] = jnp.broadcast_to(
        jnp.max(speed, keepdims=True), (stage_ref.shape[0] - used, nx)
    )
    window = shifter(line_ref, wide == 0, wide == nx - 1, 1)
    for slot, flux in enumerate(face_fluxes(window, 0)):
        lower, upper = flux[:rows], flux[rows:]
        change = jnp.where(lane == nx - 1, upper, pltpu.roll(lower, nx - 1, 1)) - lower
        start = (FIELDS + 1 + slot) * rows
        stage_ref[start : start + rows] = change
    out_ref[...] = stage_ref[...].T


def shifter(line_ref, first, last, width):
    nx = line_ref.shape[2]
    cache = {}

    def window(field, k):
        if (field, k) not in cache:
            if k == REACH:
                value = line_ref[field]
            elif k < REACH:
                near = window(field, k + 1)
                value = jnp.where(first, near, pltpu.roll(near, width, 1))
            else:
                near = window(field, k - 1)
                value = jnp.where(last, near, pltpu.roll(near, nx - width, 1))
            cache[field, k] = value
        return cache[field, k]

    return window


def sweeps_kernel(rows, count_a, count_b, in_ref, out_ref, stage_ref, line_ref, face_ref, deep_ref):
    nx = in_ref.shape[0]
    group = nx // count_a
    width = group // count_b
    stage_ref[...] = in_ref[...].T
    used = (FIELDS + 1 + CHANGED) * rows
    best = jnp.max(stage_ref[used : used + 1, :], axis=1, keepdims=True)
    step = COURANT / best

    def block(index):
        return stage_ref[index * rows : (index + 1) * rows, :]

    label = block(FIELDS)
    fields = [block(field) for field in range(FIELDS)]
    for slot, field in enumerate(changed_fields(0)):
        fields[field] = fields[field] - step * block(FIELDS + 1 + slot)
    fields = plastic(fields, label)

    lane = lax.broadcasted_iota(jnp.int32, (REACH, nx), 1)
    faces = face_ref.shape[1]
    for field, cells in enumerate(fields + [label]):
        low = pltpu.roll(cells, group, 1)[rows - REACH :]
        high = pltpu.roll(cells, nx - group, 1)[:REACH]
        line_ref[field, :REACH] = jnp.where(lane < group, cells[:1], low)
        line_ref[field, REACH : REACH + rows] = cells
        line_ref[field, REACH + rows : 2 * REACH + rows] = jnp.where(
            lane >= nx - group, cells[rows - 1 :], high
        )
        rest = line_ref.shape[1] - 2 * REACH - rows
        line_ref[field, 2 * REACH + rows :] = jnp.zeros((rest, nx), jnp.float32)
    fluxes = face_fluxes(lambda field, k: line_ref[field, k : k + faces], 1)
    for slot in range(CHANGED):
        face_ref[slot] = fluxes[slot]
    for slot, field in enumerate(changed_fields(1)):
        change = face_ref[slot, 1 : rows + 1] - face_ref[slot, :rows]
        fields[field] = fields[field] - step * change
    fields = plastic(fields, label)

    lane = lax.broadcasted_iota(jnp.int32, (2 * rows, nx), 1)
    first = lane < 0
    last = lane < 0
    for a in range(count_a):
        start, end = a * group, (a + 1) * group
        first = first | ((lane >= start) & (lane < start + width))
        last = last | ((lane >= end - width) & (lane < end))
    short = last[:rows]
    for field, cells in enumerate(fields + [label]):
        deep_ref[field, :rows] = cells
        deep_ref[field, rows:] = jnp.where(short, cells, pltpu.roll(cells, nx - width, 1))
    window = shifter(deep_ref, first, last, width)
    fluxes = face_fluxes(window, 2)
    for slot, field in enumerate(changed_fields(2)):
        lower, upper = fluxes[slot][:rows], fluxes[slot][rows:]
        change = jnp.where(short, upper, pltpu.roll(lower, nx - width, 1)) - lower
        fields[field] = fields[field] - step * change
    fields = plastic(fields, label)
    for field in range(FIELDS):
        stage_ref[field * rows : (field + 1) * rows, :] = fields[field]
    out_ref[...] = stage_ref[...].T


def home_kernel(in_ref, out_ref):
    _, _, rows, _ = out_ref.shape
    back = in_ref[...].T
    for field in range(FIELDS):
        out_ref[field, 0] = back[field * rows : (field + 1) * rows]


def up8(size):
    return -(-size // 8) * 8


def call(kernel, outs, scratch, cost, name, space=pltpu.VMEM):
    vmem = pl.BlockSpec(memory_space=pltpu.VMEM)
    given = pl.BlockSpec(memory_space=space)
    shapes = [jax.ShapeDtypeStruct(shape, jnp.float32) for shape in outs]

    def run(*args):
        return pl.pallas_call(
            kernel,
            out_shape=shapes if len(shapes) > 1 else shapes[0],
            in_specs=[given] * len(args),
            out_specs=[vmem] * len(shapes) if len(shapes) > 1 else vmem,
            scratch_shapes=[
                pltpu.VMEM(shape, jnp.float32) if isinstance(shape, tuple) else shape
                for shape in scratch
            ],
            cost_estimate=pl.CostEstimate(flops=cost, bytes_accessed=cost // 4, transcendentals=0),
            name=name,
            compiler_params=pltpu.CompilerParams(vmem_limit_bytes=16 * 1024 * 1024),
        )(*args)

    return run


def by_columns(state, labels):
    _, _, rows, nx = state.shape
    count_a, count_b = lax.axis_size("aa"), lax.axis_size("ba")
    devices = count_a * count_b
    used = (FIELDS + 1 + CHANGED) * rows + 1
    padded = -(-used // 128) * 128

    def swap(array):
        parts = array.reshape(devices, nx // devices, padded)
        return lax.all_to_all(parts, ("aa", "ba"), 0, 0, tiled=True).reshape(nx, padded)

    columns = call(
        columns_kernel,
        [(nx, padded)],
        [
            state.shape,
            pltpu.VMEM(labels.shape, labels.dtype),
            (FIELDS + 1, 2 * rows, nx),
            (padded, nx),
            pltpu.SemaphoreType.DMA((2,)),
        ],
        4_000_000,
        "columns",
        pl.ANY,
    )(state, labels)
    faces = up8(rows + 1)
    swept = call(
        functools.partial(sweeps_kernel, rows, count_a, count_b),
        [(nx, padded)],
        [
            (padded, nx),
            (FIELDS + 1, up8(2 * REACH - 1 + faces), nx),
            (CHANGED, faces, nx),
            (FIELDS + 1, 2 * rows, nx),
        ],
        8_000_000,
        "sweeps",
    )(swap(columns))
    return call(home_kernel, [state.shape], [], 100_000, "home")(swap(swept))


def shards(state, labels):
    _, depth, rows, nx = state.shape
    assert depth == 1 and rows >= REACH and nx % 128 == 0
    count_a, count_b = lax.axis_size("aa"), lax.axis_size("ba")
    devices = count_a * count_b
    if nx % devices == 0:
        return by_columns(state, labels)
    total = rows + 2 * REACH
    tall = up8(total)
    small = devices <= SMALL_GROUP
    peak, packed = call(
        peak_kernel,
        [(devices if small else 8, 128), (FIELDS + 1, rows, nx)],
        [],
        200_000,
        "peak",
    )(state, labels)
    ups = [(i, i + 1) for i in range(count_a - 1)]
    low = lax.ppermute(packed, "aa", ups)
    high = lax.ppermute(packed, "aa", [(j, i) for i, j in ups])
    if small:
        peaks = lax.all_to_all(peak, ("aa", "ba"), 0, 0, tiled=True)
    else:
        peaks = lax.pmax(peak, ("aa", "ba"))
    cells, change = call(
        x_kernel,
        [(FIELDS + 1, tall, nx), (8, tall, nx)],
        [(FIELDS + 1, up8(2 * total), nx)],
        4_000_000,
        "xflux",
    )(packed, low, high)
    exchange = count_b <= SMALL_AXIS
    faces = up8(rows + 1)
    after_y, step = call(
        y_kernel,
        [(count_b if exchange else 1, FIELDS + 1, rows, nx), (8, 128)],
        [(FIELDS + 1, max(tall, up8(2 * REACH - 1 + faces)), nx), (8, faces, nx)],
        4_000_000,
        "ysweep",
    )(peaks, cells, change)
    if exchange:
        lines = lax.all_to_all(after_y, "ba", 0, 0, tiled=True)
    else:
        near = []
        for shift in range(-REACH, REACH + 1):
            pairs = [(i, i - shift) for i in range(count_b) if 0 <= i - shift < count_b]
            near.append(lax.ppermute(after_y, "ba", pairs) if shift else after_y)
        lines = jnp.concatenate(near, axis=0)
    return call(
        functools.partial(z_kernel, not exchange),
        [(FIELDS, 1, rows, nx)],
        [(FIELDS + 1, (2 * REACH + 1) * rows, nx)],
        4_000_000,
        "zsweep",
    )(step, lines)


def solution(mesh):
    return jax.shard_map(
        shards,
        mesh=mesh,
        in_specs=(P(None, "ba", "aa", None), P("ba", "aa", None)),
        out_specs=P(None, "ba", "aa", None),
        check_vma=False,
    )
```

```python
import functools

import jax
import jax.numpy as jnp
from jax import lax
from jax.experimental import pallas as pl
from jax.experimental.pallas import tpu as pltpu
from jax.sharding import PartitionSpec as P

RETURN_ITERS = 2
REACH = 3
FIELDS = 14
DENSITY_FLOOR = 0.2
TRACTION_FLOOR = 0.1
COURANT = 0.4
WENO_EPSILON = 1e-06
SMALL_GROUP = 32
SMALL_AXIS = 8


def pick(label, sand, solid, void):
    return jnp.where(label == 0.0, sand, jnp.where(label == 1.0, solid, void))


def material(label):
    gamma = pick(label, 3.0, 4.0, 1.4)
    stiff = jnp.where(label == 1.0, 6.0, jnp.where(label == 0.0, 1.0, 0.0))
    shear = pick(label, 0.6, 3.0, 0.0)
    return gamma, stiff, shear


def deviator(grad):
    metric = {}
    for i in range(3):
        for j in range(i, 3):
            metric[i, j] = (
                grad[0][i] * grad[0][j] + grad[1][i] * grad[1][j] + grad[2][i] * grad[2][j]
            )
    third = (metric[0, 0] + metric[1, 1] + metric[2, 2]) * (1.0 / 3.0)
    for i in range(3):
        metric[i, i] = metric[i, i] - third
    return metric


def square_sum(dev):
    off = dev[0, 1] * dev[0, 1] + dev[0, 2] * dev[0, 2] + dev[1, 2] * dev[1, 2]
    diag = dev[0, 0] * dev[0, 0] + dev[1, 1] * dev[1, 1] + dev[2, 2] * dev[2, 2]
    return diag + (off + off)


def grad_of(fields):
    return [[fields[5 + 3 * row + col] for col in range(3)] for row in range(3)]


def pressure_of(fields, dev, mats):
    gamma, stiff, shear = mats
    density = jnp.maximum(fields[0], DENSITY_FLOOR)
    inverse = 1.0 / density
    velocity = [fields[1 + comp] * inverse for comp in range(3)]
    kinetic = 0.5 * (
        fields[1] * velocity[0] + fields[2] * velocity[1] + fields[3] * velocity[2]
    )
    energy = (0.25 * shear) * square_sum(dev)
    pressure = (gamma - 1.0) * (fields[4] - kinetic - energy) - gamma * stiff
    return density, inverse, velocity, pressure


def primitives(fields, mats):
    gamma, stiff, shear = mats
    dev = deviator(grad_of(fields))
    density, inverse, velocity, pressure = pressure_of(fields, dev, mats)
    sound = jnp.sqrt(
        (gamma * jnp.maximum(pressure + stiff, TRACTION_FLOOR) + (4.0 / 3.0) * shear) * inverse
    )
    return density, velocity, dev, pressure, sound


def weno_pair(v):
    d = [v[i + 1] - v[i] for i in range(5)]
    b = [d[i + 1] - d[i] for i in range(4)]
    d1, d2, d3 = d[1] + d[1], d[2] + d[2], d[3] + d[3]
    bend = [4.0 * WENO_EPSILON + (13.0 / 3.0) * (x * x) for x in b]
    outer0, outer3 = (4.0 / 3.0) * b[0], (4.0 / 3.0) * b[3]
    inner1, inner2 = (2.0 / 3.0) * b[1], (2.0 / 3.0) * b[2]

    def shift(slopes, bends, steps):
        inv = [1.0 / (bends[i] + slopes[i] * slopes[i]) for i in range(3)]
        weight = [inv[0] * inv[0], 6.0 * (inv[1] * inv[1]), 3.0 * (inv[2] * inv[2])]
        total = weight[0] * steps[0] + weight[1] * steps[1] + weight[2] * steps[2]
        return 0.25 * (total / (weight[0] + weight[1] + weight[2]))

    left = v[2] + shift(
        (d1 + b[0], d1 + b[1], d2 - b[2]),
        (bend[0], bend[1], bend[2]),
        (d1 + outer0, d2 - inner1, d2 - inner2),
    )
    right = v[3] - shift(
        (d3 - b[3], d2 + b[2], d2 + b[1]),
        (bend[3], bend[2], bend[1]),
        (d3 - outer3, d2 + inner2, d2 + inner1),
    )
    return left, right


def riemann(lf, rf, left_label, right_label, d):
    left_mats, right_mats = material(left_label), material(right_label)
    l_rho, l_vel, l_dev, l_p, l_c = primitives(lf, left_mats)
    r_rho, r_vel, r_dev, r_p, r_c = primitives(rf, right_mats)

    def stress(dev, mats, i, j):
        return -mats[2] * dev[min(i, j), max(i, j)]

    l_s = [stress(l_dev, left_mats, k, d) for k in range(3)]
    r_s = [stress(r_dev, right_mats, k, d) for k in range(3)]
    l_u, r_u = l_vel[d], r_vel[d]
    slow = jnp.minimum(l_u - l_c, r_u - r_c)
    fast = jnp.maximum(l_u + l_c, r_u + r_c)
    l_t, r_t = l_p - l_s[d], r_p - r_s[d]
    l_gap, r_gap = slow - l_u, fast - r_u
    l_push, r_push = l_rho * l_gap, r_rho * r_gap
    contact = (r_t - l_t + l_push * l_u - r_push * r_u) / (l_push - r_push)
    width = fast - slow
    margin = 0.05 * width
    contact = jnp.minimum(jnp.maximum(contact, slow + margin), fast - margin)

    go_left = (slow >= 0.0) | (contact >= 0.0)
    plain = (slow >= 0.0) | (jnp.logical_not(contact >= 0.0) & jnp.logical_not(fast > 0.0))

    def side(a, b):
        return jnp.where(go_left, a, b)

    rho, gap, wave, trac = side(l_rho, r_rho), side(l_gap, r_gap), side(slow, fast), side(l_t, r_t)
    vel = [side(l_vel[k], r_vel[k]) for k in range(3)]
    mom = [side(lf[1 + k], rf[1 + k]) for k in range(3)]
    ener = side(lf[4], rf[4])
    u = vel[d]
    ratio = gap / (wave - contact)
    mass = rho * ratio
    star_e = ratio * (ener + (contact - u) * (rho * contact + trac / gap))
    result = [mom[d] + jnp.where(plain, 0.0, wave * (mass - rho))]
    for k in range(3):
        flux = mom[k] * u + trac if k == d else mom[k] * u
        star = mass * (contact if k == d else vel[k])
        result.append(flux + jnp.where(plain, 0.0, wave * (star - mom[k])))
    result.append((ener + trac) * u + jnp.where(plain, 0.0, wave * (star_e - ener)))
    for k in range(3):
        if k != d:
            result[1 + k] = result[1 + k] - 0.5 * (l_s[k] + r_s[k])
            result[4] = result[4] - 0.5 * (l_s[k] * l_vel[k] + r_s[k] * r_vel[k])
    inverse = 1.0 / width
    for row in range(3):
        base = 5 + 3 * row
        l_flow = lf[base] * l_vel[0] + lf[base + 1] * l_vel[1] + lf[base + 2] * l_vel[2]
        r_flow = rf[base] * r_vel[0] + rf[base + 1] * r_vel[1] + rf[base + 2] * r_vel[2]
        jump = rf[base + d] - lf[base + d]
        blend = (fast * l_flow - slow * r_flow + slow * fast * jump) * inverse
        result.append(jnp.where(slow >= 0.0, l_flow, jnp.where(fast <= 0.0, r_flow, blend)))
    return result


def changed_fields(d):
    return [0, 1, 2, 3, 4] + [5 + 3 * row + d for row in range(3)]


def face_fluxes(window, d):
    left, right = [], []
    for field in range(FIELDS):
        a, b = weno_pair([window(field, k) for k in range(6)])
        left.append(a)
        right.append(b)
    return riemann(left, right, window(FIELDS, 2), window(FIELDS, 3), d)


def plastic(fields, label):
    mats = material(label)
    shear = mats[2]
    sandy = label == 0.0
    grad = grad_of(fields)
    dev = deviator(grad)
    pressure = pressure_of(fields, dev, mats)[3]
    radius = jnp.where(sandy, 0.05 + 0.4 * jnp.maximum(pressure, 0.0), 1.0)
    for turn in range(RETURN_ITERS):
        if turn:
            dev = deviator(grad)
        scaled = {key: shear * value for key, value in dev.items()}
        norm = jnp.sqrt(square_sum(scaled))
        factor = jnp.where(sandy, 0.5 * (1.0 + radius / jnp.maximum(norm, radius)), 1.0)
        third = (1.0 - factor) * ((grad[0][0] + grad[1][1] + grad[2][2]) * (1.0 / 3.0))
        grad = [
            [factor * grad[i][j] + third if i == j else factor * grad[i][j] for j in range(3)]
            for i in range(3)
        ]
    return list(fields[:5]) + [grad[i][j] for i in range(3) for j in range(3)]


def peak_kernel(state_ref, label_ref, peak_ref, packed_ref):
    rows = state_ref.shape[2]
    label = label_ref[0].astype(jnp.float32)
    fields = [state_ref[field, 0] for field in range(FIELDS)]
    for field in range(FIELDS):
        packed_ref[field] = fields[field]
    packed_ref[FIELDS] = label
    density, velocity, dev, pressure, sound = primitives(fields, material(label))
    speed = sound + jnp.maximum(
        jnp.maximum(jnp.abs(velocity[0]), jnp.abs(velocity[1])), jnp.abs(velocity[2])
    )
    best = speed[:, :128]
    for start in range(128, speed.shape[1], 128):
        best = jnp.maximum(best, speed[:, start : start + 128])
    best = jnp.max(best, axis=0, keepdims=True)
    peak_ref[...] = jnp.broadcast_to(best, peak_ref.shape)


def x_kernel(own_ref, low_ref, high_ref, out_ref, flux_ref, line_ref):
    rows, nx = own_ref.shape[1:]
    total = rows + 2 * REACH
    stack = line_ref.shape[1]
    pos, count = lax.axis_index("aa"), lax.axis_size("aa")
    first, last = pos == 0, pos == count - 1
    for field in range(FIELDS + 1):
        own = own_ref[field]
        low = jnp.where(first, own[:1], low_ref[field, rows - REACH :])
        high = jnp.where(last, own[rows - 1 :], high_ref[field, :REACH])
        out_ref[field, :REACH] = low
        out_ref[field, REACH : REACH + rows] = own
        out_ref[field, REACH + rows : total] = high
        out_ref[field, total:] = jnp.zeros((out_ref.shape[1] - total, nx), jnp.float32)
    lane = lax.broadcasted_iota(jnp.int32, (total, nx), 1)
    wide = lax.broadcasted_iota(jnp.int32, (stack, nx), 1)
    for field in range(FIELDS + 1):
        cells = out_ref[field, :total]
        line_ref[field, :total] = cells
        line_ref[field, total : 2 * total] = jnp.where(
            lane == nx - 1, cells, pltpu.roll(cells, nx - 1, 1)
        )
        if stack > 2 * total:
            line_ref[field, 2 * total :] = jnp.zeros((stack - 2 * total, nx), jnp.float32)
    cache = {}

    def window(field, k):
        if (field, k) not in cache:
            if k == 3:
                value = line_ref[field]
            elif k < 3:
                near = window(field, k + 1)
                value = jnp.where(wide == 0, near, pltpu.roll(near, 1, 1))
            else:
                near = window(field, k - 1)
                value = jnp.where(wide == nx - 1, near, pltpu.roll(near, nx - 1, 1))
            cache[field, k] = value
        return cache[field, k]

    for slot, flux in enumerate(face_fluxes(window, 0)):
        line_ref[slot] = flux
    for slot in range(8):
        lower = line_ref[slot, :total]
        upper = line_ref[slot, total : 2 * total]
        flux_ref[slot, :total] = (
            jnp.where(lane == nx - 1, upper, pltpu.roll(lower, nx - 1, 1)) - lower
        )
        flux_ref[slot, total:] = jnp.zeros((flux_ref.shape[1] - total, nx), jnp.float32)


def step_of(peak_ref):
    best = jnp.max(peak_ref[...], axis=0, keepdims=True)
    return COURANT / jnp.max(best, axis=1, keepdims=True)


def y_kernel(peak_ref, cells_ref, change_ref, out_ref, step_ref, line_ref, face_ref):
    copies, _, rows, nx = out_ref.shape
    step = step_of(peak_ref)
    step_ref[...] = jnp.broadcast_to(step, step_ref.shape)
    label = cells_ref[FIELDS]
    fields = [cells_ref[field] for field in range(FIELDS)]
    for slot, field in enumerate(changed_fields(0)):
        fields[field] = fields[field] - step * change_ref[slot]
    fields = plastic(fields, label)
    height = label.shape[0]
    for field in range(FIELDS):
        line_ref[field, :height] = fields[field]
    line_ref[FIELDS, :height] = label
    faces = face_ref.shape[1]
    for field in range(FIELDS + 1):
        if line_ref.shape[1] > height:
            line_ref[field, height:] = jnp.zeros((line_ref.shape[1] - height, nx), jnp.float32)
    fluxes = face_fluxes(lambda field, k: line_ref[field, k : k + faces], 1)
    for slot in range(8):
        face_ref[slot] = fluxes[slot]
    label = line_ref[FIELDS, REACH : REACH + rows]
    fields = [line_ref[field, REACH : REACH + rows] for field in range(FIELDS)]
    for slot, field in enumerate(changed_fields(1)):
        change = face_ref[slot, 1 : rows + 1] - face_ref[slot, :rows]
        fields[field] = fields[field] - step * change
    fields = plastic(fields, label) + [label]
    for copy in range(copies):
        for field in range(FIELDS + 1):
            out_ref[copy, field] = fields[field]


def z_kernel(centred, step_ref, lines_ref, out_ref, line_ref):
    rows = out_ref.shape[2]
    pos, count = lax.axis_index("ba"), lax.axis_size("ba")
    step = step_ref[:rows, :1]
    for k in range(2 * REACH + 1):
        where = jnp.clip(pos + k - REACH, 0, count - 1)
        if centred:
            where = where - pos + REACH
        for field in range(FIELDS + 1):
            line_ref[field, k * rows : (k + 1) * rows] = lines_ref[where, field]
    fluxes = face_fluxes(
        lambda field, k: line_ref[field, k * rows : (k + 2) * rows], 2
    )
    centre = slice(REACH * rows, (REACH + 1) * rows)
    label = line_ref[FIELDS, centre]
    fields = [line_ref[field, centre] for field in range(FIELDS)]
    for slot, field in enumerate(changed_fields(2)):
        fields[field] = fields[field] - step * (fluxes[slot][rows:] - fluxes[slot][:rows])
    fields = plastic(fields, label)
    for field in range(FIELDS):
        out_ref[field, 0] = fields[field]


CHANGED = 8


def columns_kernel(
    state_ref, label_ref, out_ref, line_ref, stage_ref
):
    _, _, rows, nx = state_ref.shape
    label = label_ref[0]
    fields = [state_ref[field, 0] for field in range(FIELDS)]
    lane = lax.broadcasted_iota(jnp.int32, (rows, nx), 1)
    wide = lax.broadcasted_iota(jnp.int32, (2 * rows, nx), 1)
    for field, cells in enumerate(fields + [label]):
        stage_ref[field * rows : (field + 1) * rows] = cells
        line_ref[field, :rows] = cells
        line_ref[field, rows:] = jnp.where(lane == nx - 1, cells, pltpu.roll(cells, nx - 1, 1))
    density, velocity, dev, pressure, sound = primitives(fields, material(label))
    speed = sound + jnp.maximum(
        jnp.maximum(jnp.abs(velocity[0]), jnp.abs(velocity[1])), jnp.abs(velocity[2])
    )
    used = (FIELDS + 1 + CHANGED) * rows
    stage_ref[used:] = jnp.broadcast_to(
        jnp.max(speed, keepdims=True), (stage_ref.shape[0] - used, nx)
    )
    window = shifter(line_ref, wide == 0, wide == nx - 1, 1)
    for slot, flux in enumerate(face_fluxes(window, 0)):
        lower, upper = flux[:rows], flux[rows:]
        change = jnp.where(lane == nx - 1, upper, pltpu.roll(lower, nx - 1, 1)) - lower
        start = (FIELDS + 1 + slot) * rows
        stage_ref[start : start + rows] = change
    tall = stage_ref.shape[0]
    out_ref[:, :tall] = stage_ref[...].T


def shifter(line_ref, first, last, width):
    nx = line_ref.shape[2]
    cache = {}

    def window(field, k):
        if (field, k) not in cache:
            if k == REACH:
                value = line_ref[field]
            elif k < REACH:
                near = window(field, k + 1)
                value = jnp.where(first, near, pltpu.roll(near, width, 1))
            else:
                near = window(field, k - 1)
                value = jnp.where(last, near, pltpu.roll(near, nx - width, 1))
            cache[field, k] = value
        return cache[field, k]

    return window


def sweeps_kernel(rows, count_a, count_b, in_ref, out_ref, stage_ref, line_ref, face_ref, deep_ref):
    nx = in_ref.shape[0]
    group = nx // count_a
    width = group // count_b
    tall = stage_ref.shape[0]
    stage_ref[...] = in_ref[:, :tall].T
    used = (FIELDS + 1 + CHANGED) * rows
    best = jnp.max(stage_ref[used : used + 1, :], axis=1, keepdims=True)
    step = COURANT / best

    def block(index):
        return stage_ref[index * rows : (index + 1) * rows, :]

    label = block(FIELDS)
    fields = [block(field) for field in range(FIELDS)]
    for slot, field in enumerate(changed_fields(0)):
        fields[field] = fields[field] - step * block(FIELDS + 1 + slot)
    fields = plastic(fields, label)

    lane = lax.broadcasted_iota(jnp.int32, (REACH, nx), 1)
    faces = face_ref.shape[1]
    for field, cells in enumerate(fields + [label]):
        low = pltpu.roll(cells, group, 1)[rows - REACH :]
        high = pltpu.roll(cells, nx - group, 1)[:REACH]
        line_ref[field, :REACH] = jnp.where(lane < group, cells[:1], low)
        line_ref[field, REACH : REACH + rows] = cells
        line_ref[field, REACH + rows : 2 * REACH + rows] = jnp.where(
            lane >= nx - group, cells[rows - 1 :], high
        )
        rest = line_ref.shape[1] - 2 * REACH - rows
        line_ref[field, 2 * REACH + rows :] = jnp.zeros((rest, nx), jnp.float32)
    fluxes = face_fluxes(lambda field, k: line_ref[field, k : k + faces], 1)
    for slot in range(CHANGED):
        face_ref[slot] = fluxes[slot]
    for slot, field in enumerate(changed_fields(1)):
        change = face_ref[slot, 1 : rows + 1] - face_ref[slot, :rows]
        fields[field] = fields[field] - step * change
    fields = plastic(fields, label)

    lane = lax.broadcasted_iota(jnp.int32, (2 * rows, nx), 1)
    first = lane < 0
    last = lane < 0
    for a in range(count_a):
        start, end = a * group, (a + 1) * group
        first = first | ((lane >= start) & (lane < start + width))
        last = last | ((lane >= end - width) & (lane < end))
    short = last[:rows]
    for field, cells in enumerate(fields + [label]):
        deep_ref[field, :rows] = cells
        deep_ref[field, rows:] = jnp.where(short, cells, pltpu.roll(cells, nx - width, 1))
    window = shifter(deep_ref, first, last, width)
    fluxes = face_fluxes(window, 2)
    for slot, field in enumerate(changed_fields(2)):
        lower, upper = fluxes[slot][:rows], fluxes[slot][rows:]
        change = jnp.where(short, upper, pltpu.roll(lower, nx - width, 1)) - lower
        fields[field] = fields[field] - step * change
    fields = plastic(fields, label)
    for field in range(FIELDS):
        stage_ref[field * rows : (field + 1) * rows, :] = fields[field]
    tall = up8(FIELDS * rows)
    out_ref[:, :tall] = stage_ref[:tall].T


def home_kernel(in_ref, out_ref):
    _, _, rows, _ = out_ref.shape
    back = in_ref[:, : up8(FIELDS * rows)].T
    for field in range(FIELDS):
        out_ref[field, 0] = back[field * rows : (field + 1) * rows]


def up8(size):
    return -(-size // 8) * 8


def call(kernel, outs, scratch, cost, name, space=pltpu.VMEM, fuse=None):
    vmem = pl.BlockSpec(memory_space=pltpu.VMEM)
    given = pl.BlockSpec(memory_space=space)
    shapes = [jax.ShapeDtypeStruct(shape, jnp.float32) for shape in outs]

    def run(*args):
        return pl.pallas_call(
            kernel,
            out_shape=shapes if len(shapes) > 1 else shapes[0],
            in_specs=[given] * len(args),
            out_specs=[vmem] * len(shapes) if len(shapes) > 1 else vmem,
            scratch_shapes=[
                pltpu.VMEM(shape, jnp.float32) if isinstance(shape, tuple) else shape
                for shape in scratch
            ],
            cost_estimate=pl.CostEstimate(flops=cost, bytes_accessed=cost // 4, transcendentals=0),
            name=name,
            compiler_params=pltpu.CompilerParams(vmem_limit_bytes=16 * 1024 * 1024, allow_input_fusion=fuse),
        )(*args)

    return run


def by_columns(state, labels):
    _, _, rows, nx = state.shape
    count_a, count_b = lax.axis_size("aa"), lax.axis_size("ba")
    devices = count_a * count_b
    used = (FIELDS + 1 + CHANGED) * rows + 1
    padded = -(-used // 128) * 128

    def swap(array):
        parts = array.reshape(devices, nx // devices, padded)
        return lax.all_to_all(parts, ("aa", "ba"), 0, 0, tiled=True).reshape(nx, padded)

    columns = call(
        columns_kernel,
        [(nx, padded)],
        [
            (FIELDS + 1, 2 * rows, nx),
            (up8(used), nx),
        ],
        4_000_000,
        "columns",
        fuse=[False, True],
    )(state, labels.astype(jnp.float32))
    faces = up8(rows + 1)
    swept = call(
        functools.partial(sweeps_kernel, rows, count_a, count_b),
        [(nx, padded)],
        [
            (up8(used), nx),
            (FIELDS + 1, up8(2 * REACH - 1 + faces), nx),
            (CHANGED, faces, nx),
            (FIELDS + 1, 2 * rows, nx),
        ],
        8_000_000,
        "sweeps",
    )(swap(columns))
    return call(home_kernel, [state.shape], [], 100_000, "home")(swap(swept))


def shards(state, labels):
    _, depth, rows, nx = state.shape
    assert depth == 1 and rows >= REACH and nx % 128 == 0
    count_a, count_b = lax.axis_size("aa"), lax.axis_size("ba")
    devices = count_a * count_b
    if nx % devices == 0:
        return by_columns(state, labels)
    total = rows + 2 * REACH
    tall = up8(total)
    small = devices <= SMALL_GROUP
    peak, packed = call(
        peak_kernel,
        [(devices if small else 8, 128), (FIELDS + 1, rows, nx)],
        [],
        200_000,
        "peak",
    )(state, labels)
    ups = [(i, i + 1) for i in range(count_a - 1)]
    low = lax.ppermute(packed, "aa", ups)
    high = lax.ppermute(packed, "aa", [(j, i) for i, j in ups])
    if small:
        peaks = lax.all_to_all(peak, ("aa", "ba"), 0, 0, tiled=True)
    else:
        peaks = lax.pmax(peak, ("aa", "ba"))
    cells, change = call(
        x_kernel,
        [(FIELDS + 1, tall, nx), (8, tall, nx)],
        [(FIELDS + 1, up8(2 * total), nx)],
        4_000_000,
        "xflux",
    )(packed, low, high)
    exchange = count_b <= SMALL_AXIS
    faces = up8(rows + 1)
    after_y, step = call(
        y_kernel,
        [(count_b if exchange else 1, FIELDS + 1, rows, nx), (8, 128)],
        [(FIELDS + 1, max(tall, up8(2 * REACH - 1 + faces)), nx), (8, faces, nx)],
        4_000_000,
        "ysweep",
    )(peaks, cells, change)
    if exchange:
        lines = lax.all_to_all(after_y, "ba", 0, 0, tiled=True)
    else:
        near = []
        for shift in range(-REACH, REACH + 1):
            pairs = [(i, i - shift) for i in range(count_b) if 0 <= i - shift < count_b]
            near.append(lax.ppermute(after_y, "ba", pairs) if shift else after_y)
        lines = jnp.concatenate(near, axis=0)
    return call(
        functools.partial(z_kernel, not exchange),
        [(FIELDS, 1, rows, nx)],
        [(FIELDS + 1, (2 * REACH + 1) * rows, nx)],
        4_000_000,
        "zsweep",
    )(step, lines)


def solution(mesh):
    return jax.shard_map(
        shards,
        mesh=mesh,
        in_specs=(P(None, "ba", "aa", None), P("ba", "aa", None)),
        out_specs=P(None, "ba", "aa", None),
        check_vma=False,
    )
```

```python
import functools

import jax
import jax.numpy as jnp
from jax import lax
from jax.experimental import pallas as pl
from jax.experimental.pallas import tpu as pltpu
from jax.sharding import PartitionSpec as P

RETURN_ITERS = 2
REACH = 3
FIELDS = 14
DENSITY_FLOOR = 0.2
TRACTION_FLOOR = 0.1
COURANT = 0.4
WENO_EPSILON = 1e-06
SMALL_GROUP = 32
SMALL_AXIS = 8


def pick(label, sand, solid, void):
    return jnp.where(label == 0.0, sand, jnp.where(label == 1.0, solid, void))


def material(label):
    gamma = pick(label, 3.0, 4.0, 1.4)
    stiff = jnp.where(label == 1.0, 6.0, jnp.where(label == 0.0, 1.0, 0.0))
    shear = pick(label, 0.6, 3.0, 0.0)
    return gamma, stiff, shear


def deviator(grad):
    metric = {}
    for i in range(3):
        for j in range(i, 3):
            metric[i, j] = (
                grad[0][i] * grad[0][j] + grad[1][i] * grad[1][j] + grad[2][i] * grad[2][j]
            )
    third = (metric[0, 0] + metric[1, 1] + metric[2, 2]) * (1.0 / 3.0)
    for i in range(3):
        metric[i, i] = metric[i, i] - third
    return metric


def square_sum(dev):
    off = dev[0, 1] * dev[0, 1] + dev[0, 2] * dev[0, 2] + dev[1, 2] * dev[1, 2]
    diag = dev[0, 0] * dev[0, 0] + dev[1, 1] * dev[1, 1] + dev[2, 2] * dev[2, 2]
    return diag + (off + off)


def grad_of(fields):
    return [[fields[5 + 3 * row + col] for col in range(3)] for row in range(3)]


def pressure_of(fields, dev, mats):
    gamma, stiff, shear = mats
    density = jnp.maximum(fields[0], DENSITY_FLOOR)
    inverse = 1.0 / density
    velocity = [fields[1 + comp] * inverse for comp in range(3)]
    kinetic = 0.5 * (
        fields[1] * velocity[0] + fields[2] * velocity[1] + fields[3] * velocity[2]
    )
    energy = (0.25 * shear) * square_sum(dev)
    pressure = (gamma - 1.0) * (fields[4] - kinetic - energy) - gamma * stiff
    return density, inverse, velocity, pressure


def primitives(fields, mats):
    gamma, stiff, shear = mats
    dev = deviator(grad_of(fields))
    density, inverse, velocity, pressure = pressure_of(fields, dev, mats)
    sound = jnp.sqrt(
        (gamma * jnp.maximum(pressure + stiff, TRACTION_FLOOR) + (4.0 / 3.0) * shear) * inverse
    )
    return density, velocity, dev, pressure, sound


def weno_pair(v):
    d = [v[i + 1] - v[i] for i in range(5)]
    b = [d[i + 1] - d[i] for i in range(4)]
    d1, d2, d3 = d[1] + d[1], d[2] + d[2], d[3] + d[3]
    bend = [4.0 * WENO_EPSILON + (13.0 / 3.0) * (x * x) for x in b]
    outer0, outer3 = (4.0 / 3.0) * b[0], (4.0 / 3.0) * b[3]
    inner1, inner2 = (2.0 / 3.0) * b[1], (2.0 / 3.0) * b[2]

    def shift(slopes, bends, steps):
        inv = [1.0 / (bends[i] + slopes[i] * slopes[i]) for i in range(3)]
        weight = [inv[0] * inv[0], 6.0 * (inv[1] * inv[1]), 3.0 * (inv[2] * inv[2])]
        total = weight[0] * steps[0] + weight[1] * steps[1] + weight[2] * steps[2]
        return 0.25 * (total / (weight[0] + weight[1] + weight[2]))

    left = v[2] + shift(
        (d1 + b[0], d1 + b[1], d2 - b[2]),
        (bend[0], bend[1], bend[2]),
        (d1 + outer0, d2 - inner1, d2 - inner2),
    )
    right = v[3] - shift(
        (d3 - b[3], d2 + b[2], d2 + b[1]),
        (bend[3], bend[2], bend[1]),
        (d3 - outer3, d2 + inner2, d2 + inner1),
    )
    return left, right


def riemann(lf, rf, left_label, right_label, d):
    left_mats, right_mats = material(left_label), material(right_label)
    l_rho, l_vel, l_dev, l_p, l_c = primitives(lf, left_mats)
    r_rho, r_vel, r_dev, r_p, r_c = primitives(rf, right_mats)

    def stress(dev, mats, i, j):
        return -mats[2] * dev[min(i, j), max(i, j)]

    l_s = [stress(l_dev, left_mats, k, d) for k in range(3)]
    r_s = [stress(r_dev, right_mats, k, d) for k in range(3)]
    l_u, r_u = l_vel[d], r_vel[d]
    slow = jnp.minimum(l_u - l_c, r_u - r_c)
    fast = jnp.maximum(l_u + l_c, r_u + r_c)
    l_t, r_t = l_p - l_s[d], r_p - r_s[d]
    l_gap, r_gap = slow - l_u, fast - r_u
    l_push, r_push = l_rho * l_gap, r_rho * r_gap
    contact = (r_t - l_t + l_push * l_u - r_push * r_u) / (l_push - r_push)
    width = fast - slow
    margin = 0.05 * width
    contact = jnp.minimum(jnp.maximum(contact, slow + margin), fast - margin)

    go_left = (slow >= 0.0) | (contact >= 0.0)
    plain = (slow >= 0.0) | (jnp.logical_not(contact >= 0.0) & jnp.logical_not(fast > 0.0))

    def side(a, b):
        return jnp.where(go_left, a, b)

    rho, gap, wave, trac = side(l_rho, r_rho), side(l_gap, r_gap), side(slow, fast), side(l_t, r_t)
    vel = [side(l_vel[k], r_vel[k]) for k in range(3)]
    mom = [side(lf[1 + k], rf[1 + k]) for k in range(3)]
    ener = side(lf[4], rf[4])
    u = vel[d]
    ratio = gap / (wave - contact)
    mass = rho * ratio
    star_e = ratio * (ener + (contact - u) * (rho * contact + trac / gap))
    result = [mom[d] + jnp.where(plain, 0.0, wave * (mass - rho))]
    for k in range(3):
        flux = mom[k] * u + trac if k == d else mom[k] * u
        star = mass * (contact if k == d else vel[k])
        result.append(flux + jnp.where(plain, 0.0, wave * (star - mom[k])))
    result.append((ener + trac) * u + jnp.where(plain, 0.0, wave * (star_e - ener)))
    for k in range(3):
        if k != d:
            result[1 + k] = result[1 + k] - 0.5 * (l_s[k] + r_s[k])
            result[4] = result[4] - 0.5 * (l_s[k] * l_vel[k] + r_s[k] * r_vel[k])
    inverse = 1.0 / width
    for row in range(3):
        base = 5 + 3 * row
        l_flow = lf[base] * l_vel[0] + lf[base + 1] * l_vel[1] + lf[base + 2] * l_vel[2]
        r_flow = rf[base] * r_vel[0] + rf[base + 1] * r_vel[1] + rf[base + 2] * r_vel[2]
        jump = rf[base + d] - lf[base + d]
        blend = (fast * l_flow - slow * r_flow + slow * fast * jump) * inverse
        result.append(jnp.where(slow >= 0.0, l_flow, jnp.where(fast <= 0.0, r_flow, blend)))
    return result


def changed_fields(d):
    return [0, 1, 2, 3, 4] + [5 + 3 * row + d for row in range(3)]


def face_values(window, fields):
    return [weno_pair([window(field, k) for k in range(6)]) for field in fields]


def face_fluxes(window, d, values=()):
    values = list(values) + face_values(window, range(len(values), FIELDS))
    left = [value[0] for value in values]
    right = [value[1] for value in values]
    return riemann(left, right, window(FIELDS, 2), window(FIELDS, 3), d)


def plastic(fields, label):
    mats = material(label)
    sandy = label == 0.0
    grad = grad_of(fields)
    dev = deviator(grad)
    third = (grad[0][0] + grad[1][1] + grad[2][2]) * (1.0 / 3.0)
    rest = [[grad[i][j] - third if i == j else grad[i][j] for j in range(3)] for i in range(3)]
    even = {(i, j): third * (rest[i][j] + rest[j][i]) for i, j in dev}
    pure = {key: dev[key] - even[key] for key in dev}
    pressure = pressure_of(fields, dev, mats)[3]
    radius = 0.05 + 0.4 * jnp.maximum(pressure, 0.0)
    product = None
    for turn in range(RETURN_ITERS):
        if turn:
            dev = {key: product * (product * pure[key] + even[key]) for key in dev}
        norm = jnp.sqrt(0.36 * square_sum(dev))
        factor = 0.5 + 0.5 * (radius / jnp.maximum(norm, radius))
        product = product * factor if turn else factor
    product = jnp.where(sandy, product, 1.0)
    less = product - 1.0
    return list(fields[:5]) + [
        grad[i][j] + less * rest[i][j] if i == j else product * grad[i][j]
        for i in range(3)
        for j in range(3)
    ]


def peak_kernel(state_ref, label_ref, peak_ref, packed_ref):
    rows = state_ref.shape[2]
    label = label_ref[0].astype(jnp.float32)
    fields = [state_ref[field, 0] for field in range(FIELDS)]
    for field in range(FIELDS):
        packed_ref[field] = fields[field]
    packed_ref[FIELDS] = label
    density, velocity, dev, pressure, sound = primitives(fields, material(label))
    speed = sound + jnp.maximum(
        jnp.maximum(jnp.abs(velocity[0]), jnp.abs(velocity[1])), jnp.abs(velocity[2])
    )
    best = speed[:, :128]
    for start in range(128, speed.shape[1], 128):
        best = jnp.maximum(best, speed[:, start : start + 128])
    best = jnp.max(best, axis=0, keepdims=True)
    peak_ref[...] = jnp.broadcast_to(best, peak_ref.shape)


def x_kernel(own_ref, low_ref, high_ref, out_ref, flux_ref, line_ref):
    rows, nx = own_ref.shape[1:]
    total = rows + 2 * REACH
    stack = line_ref.shape[1]
    pos, count = lax.axis_index("aa"), lax.axis_size("aa")
    first, last = pos == 0, pos == count - 1
    for field in range(FIELDS + 1):
        own = own_ref[field]
        low = jnp.where(first, own[:1], low_ref[field, rows - REACH :])
        high = jnp.where(last, own[rows - 1 :], high_ref[field, :REACH])
        out_ref[field, :REACH] = low
        out_ref[field, REACH : REACH + rows] = own
        out_ref[field, REACH + rows : total] = high
        out_ref[field, total:] = jnp.zeros((out_ref.shape[1] - total, nx), jnp.float32)
    lane = lax.broadcasted_iota(jnp.int32, (total, nx), 1)
    wide = lax.broadcasted_iota(jnp.int32, (stack, nx), 1)
    for field in range(FIELDS + 1):
        cells = out_ref[field, :total]
        line_ref[field, :total] = cells
        line_ref[field, total : 2 * total] = jnp.where(
            lane == nx - 1, cells, pltpu.roll(cells, nx - 1, 1)
        )
        if stack > 2 * total:
            line_ref[field, 2 * total :] = jnp.zeros((stack - 2 * total, nx), jnp.float32)
    cache = {}

    def window(field, k):
        if (field, k) not in cache:
            if k == 3:
                value = line_ref[field]
            elif k < 3:
                near = window(field, k + 1)
                value = jnp.where(wide == 0, near, pltpu.roll(near, 1, 1))
            else:
                near = window(field, k - 1)
                value = jnp.where(wide == nx - 1, near, pltpu.roll(near, nx - 1, 1))
            cache[field, k] = value
        return cache[field, k]

    for slot, flux in enumerate(face_fluxes(window, 0)):
        line_ref[slot] = flux
    for slot in range(8):
        lower = line_ref[slot, :total]
        upper = line_ref[slot, total : 2 * total]
        flux_ref[slot, :total] = (
            jnp.where(lane == nx - 1, upper, pltpu.roll(lower, nx - 1, 1)) - lower
        )
        flux_ref[slot, total:] = jnp.zeros((flux_ref.shape[1] - total, nx), jnp.float32)


def step_of(peak_ref):
    best = jnp.max(peak_ref[...], axis=0, keepdims=True)
    return COURANT / jnp.max(best, axis=1, keepdims=True)


def y_kernel(peak_ref, cells_ref, change_ref, out_ref, step_ref, line_ref, face_ref):
    copies, _, rows, nx = out_ref.shape
    step = step_of(peak_ref)
    step_ref[...] = jnp.broadcast_to(step, step_ref.shape)
    label = cells_ref[FIELDS]
    fields = [cells_ref[field] for field in range(FIELDS)]
    for slot, field in enumerate(changed_fields(0)):
        fields[field] = fields[field] - step * change_ref[slot]
    fields = plastic(fields, label)
    height = label.shape[0]
    for field in range(FIELDS):
        line_ref[field, :height] = fields[field]
    line_ref[FIELDS, :height] = label
    faces = face_ref.shape[1]
    for field in range(FIELDS + 1):
        if line_ref.shape[1] > height:
            line_ref[field, height:] = jnp.zeros((line_ref.shape[1] - height, nx), jnp.float32)
    fluxes = face_fluxes(lambda field, k: line_ref[field, k : k + faces], 1)
    for slot in range(8):
        face_ref[slot] = fluxes[slot]
    label = line_ref[FIELDS, REACH : REACH + rows]
    fields = [line_ref[field, REACH : REACH + rows] for field in range(FIELDS)]
    for slot, field in enumerate(changed_fields(1)):
        change = face_ref[slot, 1 : rows + 1] - face_ref[slot, :rows]
        fields[field] = fields[field] - step * change
    fields = plastic(fields, label) + [label]
    for copy in range(copies):
        for field in range(FIELDS + 1):
            out_ref[copy, field] = fields[field]


def z_kernel(centred, step_ref, lines_ref, out_ref, line_ref):
    rows = out_ref.shape[2]
    pos, count = lax.axis_index("ba"), lax.axis_size("ba")
    step = step_ref[:rows, :1]
    for k in range(2 * REACH + 1):
        where = jnp.clip(pos + k - REACH, 0, count - 1)
        if centred:
            where = where - pos + REACH
        for field in range(FIELDS + 1):
            line_ref[field, k * rows : (k + 1) * rows] = lines_ref[where, field]
    fluxes = face_fluxes(
        lambda field, k: line_ref[field, k * rows : (k + 2) * rows], 2
    )
    centre = slice(REACH * rows, (REACH + 1) * rows)
    label = line_ref[FIELDS, centre]
    fields = [line_ref[field, centre] for field in range(FIELDS)]
    for slot, field in enumerate(changed_fields(2)):
        fields[field] = fields[field] - step * (fluxes[slot][rows:] - fluxes[slot][:rows])
    fields = plastic(fields, label)
    for field in range(FIELDS):
        out_ref[field, 0] = fields[field]


CHANGED = 8
KEPT = 5


def columns_kernel(
    state_ref, label_ref, out_ref, line_ref, stage_ref
):
    _, _, rows, nx = state_ref.shape
    label = label_ref[0]
    fields = [state_ref[field, 0] for field in range(FIELDS)]
    for field, cells in enumerate(fields + [label]):
        stage_ref[field * rows : (field + 1) * rows] = cells
        line_ref[field, :rows] = cells
        line_ref[field, rows:] = cells
    density, velocity, dev, pressure, sound = primitives(fields, material(label))
    speed = sound + jnp.maximum(
        jnp.maximum(jnp.abs(velocity[0]), jnp.abs(velocity[1])), jnp.abs(velocity[2])
    )
    used = (FIELDS + 1 + CHANGED) * rows
    stage_ref[used:] = jnp.broadcast_to(
        jnp.max(speed, keepdims=True), (stage_ref.shape[0] - used, nx)
    )
    window, change = line_window(line_ref, nx, 1)
    for slot, flux in enumerate(face_fluxes(window, 0)):
        start = (FIELDS + 1 + slot) * rows
        stage_ref[start : start + rows] = change(flux)
    tall = stage_ref.shape[0]
    out_ref[:, :tall] = stage_ref[...].T


def line_window(line_ref, group, width):
    rows, nx = line_ref.shape[1] // 2, line_ref.shape[2]
    shape = line_ref.shape[1:]
    lane = lax.broadcasted_iota(jnp.int32, shape, 1)
    upper = lax.broadcasted_iota(jnp.int32, shape, 0) >= rows

    def within(low, high):
        hit = lane < 0
        for start in range(0, nx, group):
            hit = hit | ((lane >= start + low) & (lane < start + high))
        return hit

    first = {n: within(0, n * width) & jnp.logical_not(upper) for n in range(1, 4)}
    last = {n: within(group - n * width, group) | upper for n in range(1, 3)}
    cache = {}

    def moved(field, cells):
        if (field, "moved", cells) not in cache:
            shift = cells * width if cells > 0 else nx + cells * width
            cache[field, "moved", cells] = pltpu.roll(line_ref[field], shift, 1)
        return cache[field, "moved", cells]

    def window(field, k):
        if (field, k) not in cache:
            away = k - REACH
            if away == 0:
                value = jnp.where(upper, moved(field, 1), line_ref[field])
            elif away == -1:
                value = jnp.where(first[1], line_ref[field], moved(field, 1))
            elif away < 0:
                value = jnp.where(first[-away], window(field, k + 1), moved(field, -away))
            else:
                value = jnp.where(last[away], window(field, k - 1), moved(field, -away))
            cache[field, k] = value
        return cache[field, k]

    start = within(0, width)[:rows]

    def change(flux):
        faces = jnp.where(start, flux[rows:], flux[:rows])
        return pltpu.roll(faces, nx - width, 1) - flux[:rows]

    return window, change


def sweeps_kernel(rows, count_a, count_b, in_ref, out_ref, stage_ref, line_ref, face_ref, deep_ref):
    nx = in_ref.shape[0]
    group = nx // count_a
    width = group // count_b
    tall = stage_ref.shape[0]
    stage_ref[...] = in_ref[:, :tall].T
    used = (FIELDS + 1 + CHANGED) * rows
    step = COURANT / jnp.max(in_ref[:, used : used + 1], axis=0, keepdims=True)

    def block(index):
        return stage_ref[index * rows : (index + 1) * rows, :]

    label = block(FIELDS)
    fields = [block(field) for field in range(FIELDS)]
    for slot, field in enumerate(changed_fields(0)):
        fields[field] = fields[field] - step * block(FIELDS + 1 + slot)

    lane = lax.broadcasted_iota(jnp.int32, (REACH, nx), 1)
    faces = face_ref.shape[1]

    def lay(field, cells):
        low = pltpu.roll(cells, group, 1)[rows - REACH :]
        high = pltpu.roll(cells, nx - group, 1)[:REACH]
        line_ref[field, :REACH] = jnp.where(lane < group, cells[:1], low)
        line_ref[field, REACH : REACH + rows] = cells
        line_ref[field, REACH + rows : 2 * REACH + rows] = jnp.where(
            lane >= nx - group, cells[rows - 1 :], high
        )
        rest = line_ref.shape[1] - 2 * REACH - rows
        line_ref[field, 2 * REACH + rows :] = jnp.zeros((rest, nx), jnp.float32)

    def window(field, k):
        return line_ref[field, k : k + faces]

    lay(FIELDS, label)
    for field in range(KEPT):
        lay(field, fields[field])
    values = face_values(window, range(KEPT))
    fields = plastic(fields, label)
    for field in range(KEPT, FIELDS):
        lay(field, fields[field])
    fluxes = face_fluxes(window, 1, values)
    for slot in range(CHANGED):
        face_ref[slot] = fluxes[slot]
    for slot, field in enumerate(changed_fields(1)):
        change = face_ref[slot, 1 : rows + 1] - face_ref[slot, :rows]
        fields[field] = fields[field] - step * change

    def stack(field, cells):
        deep_ref[field, :rows] = cells
        deep_ref[field, rows:] = cells

    window, change = line_window(deep_ref, group, width)
    stack(FIELDS, label)
    for field in range(KEPT):
        stack(field, fields[field])
    values = face_values(window, range(KEPT))
    fields = plastic(fields, label)
    for field in range(KEPT, FIELDS):
        stack(field, fields[field])
    fluxes = face_fluxes(window, 2, values)
    for slot, field in enumerate(changed_fields(2)):
        fields[field] = fields[field] - step * change(fluxes[slot])
    fields = plastic(fields, label)
    for field in range(FIELDS):
        stage_ref[field * rows : (field + 1) * rows, :] = fields[field]
    tall = up8(FIELDS * rows)
    out_ref[:, :tall] = stage_ref[:tall].T


def home_kernel(in_ref, out_ref):
    _, _, rows, _ = out_ref.shape
    back = in_ref[:, : up8(FIELDS * rows)].T
    for field in range(FIELDS):
        out_ref[field, 0] = back[field * rows : (field + 1) * rows]


def up8(size):
    return -(-size // 8) * 8


def call(kernel, outs, scratch, cost, name, space=pltpu.VMEM, fuse=None):
    vmem = pl.BlockSpec(memory_space=pltpu.VMEM)
    given = pl.BlockSpec(memory_space=space)
    shapes = [jax.ShapeDtypeStruct(shape, jnp.float32) for shape in outs]

    def run(*args):
        return pl.pallas_call(
            kernel,
            out_shape=shapes if len(shapes) > 1 else shapes[0],
            in_specs=[given] * len(args),
            out_specs=[vmem] * len(shapes) if len(shapes) > 1 else vmem,
            scratch_shapes=[
                pltpu.VMEM(shape, jnp.float32) if isinstance(shape, tuple) else shape
                for shape in scratch
            ],
            cost_estimate=pl.CostEstimate(flops=cost, bytes_accessed=cost // 4, transcendentals=0),
            name=name,
            compiler_params=pltpu.CompilerParams(vmem_limit_bytes=16 * 1024 * 1024, allow_input_fusion=fuse),
        )(*args)

    return run


def by_columns(state, labels):
    _, _, rows, nx = state.shape
    count_a, count_b = lax.axis_size("aa"), lax.axis_size("ba")
    devices = count_a * count_b
    used = (FIELDS + 1 + CHANGED) * rows + 1
    padded = -(-used // 128) * 128

    def swap(array):
        parts = array.reshape(devices, nx // devices, padded)
        return lax.all_to_all(parts, ("aa", "ba"), 0, 0, tiled=True).reshape(nx, padded)

    columns = call(
        columns_kernel,
        [(nx, padded)],
        [
            (FIELDS + 1, 2 * rows, nx),
            (up8(used), nx),
        ],
        4_000_000,
        "columns",
        fuse=[False, True],
    )(state, labels.astype(jnp.float32))
    faces = up8(rows + 1)
    swept = call(
        functools.partial(sweeps_kernel, rows, count_a, count_b),
        [(nx, padded)],
        [
            (up8(used), nx),
            (FIELDS + 1, up8(2 * REACH - 1 + faces), nx),
            (CHANGED, faces, nx),
            (FIELDS + 1, 2 * rows, nx),
        ],
        8_000_000,
        "sweeps",
    )(swap(columns))
    return call(home_kernel, [state.shape], [], 100_000, "home")(swap(swept))


def shards(state, labels):
    _, depth, rows, nx = state.shape
    assert depth == 1 and rows >= REACH and nx % 128 == 0
    count_a, count_b = lax.axis_size("aa"), lax.axis_size("ba")
    devices = count_a * count_b
    if nx % devices == 0:
        return by_columns(state, labels)
    total = rows + 2 * REACH
    tall = up8(total)
    small = devices <= SMALL_GROUP
    peak, packed = call(
        peak_kernel,
        [(devices if small else 8, 128), (FIELDS + 1, rows, nx)],
        [],
        200_000,
        "peak",
    )(state, labels)
    ups = [(i, i + 1) for i in range(count_a - 1)]
    low = lax.ppermute(packed, "aa", ups)
    high = lax.ppermute(packed, "aa", [(j, i) for i, j in ups])
    if small:
        peaks = lax.all_to_all(peak, ("aa", "ba"), 0, 0, tiled=True)
    else:
        peaks = lax.pmax(peak, ("aa", "ba"))
    cells, change = call(
        x_kernel,
        [(FIELDS + 1, tall, nx), (8, tall, nx)],
        [(FIELDS + 1, up8(2 * total), nx)],
        4_000_000,
        "xflux",
    )(packed, low, high)
    exchange = count_b <= SMALL_AXIS
    faces = up8(rows + 1)
    after_y, step = call(
        y_kernel,
        [(count_b if exchange else 1, FIELDS + 1, rows, nx), (8, 128)],
        [(FIELDS + 1, max(tall, up8(2 * REACH - 1 + faces)), nx), (8, faces, nx)],
        4_000_000,
        "ysweep",
    )(peaks, cells, change)
    if exchange:
        lines = lax.all_to_all(after_y, "ba", 0, 0, tiled=True)
    else:
        near = []
        for shift in range(-REACH, REACH + 1):
            pairs = [(i, i - shift) for i in range(count_b) if 0 <= i - shift < count_b]
            near.append(lax.ppermute(after_y, "ba", pairs) if shift else after_y)
        lines = jnp.concatenate(near, axis=0)
    return call(
        functools.partial(z_kernel, not exchange),
        [(FIELDS, 1, rows, nx)],
        [(FIELDS + 1, (2 * REACH + 1) * rows, nx)],
        4_000_000,
        "zsweep",
    )(step, lines)


def solution(mesh):
    return jax.shard_map(
        shards,
        mesh=mesh,
        in_specs=(P(None, "ba", "aa", None), P("ba", "aa", None)),
        out_specs=P(None, "ba", "aa", None),
        check_vma=False,
    )
```

```python
import functools

import jax
import jax.numpy as jnp
from jax import lax
from jax.experimental import pallas as pl
from jax.experimental.pallas import tpu as pltpu
from jax.sharding import PartitionSpec as P

RETURN_ITERS = 2
REACH = 3
FIELDS = 14
DENSITY_FLOOR = 0.2
TRACTION_FLOOR = 0.1
COURANT = 0.4
WENO_EPSILON = 1e-06
TINY = 1e-36
SMALL_GROUP = 32
SMALL_AXIS = 8


def pick(label, sand, solid, void):
    return jnp.where(label == 0.0, sand, jnp.where(label == 1.0, solid, void))


def material(label):
    gamma = pick(label, 3.0, 4.0, 1.4)
    stiff = jnp.where(label == 1.0, 6.0, jnp.where(label == 0.0, 1.0, 0.0))
    shear = pick(label, 0.6, 3.0, 0.0)
    return gamma, stiff, shear


def deviator(grad):
    metric = {}
    for i in range(3):
        for j in range(i, 3):
            metric[i, j] = (
                grad[0][i] * grad[0][j] + grad[1][i] * grad[1][j] + grad[2][i] * grad[2][j]
            )
    third = (metric[0, 0] + metric[1, 1] + metric[2, 2]) * (1.0 / 3.0)
    for i in range(3):
        metric[i, i] = metric[i, i] - third
    return metric


def square_sum(dev):
    off = dev[0, 1] * dev[0, 1] + dev[0, 2] * dev[0, 2] + dev[1, 2] * dev[1, 2]
    diag = dev[0, 0] * dev[0, 0] + dev[1, 1] * dev[1, 1] + dev[2, 2] * dev[2, 2]
    return diag + (off + off)


def grad_of(fields):
    return [[fields[5 + 3 * row + col] for col in range(3)] for row in range(3)]


def pressure_of(fields, dev, mats):
    gamma, stiff, shear = mats
    density = jnp.maximum(fields[0], DENSITY_FLOOR)
    inverse = 1.0 / density
    velocity = [fields[1 + comp] * inverse for comp in range(3)]
    kinetic = 0.5 * (
        fields[1] * velocity[0] + fields[2] * velocity[1] + fields[3] * velocity[2]
    )
    energy = (0.25 * shear) * square_sum(dev)
    pressure = (gamma - 1.0) * (fields[4] - kinetic - energy) - gamma * stiff
    return density, inverse, velocity, pressure


def primitives(fields, mats):
    gamma, stiff, shear = mats
    dev = deviator(grad_of(fields))
    density, inverse, velocity, pressure = pressure_of(fields, dev, mats)
    square = (gamma * jnp.maximum(pressure + stiff, TRACTION_FLOOR) + (4.0 / 3.0) * shear) * inverse
    sound = square * lax.rsqrt(jnp.maximum(square, TINY))
    return density, velocity, dev, pressure, sound


def weno_pair(v):
    d = [v[i + 1] - v[i] for i in range(5)]
    b = [d[i + 1] - d[i] for i in range(4)]
    d1, d2, d3 = d[1] + d[1], d[2] + d[2], d[3] + d[3]
    bend = [4.0 * WENO_EPSILON + (13.0 / 3.0) * (x * x) for x in b]
    outer0, outer3 = (4.0 / 3.0) * b[0], (4.0 / 3.0) * b[3]
    inner1, inner2 = (2.0 / 3.0) * b[1], (2.0 / 3.0) * b[2]

    def shift(slopes, bends, steps):
        inv = [1.0 / (bends[i] + slopes[i] * slopes[i]) for i in range(3)]
        weight = [inv[0] * inv[0], 6.0 * (inv[1] * inv[1]), 3.0 * (inv[2] * inv[2])]
        total = weight[0] * steps[0] + weight[1] * steps[1] + weight[2] * steps[2]
        return 0.25 * (total / (weight[0] + weight[1] + weight[2]))

    left = v[2] + shift(
        (d1 + b[0], d1 + b[1], d2 - b[2]),
        (bend[0], bend[1], bend[2]),
        (d1 + outer0, d2 - inner1, d2 - inner2),
    )
    right = v[3] - shift(
        (d3 - b[3], d2 + b[2], d2 + b[1]),
        (bend[3], bend[2], bend[1]),
        (d3 - outer3, d2 + inner2, d2 + inner1),
    )
    return left, right


def riemann(lf, rf, left_label, right_label, d):
    left_mats, right_mats = material(left_label), material(right_label)
    l_rho, l_vel, l_dev, l_p, l_c = primitives(lf, left_mats)
    r_rho, r_vel, r_dev, r_p, r_c = primitives(rf, right_mats)

    def stress(dev, mats, i, j):
        return -mats[2] * dev[min(i, j), max(i, j)]

    l_s = [stress(l_dev, left_mats, k, d) for k in range(3)]
    r_s = [stress(r_dev, right_mats, k, d) for k in range(3)]
    l_u, r_u = l_vel[d], r_vel[d]
    slow = jnp.minimum(l_u - l_c, r_u - r_c)
    fast = jnp.maximum(l_u + l_c, r_u + r_c)
    l_t, r_t = l_p - l_s[d], r_p - r_s[d]
    l_gap, r_gap = slow - l_u, fast - r_u
    l_push, r_push = l_rho * l_gap, r_rho * r_gap
    contact = (r_t - l_t + l_push * l_u - r_push * r_u) / (l_push - r_push)
    width = fast - slow
    margin = 0.05 * width
    contact = jnp.minimum(jnp.maximum(contact, slow + margin), fast - margin)

    go_left = (slow >= 0.0) | (contact >= 0.0)
    plain = (slow >= 0.0) | (jnp.logical_not(contact >= 0.0) & jnp.logical_not(fast > 0.0))

    def side(a, b):
        return jnp.where(go_left, a, b)

    rho, gap, wave, trac = side(l_rho, r_rho), side(l_gap, r_gap), side(slow, fast), side(l_t, r_t)
    vel = [side(l_vel[k], r_vel[k]) for k in range(3)]
    mom = [side(lf[1 + k], rf[1 + k]) for k in range(3)]
    ener = side(lf[4], rf[4])
    u = vel[d]
    ratio = gap / (wave - contact)
    mass = rho * ratio
    star_e = ratio * (ener + (contact - u) * (rho * contact + trac / gap))
    result = [mom[d] + jnp.where(plain, 0.0, wave * (mass - rho))]
    for k in range(3):
        flux = mom[k] * u + trac if k == d else mom[k] * u
        star = mass * (contact if k == d else vel[k])
        result.append(flux + jnp.where(plain, 0.0, wave * (star - mom[k])))
    result.append((ener + trac) * u + jnp.where(plain, 0.0, wave * (star_e - ener)))
    for k in range(3):
        if k != d:
            result[1 + k] = result[1 + k] - 0.5 * (l_s[k] + r_s[k])
            result[4] = result[4] - 0.5 * (l_s[k] * l_vel[k] + r_s[k] * r_vel[k])
    inverse = 1.0 / width
    for row in range(3):
        base = 5 + 3 * row
        l_flow = lf[base] * l_vel[0] + lf[base + 1] * l_vel[1] + lf[base + 2] * l_vel[2]
        r_flow = rf[base] * r_vel[0] + rf[base + 1] * r_vel[1] + rf[base + 2] * r_vel[2]
        jump = rf[base + d] - lf[base + d]
        blend = (fast * l_flow - slow * r_flow + slow * fast * jump) * inverse
        result.append(jnp.where(slow >= 0.0, l_flow, jnp.where(fast <= 0.0, r_flow, blend)))
    return result


def changed_fields(d):
    return [0, 1, 2, 3, 4] + [5 + 3 * row + d for row in range(3)]


def face_values(window, fields):
    return [weno_pair([window(field, k) for k in range(6)]) for field in fields]


def face_fluxes(window, d, values=()):
    values = list(values) + face_values(window, range(len(values), FIELDS))
    left = [value[0] for value in values]
    right = [value[1] for value in values]
    return riemann(left, right, window(FIELDS, 2), window(FIELDS, 3), d)


def plastic(fields, label):
    mats = material(label)
    sandy = label == 0.0
    grad = grad_of(fields)
    dev = deviator(grad)
    third = (grad[0][0] + grad[1][1] + grad[2][2]) * (1.0 / 3.0)
    rest = [[grad[i][j] - third if i == j else grad[i][j] for j in range(3)] for i in range(3)]
    even = {(i, j): third * (rest[i][j] + rest[j][i]) for i, j in dev}
    pure = {key: dev[key] - even[key] for key in dev}
    pressure = pressure_of(fields, dev, mats)[3]
    radius = 0.025 + 0.2 * jnp.maximum(pressure, 0.0)
    product = None
    for turn in range(RETURN_ITERS):
        if turn:
            dev = {key: product * (product * pure[key] + even[key]) for key in dev}
        factor = 0.5 + jnp.minimum(radius * lax.rsqrt(0.36 * square_sum(dev)), 0.5)
        product = product * factor if turn else factor
    product = jnp.where(sandy, product, 1.0)
    less = product - 1.0
    return list(fields[:5]) + [
        grad[i][j] + less * rest[i][j] if i == j else product * grad[i][j]
        for i in range(3)
        for j in range(3)
    ]


def peak_kernel(state_ref, label_ref, peak_ref, packed_ref):
    rows = state_ref.shape[2]
    label = label_ref[0].astype(jnp.float32)
    fields = [state_ref[field, 0] for field in range(FIELDS)]
    for field in range(FIELDS):
        packed_ref[field] = fields[field]
    packed_ref[FIELDS] = label
    density, velocity, dev, pressure, sound = primitives(fields, material(label))
    speed = sound + jnp.maximum(
        jnp.maximum(jnp.abs(velocity[0]), jnp.abs(velocity[1])), jnp.abs(velocity[2])
    )
    best = speed[:, :128]
    for start in range(128, speed.shape[1], 128):
        best = jnp.maximum(best, speed[:, start : start + 128])
    best = jnp.max(best, axis=0, keepdims=True)
    peak_ref[...] = jnp.broadcast_to(best, peak_ref.shape)


def x_kernel(own_ref, low_ref, high_ref, out_ref, flux_ref, line_ref):
    rows, nx = own_ref.shape[1:]
    total = rows + 2 * REACH
    stack = line_ref.shape[1]
    pos, count = lax.axis_index("aa"), lax.axis_size("aa")
    first, last = pos == 0, pos == count - 1
    for field in range(FIELDS + 1):
        own = own_ref[field]
        low = jnp.where(first, own[:1], low_ref[field, rows - REACH :])
        high = jnp.where(last, own[rows - 1 :], high_ref[field, :REACH])
        out_ref[field, :REACH] = low
        out_ref[field, REACH : REACH + rows] = own
        out_ref[field, REACH + rows : total] = high
        out_ref[field, total:] = jnp.zeros((out_ref.shape[1] - total, nx), jnp.float32)
    lane = lax.broadcasted_iota(jnp.int32, (total, nx), 1)
    wide = lax.broadcasted_iota(jnp.int32, (stack, nx), 1)
    for field in range(FIELDS + 1):
        cells = out_ref[field, :total]
        line_ref[field, :total] = cells
        line_ref[field, total : 2 * total] = jnp.where(
            lane == nx - 1, cells, pltpu.roll(cells, nx - 1, 1)
        )
        if stack > 2 * total:
            line_ref[field, 2 * total :] = jnp.zeros((stack - 2 * total, nx), jnp.float32)
    cache = {}

    def window(field, k):
        if (field, k) not in cache:
            if k == 3:
                value = line_ref[field]
            elif k < 3:
                near = window(field, k + 1)
                value = jnp.where(wide == 0, near, pltpu.roll(near, 1, 1))
            else:
                near = window(field, k - 1)
                value = jnp.where(wide == nx - 1, near, pltpu.roll(near, nx - 1, 1))
            cache[field, k] = value
        return cache[field, k]

    for slot, flux in enumerate(face_fluxes(window, 0)):
        line_ref[slot] = flux
    for slot in range(8):
        lower = line_ref[slot, :total]
        upper = line_ref[slot, total : 2 * total]
        flux_ref[slot, :total] = (
            jnp.where(lane == nx - 1, upper, pltpu.roll(lower, nx - 1, 1)) - lower
        )
        flux_ref[slot, total:] = jnp.zeros((flux_ref.shape[1] - total, nx), jnp.float32)


def step_of(peak_ref):
    best = jnp.max(peak_ref[...], axis=0, keepdims=True)
    return COURANT / jnp.max(best, axis=1, keepdims=True)


def y_kernel(peak_ref, cells_ref, change_ref, out_ref, step_ref, line_ref, face_ref):
    copies, _, rows, nx = out_ref.shape
    step = step_of(peak_ref)
    step_ref[...] = jnp.broadcast_to(step, step_ref.shape)
    label = cells_ref[FIELDS]
    fields = [cells_ref[field] for field in range(FIELDS)]
    for slot, field in enumerate(changed_fields(0)):
        fields[field] = fields[field] - step * change_ref[slot]
    fields = plastic(fields, label)
    height = label.shape[0]
    for field in range(FIELDS):
        line_ref[field, :height] = fields[field]
    line_ref[FIELDS, :height] = label
    faces = face_ref.shape[1]
    for field in range(FIELDS + 1):
        if line_ref.shape[1] > height:
            line_ref[field, height:] = jnp.zeros((line_ref.shape[1] - height, nx), jnp.float32)
    fluxes = face_fluxes(lambda field, k: line_ref[field, k : k + faces], 1)
    for slot in range(8):
        face_ref[slot] = fluxes[slot]
    label = line_ref[FIELDS, REACH : REACH + rows]
    fields = [line_ref[field, REACH : REACH + rows] for field in range(FIELDS)]
    for slot, field in enumerate(changed_fields(1)):
        change = face_ref[slot, 1 : rows + 1] - face_ref[slot, :rows]
        fields[field] = fields[field] - step * change
    fields = plastic(fields, label) + [label]
    for copy in range(copies):
        for field in range(FIELDS + 1):
            out_ref[copy, field] = fields[field]


def z_kernel(centred, step_ref, lines_ref, out_ref, line_ref):
    rows = out_ref.shape[2]
    pos, count = lax.axis_index("ba"), lax.axis_size("ba")
    step = step_ref[:rows, :1]
    for k in range(2 * REACH + 1):
        where = jnp.clip(pos + k - REACH, 0, count - 1)
        if centred:
            where = where - pos + REACH
        for field in range(FIELDS + 1):
            line_ref[field, k * rows : (k + 1) * rows] = lines_ref[where, field]
    fluxes = face_fluxes(
        lambda field, k: line_ref[field, k * rows : (k + 2) * rows], 2
    )
    centre = slice(REACH * rows, (REACH + 1) * rows)
    label = line_ref[FIELDS, centre]
    fields = [line_ref[field, centre] for field in range(FIELDS)]
    for slot, field in enumerate(changed_fields(2)):
        fields[field] = fields[field] - step * (fluxes[slot][rows:] - fluxes[slot][:rows])
    fields = plastic(fields, label)
    for field in range(FIELDS):
        out_ref[field, 0] = fields[field]


CHANGED = 8
KEPT = 5


def columns_kernel(
    state_ref, label_ref, out_ref, line_ref, stage_ref
):
    _, _, rows, nx = state_ref.shape
    label = label_ref[0]
    fields = [state_ref[field, 0] for field in range(FIELDS)]
    for field, cells in enumerate(fields + [label]):
        stage_ref[field * rows : (field + 1) * rows] = cells
        line_ref[field, :rows] = cells
        line_ref[field, rows:] = cells
    density, velocity, dev, pressure, sound = primitives(fields, material(label))
    speed = sound + jnp.maximum(
        jnp.maximum(jnp.abs(velocity[0]), jnp.abs(velocity[1])), jnp.abs(velocity[2])
    )
    used = (FIELDS + 1 + CHANGED) * rows
    stage_ref[used:] = jnp.broadcast_to(
        jnp.max(speed, keepdims=True), (stage_ref.shape[0] - used, nx)
    )
    window, change = line_window(line_ref, nx, 1)
    for slot, flux in enumerate(face_fluxes(window, 0)):
        start = (FIELDS + 1 + slot) * rows
        stage_ref[start : start + rows] = change(flux)
    tall = stage_ref.shape[0]
    out_ref[:, :tall] = stage_ref[...].T


def line_window(line_ref, group, width):
    rows, nx = line_ref.shape[1] // 2, line_ref.shape[2]
    shape = line_ref.shape[1:]
    lane = lax.broadcasted_iota(jnp.int32, shape, 1)
    upper = lax.broadcasted_iota(jnp.int32, shape, 0) >= rows

    def within(low, high):
        hit = lane < 0
        for start in range(0, nx, group):
            hit = hit | ((lane >= start + low) & (lane < start + high))
        return hit

    first = {n: within(0, n * width) & jnp.logical_not(upper) for n in range(1, 4)}
    last = {n: within(group - n * width, group) | upper for n in range(1, 3)}
    cache = {}

    def moved(field, cells):
        if (field, "moved", cells) not in cache:
            shift = cells * width if cells > 0 else nx + cells * width
            cache[field, "moved", cells] = pltpu.roll(line_ref[field], shift, 1)
        return cache[field, "moved", cells]

    def window(field, k):
        if (field, k) not in cache:
            away = k - REACH
            if away == 0:
                value = jnp.where(upper, moved(field, 1), line_ref[field])
            elif away == -1:
                value = jnp.where(first[1], line_ref[field], moved(field, 1))
            elif away < 0:
                value = jnp.where(first[-away], window(field, k + 1), moved(field, -away))
            else:
                value = jnp.where(last[away], window(field, k - 1), moved(field, -away))
            cache[field, k] = value
        return cache[field, k]

    start = within(0, width)[:rows]

    def change(flux):
        faces = jnp.where(start, flux[rows:], flux[:rows])
        return pltpu.roll(faces, nx - width, 1) - flux[:rows]

    return window, change


def sweeps_kernel(rows, count_a, count_b, in_ref, out_ref, stage_ref, line_ref, face_ref, deep_ref):
    nx = in_ref.shape[0]
    group = nx // count_a
    width = group // count_b
    tall = stage_ref.shape[0]
    stage_ref[...] = in_ref[:, :tall].T
    used = (FIELDS + 1 + CHANGED) * rows
    step = COURANT / jnp.max(in_ref[:, used : used + 1], axis=0, keepdims=True)

    def block(index):
        return stage_ref[index * rows : (index + 1) * rows, :]

    label = block(FIELDS)
    fields = [block(field) for field in range(FIELDS)]
    for slot, field in enumerate(changed_fields(0)):
        fields[field] = fields[field] - step * block(FIELDS + 1 + slot)

    lane = lax.broadcasted_iota(jnp.int32, (REACH, nx), 1)
    faces = face_ref.shape[1]

    def lay(field, cells):
        low = pltpu.roll(cells, group, 1)[rows - REACH :]
        high = pltpu.roll(cells, nx - group, 1)[:REACH]
        line_ref[field, :REACH] = jnp.where(lane < group, cells[:1], low)
        line_ref[field, REACH : REACH + rows] = cells
        line_ref[field, REACH + rows : 2 * REACH + rows] = jnp.where(
            lane >= nx - group, cells[rows - 1 :], high
        )
        rest = line_ref.shape[1] - 2 * REACH - rows
        line_ref[field, 2 * REACH + rows :] = jnp.zeros((rest, nx), jnp.float32)

    def window(field, k):
        return line_ref[field, k : k + faces]

    lay(FIELDS, label)
    for field in range(KEPT):
        lay(field, fields[field])
    values = face_values(window, range(KEPT))
    fields = plastic(fields, label)
    for field in range(KEPT, FIELDS):
        lay(field, fields[field])
    fluxes = face_fluxes(window, 1, values)
    for slot in range(CHANGED):
        face_ref[slot] = fluxes[slot]
    for slot, field in enumerate(changed_fields(1)):
        change = face_ref[slot, 1 : rows + 1] - face_ref[slot, :rows]
        fields[field] = fields[field] - step * change

    def stack(field, cells):
        deep_ref[field, :rows] = cells
        deep_ref[field, rows:] = cells

    window, change = line_window(deep_ref, group, width)
    stack(FIELDS, label)
    for field in range(KEPT):
        stack(field, fields[field])
    values = face_values(window, range(KEPT))
    fields = plastic(fields, label)
    for field in range(KEPT, FIELDS):
        stack(field, fields[field])
    fluxes = face_fluxes(window, 2, values)
    for slot, field in enumerate(changed_fields(2)):
        fields[field] = fields[field] - step * change(fluxes[slot])
    fields = plastic(fields, label)
    for field in range(FIELDS):
        stage_ref[field * rows : (field + 1) * rows, :] = fields[field]
    tall = up8(FIELDS * rows)
    out_ref[:, :tall] = stage_ref[:tall].T


def home_kernel(in_ref, out_ref):
    _, _, rows, _ = out_ref.shape
    back = in_ref[:, : up8(FIELDS * rows)].T
    for field in range(FIELDS):
        out_ref[field, 0] = back[field * rows : (field + 1) * rows]


def up8(size):
    return -(-size // 8) * 8


def call(kernel, outs, scratch, cost, name, space=pltpu.VMEM, fuse=None):
    vmem = pl.BlockSpec(memory_space=pltpu.VMEM)
    given = pl.BlockSpec(memory_space=space)
    shapes = [jax.ShapeDtypeStruct(shape, jnp.float32) for shape in outs]

    def run(*args):
        return pl.pallas_call(
            kernel,
            out_shape=shapes if len(shapes) > 1 else shapes[0],
            in_specs=[given] * len(args),
            out_specs=[vmem] * len(shapes) if len(shapes) > 1 else vmem,
            scratch_shapes=[
                pltpu.VMEM(shape, jnp.float32) if isinstance(shape, tuple) else shape
                for shape in scratch
            ],
            cost_estimate=pl.CostEstimate(flops=cost, bytes_accessed=cost // 4, transcendentals=0),
            name=name,
            compiler_params=pltpu.CompilerParams(vmem_limit_bytes=16 * 1024 * 1024, allow_input_fusion=fuse),
        )(*args)

    return run


def by_columns(state, labels):
    _, _, rows, nx = state.shape
    count_a, count_b = lax.axis_size("aa"), lax.axis_size("ba")
    devices = count_a * count_b
    used = (FIELDS + 1 + CHANGED) * rows + 1
    padded = -(-used // 128) * 128

    def swap(array):
        parts = array.reshape(devices, nx // devices, padded)
        return lax.all_to_all(parts, ("aa", "ba"), 0, 0, tiled=True).reshape(nx, padded)

    columns = call(
        columns_kernel,
        [(nx, padded)],
        [
            (FIELDS + 1, 2 * rows, nx),
            (up8(used), nx),
        ],
        4_000_000,
        "columns",
        fuse=[False, True],
    )(state, labels.astype(jnp.float32))
    faces = up8(rows + 1)
    swept = call(
        functools.partial(sweeps_kernel, rows, count_a, count_b),
        [(nx, padded)],
        [
            (up8(used), nx),
            (FIELDS + 1, up8(2 * REACH - 1 + faces), nx),
            (CHANGED, faces, nx),
            (FIELDS + 1, 2 * rows, nx),
        ],
        8_000_000,
        "sweeps",
    )(swap(columns))
    return call(home_kernel, [state.shape], [], 100_000, "home")(swap(swept))


def shards(state, labels):
    _, depth, rows, nx = state.shape
    assert depth == 1 and rows >= REACH and nx % 128 == 0
    count_a, count_b = lax.axis_size("aa"), lax.axis_size("ba")
    devices = count_a * count_b
    if nx % devices == 0:
        return by_columns(state, labels)
    total = rows + 2 * REACH
    tall = up8(total)
    small = devices <= SMALL_GROUP
    peak, packed = call(
        peak_kernel,
        [(devices if small else 8, 128), (FIELDS + 1, rows, nx)],
        [],
        200_000,
        "peak",
    )(state, labels)
    ups = [(i, i + 1) for i in range(count_a - 1)]
    low = lax.ppermute(packed, "aa", ups)
    high = lax.ppermute(packed, "aa", [(j, i) for i, j in ups])
    if small:
        peaks = lax.all_to_all(peak, ("aa", "ba"), 0, 0, tiled=True)
    else:
        peaks = lax.pmax(peak, ("aa", "ba"))
    cells, change = call(
        x_kernel,
        [(FIELDS + 1, tall, nx), (8, tall, nx)],
        [(FIELDS + 1, up8(2 * total), nx)],
        4_000_000,
        "xflux",
    )(packed, low, high)
    exchange = count_b <= SMALL_AXIS
    faces = up8(rows + 1)
    after_y, step = call(
        y_kernel,
        [(count_b if exchange else 1, FIELDS + 1, rows, nx), (8, 128)],
        [(FIELDS + 1, max(tall, up8(2 * REACH - 1 + faces)), nx), (8, faces, nx)],
        4_000_000,
        "ysweep",
    )(peaks, cells, change)
    if exchange:
        lines = lax.all_to_all(after_y, "ba", 0, 0, tiled=True)
    else:
        near = []
        for shift in range(-REACH, REACH + 1):
            pairs = [(i, i - shift) for i in range(count_b) if 0 <= i - shift < count_b]
            near.append(lax.ppermute(after_y, "ba", pairs) if shift else after_y)
        lines = jnp.concatenate(near, axis=0)
    return call(
        functools.partial(z_kernel, not exchange),
        [(FIELDS, 1, rows, nx)],
        [(FIELDS + 1, (2 * REACH + 1) * rows, nx)],
        4_000_000,
        "zsweep",
    )(step, lines)


def solution(mesh):
    return jax.shard_map(
        shards,
        mesh=mesh,
        in_specs=(P(None, "ba", "aa", None), P("ba", "aa", None)),
        out_specs=P(None, "ba", "aa", None),
        check_vma=False,
    )
```

```python
import functools

import jax
import jax.numpy as jnp
from jax import lax
from jax.experimental import pallas as pl
from jax.experimental.pallas import tpu as pltpu
from jax.sharding import PartitionSpec as P

RETURN_ITERS = 2
REACH = 3
FIELDS = 14
DENSITY_FLOOR = 0.2
TRACTION_FLOOR = 0.1
COURANT = 0.4
WENO_EPSILON = 1e-06
TINY = 1e-36
SMALL_GROUP = 32
SMALL_AXIS = 8


def pick(label, sand, solid, void):
    return jnp.where(label == 0.0, sand, jnp.where(label == 1.0, solid, void))


def material(label):
    gamma = pick(label, 3.0, 4.0, 1.4)
    stiff = jnp.where(label == 1.0, 6.0, jnp.where(label == 0.0, 1.0, 0.0))
    shear = pick(label, 0.6, 3.0, 0.0)
    return gamma, stiff, shear


def deviator(grad):
    metric = {}
    for i in range(3):
        for j in range(i, 3):
            metric[i, j] = (
                grad[0][i] * grad[0][j] + grad[1][i] * grad[1][j] + grad[2][i] * grad[2][j]
            )
    third = (metric[0, 0] + metric[1, 1] + metric[2, 2]) * (1.0 / 3.0)
    for i in range(3):
        metric[i, i] = metric[i, i] - third
    return metric


def square_sum(dev):
    off = dev[0, 1] * dev[0, 1] + dev[0, 2] * dev[0, 2] + dev[1, 2] * dev[1, 2]
    diag = dev[0, 0] * dev[0, 0] + dev[1, 1] * dev[1, 1] + dev[2, 2] * dev[2, 2]
    return diag + (off + off)


def grad_of(fields):
    return [[fields[5 + 3 * row + col] for col in range(3)] for row in range(3)]


def pressure_of(fields, dev, mats):
    gamma, stiff, shear = mats
    density = jnp.maximum(fields[0], DENSITY_FLOOR)
    inverse = 1.0 / density
    velocity = [fields[1 + comp] * inverse for comp in range(3)]
    kinetic = 0.5 * (
        fields[1] * velocity[0] + fields[2] * velocity[1] + fields[3] * velocity[2]
    )
    energy = (0.25 * shear) * square_sum(dev)
    pressure = (gamma - 1.0) * (fields[4] - kinetic - energy) - gamma * stiff
    return density, inverse, velocity, pressure


def primitives(fields, mats):
    gamma, stiff, shear = mats
    dev = deviator(grad_of(fields))
    density, inverse, velocity, pressure = pressure_of(fields, dev, mats)
    square = (gamma * jnp.maximum(pressure + stiff, TRACTION_FLOOR) + (4.0 / 3.0) * shear) * inverse
    sound = square * lax.rsqrt(jnp.maximum(square, TINY))
    return density, velocity, dev, pressure, sound


def weno_pair(v):
    d = [v[i + 1] - v[i] for i in range(5)]
    b = [d[i + 1] - d[i] for i in range(4)]
    d1, d2, d3 = d[1] + d[1], d[2] + d[2], d[3] + d[3]
    bend = [4.0 * WENO_EPSILON + (13.0 / 3.0) * (x * x) for x in b]
    outer0, outer3 = (4.0 / 3.0) * b[0], (4.0 / 3.0) * b[3]
    inner1, inner2 = (2.0 / 3.0) * b[1], (2.0 / 3.0) * b[2]

    def shift(slopes, bends, steps):
        inv = [1.0 / (bends[i] + slopes[i] * slopes[i]) for i in range(3)]
        weight = [inv[0] * inv[0], 6.0 * (inv[1] * inv[1]), 3.0 * (inv[2] * inv[2])]
        total = weight[0] * steps[0] + weight[1] * steps[1] + weight[2] * steps[2]
        return 0.25 * (total / (weight[0] + weight[1] + weight[2]))

    left = v[2] + shift(
        (d1 + b[0], d1 + b[1], d2 - b[2]),
        (bend[0], bend[1], bend[2]),
        (d1 + outer0, d2 - inner1, d2 - inner2),
    )
    right = v[3] - shift(
        (d3 - b[3], d2 + b[2], d2 + b[1]),
        (bend[3], bend[2], bend[1]),
        (d3 - outer3, d2 + inner2, d2 + inner1),
    )
    return left, right


def riemann(lf, rf, left_label, right_label, d):
    left_mats, right_mats = material(left_label), material(right_label)
    l_rho, l_vel, l_dev, l_p, l_c = primitives(lf, left_mats)
    r_rho, r_vel, r_dev, r_p, r_c = primitives(rf, right_mats)

    def stress(dev, mats, i, j):
        return -mats[2] * dev[min(i, j), max(i, j)]

    l_s = [stress(l_dev, left_mats, k, d) for k in range(3)]
    r_s = [stress(r_dev, right_mats, k, d) for k in range(3)]
    l_u, r_u = l_vel[d], r_vel[d]
    slow = jnp.minimum(l_u - l_c, r_u - r_c)
    fast = jnp.maximum(l_u + l_c, r_u + r_c)
    l_t, r_t = l_p - l_s[d], r_p - r_s[d]
    l_gap, r_gap = slow - l_u, fast - r_u
    l_push, r_push = l_rho * l_gap, r_rho * r_gap
    contact = (r_t - l_t + l_push * l_u - r_push * r_u) / (l_push - r_push)
    width = fast - slow
    margin = 0.05 * width
    contact = jnp.minimum(jnp.maximum(contact, slow + margin), fast - margin)

    go_left = (slow >= 0.0) | (contact >= 0.0)
    plain = (slow >= 0.0) | (jnp.logical_not(contact >= 0.0) & jnp.logical_not(fast > 0.0))

    def side(a, b):
        return jnp.where(go_left, a, b)

    rho, gap, wave, trac = side(l_rho, r_rho), side(l_gap, r_gap), side(slow, fast), side(l_t, r_t)
    vel = [side(l_vel[k], r_vel[k]) for k in range(3)]
    mom = [side(lf[1 + k], rf[1 + k]) for k in range(3)]
    ener = side(lf[4], rf[4])
    u = vel[d]
    ratio = gap / (wave - contact)
    mass = rho * ratio
    star_e = ratio * (ener + (contact - u) * (rho * contact + trac / gap))
    result = [mom[d] + jnp.where(plain, 0.0, wave * (mass - rho))]
    for k in range(3):
        flux = mom[k] * u + trac if k == d else mom[k] * u
        star = mass * (contact if k == d else vel[k])
        result.append(flux + jnp.where(plain, 0.0, wave * (star - mom[k])))
    result.append((ener + trac) * u + jnp.where(plain, 0.0, wave * (star_e - ener)))
    for k in range(3):
        if k != d:
            result[1 + k] = result[1 + k] - 0.5 * (l_s[k] + r_s[k])
            result[4] = result[4] - 0.5 * (l_s[k] * l_vel[k] + r_s[k] * r_vel[k])
    inverse = 1.0 / width
    for row in range(3):
        base = 5 + 3 * row
        l_flow = lf[base] * l_vel[0] + lf[base + 1] * l_vel[1] + lf[base + 2] * l_vel[2]
        r_flow = rf[base] * r_vel[0] + rf[base + 1] * r_vel[1] + rf[base + 2] * r_vel[2]
        jump = rf[base + d] - lf[base + d]
        blend = (fast * l_flow - slow * r_flow + slow * fast * jump) * inverse
        result.append(jnp.where(slow >= 0.0, l_flow, jnp.where(fast <= 0.0, r_flow, blend)))
    return result


def changed_fields(d):
    return [0, 1, 2, 3, 4] + [5 + 3 * row + d for row in range(3)]


def face_values(window, fields):
    return [weno_pair([window(field, k) for k in range(6)]) for field in fields]


def face_fluxes(window, d, values=()):
    values = list(values) + face_values(window, range(len(values), FIELDS))
    left = [value[0] for value in values]
    right = [value[1] for value in values]
    return riemann(left, right, window(FIELDS, 2), window(FIELDS, 3), d)


def plastic(fields, label):
    mats = material(label)
    sandy = label == 0.0
    grad = grad_of(fields)
    dev = deviator(grad)
    third = (grad[0][0] + grad[1][1] + grad[2][2]) * (1.0 / 3.0)
    rest = [[grad[i][j] - third if i == j else grad[i][j] for j in range(3)] for i in range(3)]
    even = {(i, j): third * (rest[i][j] + rest[j][i]) for i, j in dev}
    pure = {key: dev[key] - even[key] for key in dev}
    pressure = pressure_of(fields, dev, mats)[3]
    radius = 0.025 + 0.2 * jnp.maximum(pressure, 0.0)
    product = None
    for turn in range(RETURN_ITERS):
        if turn:
            dev = {key: product * (product * pure[key] + even[key]) for key in dev}
        factor = 0.5 + jnp.minimum(radius * lax.rsqrt(0.36 * square_sum(dev)), 0.5)
        product = product * factor if turn else factor
    product = jnp.where(sandy, product, 1.0)
    less = product - 1.0
    return list(fields[:5]) + [
        grad[i][j] + less * rest[i][j] if i == j else product * grad[i][j]
        for i in range(3)
        for j in range(3)
    ]


def peak_kernel(state_ref, label_ref, peak_ref, packed_ref):
    rows = state_ref.shape[2]
    label = label_ref[0].astype(jnp.float32)
    fields = [state_ref[field, 0] for field in range(FIELDS)]
    for field in range(FIELDS):
        packed_ref[field] = fields[field]
    packed_ref[FIELDS] = label
    density, velocity, dev, pressure, sound = primitives(fields, material(label))
    speed = sound + jnp.maximum(
        jnp.maximum(jnp.abs(velocity[0]), jnp.abs(velocity[1])), jnp.abs(velocity[2])
    )
    best = speed[:, :128]
    for start in range(128, speed.shape[1], 128):
        best = jnp.maximum(best, speed[:, start : start + 128])
    best = jnp.max(best, axis=0, keepdims=True)
    peak_ref[...] = jnp.broadcast_to(best, peak_ref.shape)


def x_kernel(own_ref, low_ref, high_ref, out_ref, flux_ref, line_ref):
    rows, nx = own_ref.shape[1:]
    total = rows + 2 * REACH
    stack = line_ref.shape[1]
    pos, count = lax.axis_index("aa"), lax.axis_size("aa")
    first, last = pos == 0, pos == count - 1
    for field in range(FIELDS + 1):
        own = own_ref[field]
        low = jnp.where(first, own[:1], low_ref[field, rows - REACH :])
        high = jnp.where(last, own[rows - 1 :], high_ref[field, :REACH])
        out_ref[field, :REACH] = low
        out_ref[field, REACH : REACH + rows] = own
        out_ref[field, REACH + rows : total] = high
        out_ref[field, total:] = jnp.zeros((out_ref.shape[1] - total, nx), jnp.float32)
    lane = lax.broadcasted_iota(jnp.int32, (total, nx), 1)
    wide = lax.broadcasted_iota(jnp.int32, (stack, nx), 1)
    for field in range(FIELDS + 1):
        cells = out_ref[field, :total]
        line_ref[field, :total] = cells
        line_ref[field, total : 2 * total] = jnp.where(
            lane == nx - 1, cells, pltpu.roll(cells, nx - 1, 1)
        )
        if stack > 2 * total:
            line_ref[field, 2 * total :] = jnp.zeros((stack - 2 * total, nx), jnp.float32)
    cache = {}

    def window(field, k):
        if (field, k) not in cache:
            if k == 3:
                value = line_ref[field]
            elif k < 3:
                near = window(field, k + 1)
                value = jnp.where(wide == 0, near, pltpu.roll(near, 1, 1))
            else:
                near = window(field, k - 1)
                value = jnp.where(wide == nx - 1, near, pltpu.roll(near, nx - 1, 1))
            cache[field, k] = value
        return cache[field, k]

    for slot, flux in enumerate(face_fluxes(window, 0)):
        line_ref[slot] = flux
    for slot in range(8):
        lower = line_ref[slot, :total]
        upper = line_ref[slot, total : 2 * total]
        flux_ref[slot, :total] = (
            jnp.where(lane == nx - 1, upper, pltpu.roll(lower, nx - 1, 1)) - lower
        )
        flux_ref[slot, total:] = jnp.zeros((flux_ref.shape[1] - total, nx), jnp.float32)


def step_of(peak_ref):
    best = jnp.max(peak_ref[...], axis=0, keepdims=True)
    return COURANT / jnp.max(best, axis=1, keepdims=True)


def y_kernel(peak_ref, cells_ref, change_ref, out_ref, step_ref, line_ref, face_ref):
    copies, _, rows, nx = out_ref.shape
    step = step_of(peak_ref)
    step_ref[...] = jnp.broadcast_to(step, step_ref.shape)
    label = cells_ref[FIELDS]
    fields = [cells_ref[field] for field in range(FIELDS)]
    for slot, field in enumerate(changed_fields(0)):
        fields[field] = fields[field] - step * change_ref[slot]
    fields = plastic(fields, label)
    height = label.shape[0]
    for field in range(FIELDS):
        line_ref[field, :height] = fields[field]
    line_ref[FIELDS, :height] = label
    faces = face_ref.shape[1]
    for field in range(FIELDS + 1):
        if line_ref.shape[1] > height:
            line_ref[field, height:] = jnp.zeros((line_ref.shape[1] - height, nx), jnp.float32)
    fluxes = face_fluxes(lambda field, k: line_ref[field, k : k + faces], 1)
    for slot in range(8):
        face_ref[slot] = fluxes[slot]
    label = line_ref[FIELDS, REACH : REACH + rows]
    fields = [line_ref[field, REACH : REACH + rows] for field in range(FIELDS)]
    for slot, field in enumerate(changed_fields(1)):
        change = face_ref[slot, 1 : rows + 1] - face_ref[slot, :rows]
        fields[field] = fields[field] - step * change
    fields = plastic(fields, label) + [label]
    for copy in range(copies):
        for field in range(FIELDS + 1):
            out_ref[copy, field] = fields[field]


def z_kernel(centred, step_ref, lines_ref, out_ref, line_ref):
    rows = out_ref.shape[2]
    pos, count = lax.axis_index("ba"), lax.axis_size("ba")
    step = step_ref[:rows, :1]
    for k in range(2 * REACH + 1):
        where = jnp.clip(pos + k - REACH, 0, count - 1)
        if centred:
            where = where - pos + REACH
        for field in range(FIELDS + 1):
            line_ref[field, k * rows : (k + 1) * rows] = lines_ref[where, field]
    fluxes = face_fluxes(
        lambda field, k: line_ref[field, k * rows : (k + 2) * rows], 2
    )
    centre = slice(REACH * rows, (REACH + 1) * rows)
    label = line_ref[FIELDS, centre]
    fields = [line_ref[field, centre] for field in range(FIELDS)]
    for slot, field in enumerate(changed_fields(2)):
        fields[field] = fields[field] - step * (fluxes[slot][rows:] - fluxes[slot][:rows])
    fields = plastic(fields, label)
    for field in range(FIELDS):
        out_ref[field, 0] = fields[field]


CHANGED = 8


def columns_kernel(
    state_ref, label_ref, out_ref, both_ref, stage_ref
):
    _, _, rows, nx = state_ref.shape
    label = label_ref[0]
    fields = [state_ref[field, 0] for field in range(FIELDS)]
    for field, cells in enumerate(fields + [label]):
        stage_ref[field * rows : (field + 1) * rows] = cells
    density, velocity, dev, pressure, sound = primitives(fields, material(label))
    speed = sound + jnp.maximum(
        jnp.maximum(jnp.abs(velocity[0]), jnp.abs(velocity[1])), jnp.abs(velocity[2])
    )
    used = (FIELDS + 1 + CHANGED) * rows
    stage_ref[used:] = jnp.broadcast_to(
        jnp.max(speed, keepdims=True), (stage_ref.shape[0] - used, nx)
    )
    pairs = [stage_ref[field * rows : (field + 2) * rows] for field in range(0, FIELDS, 2)]
    for slot, change in enumerate(line_changes(pairs, both_ref, label, nx, 1, 0)):
        start = (FIELDS + 1 + slot) * rows
        stage_ref[start : start + rows] = change
    tall = stage_ref.shape[0]
    out_ref[:, :tall] = stage_ref[...].T


def line_changes(pairs, both_ref, label, group, width, d):
    tall, nx = pairs[0].shape
    rows = tall // 2
    lane = lax.broadcasted_iota(jnp.int32, (tall, nx), 1)

    def within(low, high):
        hit = lane < 0
        for start in range(0, nx, group):
            hit = hit | ((lane >= start + low * width) & (lane < start + high * width))
        return hit

    cells = group // width
    first = {n: within(0, n) for n in (1, 2, 3)}
    last = {n: within(cells - n, cells) for n in (1, 2)}
    ends = None
    for p, own in enumerate(pairs):
        moved = {n: pltpu.roll(own, n * width, 1) for n in {1, 2, 3, p + 1, p + 2, p + 3}}
        ahead = [pltpu.roll(own, nx - n * width, 1) for n in (1, 2)]
        low1 = jnp.where(first[1], own, moved[1])
        low2 = jnp.where(first[2], low1, moved[2])
        low3 = jnp.where(first[3], low2, moved[3])
        high1 = jnp.where(last[1], own, ahead[0])
        high2 = jnp.where(last[2], high1, ahead[1])
        values = weno_pair([low3, low2, low1, own, high1, high2])
        for side in range(2):
            both_ref[side, 2 * p, :rows] = values[side][:rows]
            both_ref[side, 2 * p + 1, :rows] = values[side][rows:]
        mine = [moved[p + 1 + n] for n in range(3)]
        if ends is None:
            ends = mine
        else:
            slot = within(p, p + 1)
            ends = [jnp.where(slot, new, old) for new, old in zip(mine, ends)]
    values = weno_pair([ends[2], ends[1], ends[0], ends[0], ends[0], ends[0]])
    for p in range(len(pairs)):
        for side in range(2):
            value = values[side]
            value = pltpu.roll(value, nx - p * width, 1) if p else value
            both_ref[side, 2 * p, rows:] = value[:rows]
            both_ref[side, 2 * p + 1, rows:] = value[rows:]
    left = [both_ref[0, field] for field in range(FIELDS)]
    right = [both_ref[1, field] for field in range(FIELDS)]
    kinds = jnp.concatenate([label, label], axis=0)
    before = pltpu.roll(kinds, width, 1)
    upper = lax.broadcasted_iota(jnp.int32, (tall, nx), 0) >= rows
    left_kinds = jnp.where(first[1] & jnp.logical_not(upper), kinds, before)
    fluxes = riemann(left, right, left_kinds, jnp.where(upper, before, kinds), d)
    start = first[1][:rows]
    changes = []
    for flux in fluxes:
        faces = jnp.where(start, flux[rows:], flux[:rows])
        changes.append(pltpu.roll(faces, nx - width, 1) - flux[:rows])
    return changes


def sweeps_kernel(rows, count_a, count_b, in_ref, out_ref, stage_ref, line_ref, face_ref, deep_ref, pack_ref, both_ref, pair_ref):
    nx = in_ref.shape[0]
    group = nx // count_a
    width = group // count_b
    tall = stage_ref.shape[0]
    stage_ref[...] = in_ref[:, :tall].T
    used = (FIELDS + 1 + CHANGED) * rows
    step = COURANT / jnp.max(in_ref[:, used : used + 1], axis=0, keepdims=True)

    def block(index):
        return stage_ref[index * rows : (index + 1) * rows, :]

    label = block(FIELDS)
    fields = [block(field) for field in range(FIELDS)]
    for slot, field in enumerate(changed_fields(0)):
        fields[field] = fields[field] - step * block(FIELDS + 1 + slot)

    lane = lax.broadcasted_iota(jnp.int32, (REACH, nx), 1)
    faces = rows + 1

    def lay(field, cells):
        low = pltpu.roll(cells, group, 1)[rows - REACH :]
        high = pltpu.roll(cells, nx - group, 1)[:REACH]
        line_ref[field, :REACH] = jnp.where(lane < group, cells[:1], low)
        line_ref[field, REACH : REACH + rows] = cells
        line_ref[field, REACH + rows : 2 * REACH + rows] = jnp.where(
            lane >= nx - group, cells[rows - 1 :], high
        )

    def window(field, k):
        return line_ref[field, k : k + faces]

    def pack(field):
        for k in range(6):
            pack_ref[k, field * faces : (field + 1) * faces] = window(field, k)

    lay(FIELDS, label)
    fields = plastic(fields, label)
    for field in range(FIELDS):
        lay(field, fields[field])
        pack(field)
    used = FIELDS * faces
    left, right = weno_pair([pack_ref[k, :used] for k in range(6)])
    both_ref[0, :used] = left
    both_ref[1, :used] = right
    values = [
        [both_ref[side, field * faces : (field + 1) * faces] for side in range(2)]
        for field in range(FIELDS)
    ]
    fluxes = face_fluxes(window, 1, values)
    for slot in range(CHANGED):
        face_ref[slot, :faces] = fluxes[slot]
    for slot, field in enumerate(changed_fields(1)):
        change = face_ref[slot, 1 : rows + 1] - face_ref[slot, :rows]
        fields[field] = fields[field] - step * change

    fields = plastic(fields, label)
    for field in range(FIELDS):
        pair_ref[field // 2, (field % 2) * rows : (field % 2 + 1) * rows] = fields[field]
    pairs = [pair_ref[p] for p in range(FIELDS // 2)]
    changes = line_changes(pairs, deep_ref, label, group, width, 2)
    for slot, field in enumerate(changed_fields(2)):
        fields[field] = fields[field] - step * changes[slot]
    fields = plastic(fields, label)
    for field in range(FIELDS):
        stage_ref[field * rows : (field + 1) * rows, :] = fields[field]
    tall = up8(FIELDS * rows)
    out_ref[:, :tall] = stage_ref[:tall].T


def home_kernel(in_ref, out_ref):
    _, _, rows, _ = out_ref.shape
    back = in_ref[:, : up8(FIELDS * rows)].T
    for field in range(FIELDS):
        out_ref[field, 0] = back[field * rows : (field + 1) * rows]


def up8(size):
    return -(-size // 8) * 8


def call(kernel, outs, scratch, cost, name, space=pltpu.VMEM, fuse=None):
    vmem = pl.BlockSpec(memory_space=pltpu.VMEM)
    given = pl.BlockSpec(memory_space=space)
    shapes = [jax.ShapeDtypeStruct(shape, jnp.float32) for shape in outs]

    def run(*args):
        return pl.pallas_call(
            kernel,
            out_shape=shapes if len(shapes) > 1 else shapes[0],
            in_specs=[given] * len(args),
            out_specs=[vmem] * len(shapes) if len(shapes) > 1 else vmem,
            scratch_shapes=[
                pltpu.VMEM(shape, jnp.float32) if isinstance(shape, tuple) else shape
                for shape in scratch
            ],
            cost_estimate=pl.CostEstimate(flops=cost, bytes_accessed=cost // 4, transcendentals=0),
            name=name,
            compiler_params=pltpu.CompilerParams(vmem_limit_bytes=16 * 1024 * 1024, allow_input_fusion=fuse),
        )(*args)

    return run


def by_columns(state, labels):
    _, _, rows, nx = state.shape
    count_a, count_b = lax.axis_size("aa"), lax.axis_size("ba")
    devices = count_a * count_b
    used = (FIELDS + 1 + CHANGED) * rows + 1
    padded = -(-used // 128) * 128

    def swap(array):
        parts = array.reshape(devices, nx // devices, padded)
        return lax.all_to_all(parts, ("aa", "ba"), 0, 0, tiled=True).reshape(nx, padded)

    columns = call(
        columns_kernel,
        [(nx, padded)],
        [
            (2, FIELDS, 2 * rows, nx),
            (up8(used), nx),
        ],
        4_000_000,
        "columns",
        fuse=[False, True],
    )(state, labels.astype(jnp.float32))
    faces = up8(rows + 1)
    swept = call(
        functools.partial(sweeps_kernel, rows, count_a, count_b),
        [(nx, padded)],
        [
            (up8(used), nx),
            (FIELDS + 1, up8(2 * REACH + rows), nx),
            (CHANGED, faces, nx),
            (2, FIELDS, 2 * rows, nx),
            (6, up8(FIELDS * (rows + 1)), nx),
            (2, up8(FIELDS * (rows + 1)), nx),
            (FIELDS // 2, 2 * rows, nx),
        ],
        8_000_000,
        "sweeps",
    )(swap(columns))
    return call(home_kernel, [state.shape], [], 100_000, "home")(swap(swept))


def shards(state, labels):
    _, depth, rows, nx = state.shape
    assert depth == 1 and rows >= REACH and nx % 128 == 0
    count_a, count_b = lax.axis_size("aa"), lax.axis_size("ba")
    devices = count_a * count_b
    if nx % devices == 0 and count_b >= FIELDS // 2:
        return by_columns(state, labels)
    total = rows + 2 * REACH
    tall = up8(total)
    small = devices <= SMALL_GROUP
    peak, packed = call(
        peak_kernel,
        [(devices if small else 8, 128), (FIELDS + 1, rows, nx)],
        [],
        200_000,
        "peak",
    )(state, labels)
    ups = [(i, i + 1) for i in range(count_a - 1)]
    low = lax.ppermute(packed, "aa", ups)
    high = lax.ppermute(packed, "aa", [(j, i) for i, j in ups])
    if small:
        peaks = lax.all_to_all(peak, ("aa", "ba"), 0, 0, tiled=True)
    else:
        peaks = lax.pmax(peak, ("aa", "ba"))
    cells, change = call(
        x_kernel,
        [(FIELDS + 1, tall, nx), (8, tall, nx)],
        [(FIELDS + 1, up8(2 * total), nx)],
        4_000_000,
        "xflux",
    )(packed, low, high)
    exchange = count_b <= SMALL_AXIS
    faces = up8(rows + 1)
    after_y, step = call(
        y_kernel,
        [(count_b if exchange else 1, FIELDS + 1, rows, nx), (8, 128)],
        [(FIELDS + 1, max(tall, up8(2 * REACH - 1 + faces)), nx), (8, faces, nx)],
        4_000_000,
        "ysweep",
    )(peaks, cells, change)
    if exchange:
        lines = lax.all_to_all(after_y, "ba", 0, 0, tiled=True)
    else:
        near = []
        for shift in range(-REACH, REACH + 1):
            pairs = [(i, i - shift) for i in range(count_b) if 0 <= i - shift < count_b]
            near.append(lax.ppermute(after_y, "ba", pairs) if shift else after_y)
        lines = jnp.concatenate(near, axis=0)
    return call(
        functools.partial(z_kernel, not exchange),
        [(FIELDS, 1, rows, nx)],
        [(FIELDS + 1, (2 * REACH + 1) * rows, nx)],
        4_000_000,
        "zsweep",
    )(step, lines)


def solution(mesh):
    return jax.shard_map(
        shards,
        mesh=mesh,
        in_specs=(P(None, "ba", "aa", None), P("ba", "aa", None)),
        out_specs=P(None, "ba", "aa", None),
        check_vma=False,
    )
```

```python
import functools

import jax
import jax.numpy as jnp
from jax import lax
from jax.experimental import pallas as pl
from jax.experimental.pallas import tpu as pltpu
from jax.sharding import PartitionSpec as P

RETURN_ITERS = 2
REACH = 3
FIELDS = 14
DENSITY_FLOOR = 0.2
TRACTION_FLOOR = 0.1
COURANT = 0.4
WENO_EPSILON = 1e-06
TINY = 1e-36
SMALL_GROUP = 32
SMALL_AXIS = 8


def pick(label, sand, solid, void):
    return jnp.where(label == 0.0, sand, jnp.where(label == 1.0, solid, void))


def material(label):
    gamma = pick(label, 3.0, 4.0, 1.4)
    stiff = jnp.where(label == 1.0, 6.0, jnp.where(label == 0.0, 1.0, 0.0))
    shear = pick(label, 0.6, 3.0, 0.0)
    return gamma, stiff, shear


def deviator(grad):
    metric = {}
    for i in range(3):
        for j in range(i, 3):
            metric[i, j] = (
                grad[0][i] * grad[0][j] + grad[1][i] * grad[1][j] + grad[2][i] * grad[2][j]
            )
    third = (metric[0, 0] + metric[1, 1] + metric[2, 2]) * (1.0 / 3.0)
    for i in range(3):
        metric[i, i] = metric[i, i] - third
    return metric


def square_sum(dev):
    off = dev[0, 1] * dev[0, 1] + dev[0, 2] * dev[0, 2] + dev[1, 2] * dev[1, 2]
    diag = dev[0, 0] * dev[0, 0] + dev[1, 1] * dev[1, 1] + dev[2, 2] * dev[2, 2]
    return diag + (off + off)


def grad_of(fields):
    return [[fields[5 + 3 * row + col] for col in range(3)] for row in range(3)]


def pressure_of(fields, dev, mats):
    gamma, stiff, shear = mats
    density = jnp.maximum(fields[0], DENSITY_FLOOR)
    inverse = 1.0 / density
    velocity = [fields[1 + comp] * inverse for comp in range(3)]
    kinetic = 0.5 * (
        fields[1] * velocity[0] + fields[2] * velocity[1] + fields[3] * velocity[2]
    )
    energy = (0.25 * shear) * square_sum(dev)
    pressure = (gamma - 1.0) * (fields[4] - kinetic - energy) - gamma * stiff
    return density, inverse, velocity, pressure


def primitives(fields, mats):
    gamma, stiff, shear = mats
    dev = deviator(grad_of(fields))
    density, inverse, velocity, pressure = pressure_of(fields, dev, mats)
    square = (gamma * jnp.maximum(pressure + stiff, TRACTION_FLOOR) + (4.0 / 3.0) * shear) * inverse
    sound = square * lax.rsqrt(jnp.maximum(square, TINY))
    return density, velocity, dev, pressure, sound


def weno_pair(v):
    d = [v[i + 1] - v[i] for i in range(5)]
    b = [d[i + 1] - d[i] for i in range(4)]
    d1, d2, d3 = d[1] + d[1], d[2] + d[2], d[3] + d[3]
    bend = [4.0 * WENO_EPSILON + (13.0 / 3.0) * (x * x) for x in b]
    outer0, outer3 = (4.0 / 3.0) * b[0], (4.0 / 3.0) * b[3]
    inner1, inner2 = (2.0 / 3.0) * b[1], (2.0 / 3.0) * b[2]

    def shift(slopes, bends, steps):
        inv = [1.0 / (bends[i] + slopes[i] * slopes[i]) for i in range(3)]
        weight = [inv[0] * inv[0], 6.0 * (inv[1] * inv[1]), 3.0 * (inv[2] * inv[2])]
        total = weight[0] * steps[0] + weight[1] * steps[1] + weight[2] * steps[2]
        return 0.25 * (total / (weight[0] + weight[1] + weight[2]))

    left = v[2] + shift(
        (d1 + b[0], d1 + b[1], d2 - b[2]),
        (bend[0], bend[1], bend[2]),
        (d1 + outer0, d2 - inner1, d2 - inner2),
    )
    right = v[3] - shift(
        (d3 - b[3], d2 + b[2], d2 + b[1]),
        (bend[3], bend[2], bend[1]),
        (d3 - outer3, d2 + inner2, d2 + inner1),
    )
    return left, right


def riemann(lf, rf, left_label, right_label, d):
    left_mats, right_mats = material(left_label), material(right_label)
    l_rho, l_vel, l_dev, l_p, l_c = primitives(lf, left_mats)
    r_rho, r_vel, r_dev, r_p, r_c = primitives(rf, right_mats)

    def stress(dev, mats, i, j):
        return -mats[2] * dev[min(i, j), max(i, j)]

    l_s = [stress(l_dev, left_mats, k, d) for k in range(3)]
    r_s = [stress(r_dev, right_mats, k, d) for k in range(3)]
    l_u, r_u = l_vel[d], r_vel[d]
    slow = jnp.minimum(l_u - l_c, r_u - r_c)
    fast = jnp.maximum(l_u + l_c, r_u + r_c)
    l_t, r_t = l_p - l_s[d], r_p - r_s[d]
    l_gap, r_gap = slow - l_u, fast - r_u
    l_push, r_push = l_rho * l_gap, r_rho * r_gap
    contact = (r_t - l_t + l_push * l_u - r_push * r_u) / (l_push - r_push)
    width = fast - slow
    margin = 0.05 * width
    contact = jnp.minimum(jnp.maximum(contact, slow + margin), fast - margin)

    go_left = (slow >= 0.0) | (contact >= 0.0)
    plain = (slow >= 0.0) | (jnp.logical_not(contact >= 0.0) & jnp.logical_not(fast > 0.0))

    def side(a, b):
        return jnp.where(go_left, a, b)

    rho, gap, wave, trac = side(l_rho, r_rho), side(l_gap, r_gap), side(slow, fast), side(l_t, r_t)
    vel = [side(l_vel[k], r_vel[k]) for k in range(3)]
    mom = [side(lf[1 + k], rf[1 + k]) for k in range(3)]
    ener = side(lf[4], rf[4])
    u = vel[d]
    ratio = gap / (wave - contact)
    mass = rho * ratio
    star_e = ratio * (ener + (contact - u) * (rho * contact + trac / gap))
    result = [mom[d] + jnp.where(plain, 0.0, wave * (mass - rho))]
    for k in range(3):
        flux = mom[k] * u + trac if k == d else mom[k] * u
        star = mass * (contact if k == d else vel[k])
        result.append(flux + jnp.where(plain, 0.0, wave * (star - mom[k])))
    result.append((ener + trac) * u + jnp.where(plain, 0.0, wave * (star_e - ener)))
    for k in range(3):
        if k != d:
            result[1 + k] = result[1 + k] - 0.5 * (l_s[k] + r_s[k])
            result[4] = result[4] - 0.5 * (l_s[k] * l_vel[k] + r_s[k] * r_vel[k])
    inverse = 1.0 / width
    for row in range(3):
        base = 5 + 3 * row
        l_flow = lf[base] * l_vel[0] + lf[base + 1] * l_vel[1] + lf[base + 2] * l_vel[2]
        r_flow = rf[base] * r_vel[0] + rf[base + 1] * r_vel[1] + rf[base + 2] * r_vel[2]
        jump = rf[base + d] - lf[base + d]
        blend = (fast * l_flow - slow * r_flow + slow * fast * jump) * inverse
        result.append(jnp.where(slow >= 0.0, l_flow, jnp.where(fast <= 0.0, r_flow, blend)))
    return result


def changed_fields(d):
    return [0, 1, 2, 3, 4] + [5 + 3 * row + d for row in range(3)]


def face_values(window, fields):
    return [weno_pair([window(field, k) for k in range(6)]) for field in fields]


def face_fluxes(window, d, values=()):
    values = list(values) + face_values(window, range(len(values), FIELDS))
    left = [value[0] for value in values]
    right = [value[1] for value in values]
    return riemann(left, right, window(FIELDS, 2), window(FIELDS, 3), d)


def plastic(fields, label):
    mats = material(label)
    sandy = label == 0.0
    grad = grad_of(fields)
    dev = deviator(grad)
    third = (grad[0][0] + grad[1][1] + grad[2][2]) * (1.0 / 3.0)
    rest = [[grad[i][j] - third if i == j else grad[i][j] for j in range(3)] for i in range(3)]
    even = {(i, j): third * (rest[i][j] + rest[j][i]) for i, j in dev}
    pure = {key: dev[key] - even[key] for key in dev}
    pressure = pressure_of(fields, dev, mats)[3]
    radius = 0.025 + 0.2 * jnp.maximum(pressure, 0.0)
    product = None
    for turn in range(RETURN_ITERS):
        if turn:
            dev = {key: product * (product * pure[key] + even[key]) for key in dev}
        factor = 0.5 + jnp.minimum(radius * lax.rsqrt(0.36 * square_sum(dev)), 0.5)
        product = product * factor if turn else factor
    product = jnp.where(sandy, product, 1.0)
    less = product - 1.0
    return list(fields[:5]) + [
        grad[i][j] + less * rest[i][j] if i == j else product * grad[i][j]
        for i in range(3)
        for j in range(3)
    ]


def peak_kernel(state_ref, label_ref, peak_ref, packed_ref):
    rows = state_ref.shape[2]
    label = label_ref[0].astype(jnp.float32)
    fields = [state_ref[field, 0] for field in range(FIELDS)]
    for field in range(FIELDS):
        packed_ref[field] = fields[field]
    packed_ref[FIELDS] = label
    density, velocity, dev, pressure, sound = primitives(fields, material(label))
    speed = sound + jnp.maximum(
        jnp.maximum(jnp.abs(velocity[0]), jnp.abs(velocity[1])), jnp.abs(velocity[2])
    )
    best = speed[:, :128]
    for start in range(128, speed.shape[1], 128):
        best = jnp.maximum(best, speed[:, start : start + 128])
    best = jnp.max(best, axis=0, keepdims=True)
    peak_ref[...] = jnp.broadcast_to(best, peak_ref.shape)


def x_kernel(own_ref, low_ref, high_ref, out_ref, flux_ref, line_ref):
    rows, nx = own_ref.shape[1:]
    total = rows + 2 * REACH
    stack = line_ref.shape[1]
    pos, count = lax.axis_index("aa"), lax.axis_size("aa")
    first, last = pos == 0, pos == count - 1
    for field in range(FIELDS + 1):
        own = own_ref[field]
        low = jnp.where(first, own[:1], low_ref[field, rows - REACH :])
        high = jnp.where(last, own[rows - 1 :], high_ref[field, :REACH])
        out_ref[field, :REACH] = low
        out_ref[field, REACH : REACH + rows] = own
        out_ref[field, REACH + rows : total] = high
        out_ref[field, total:] = jnp.zeros((out_ref.shape[1] - total, nx), jnp.float32)
    lane = lax.broadcasted_iota(jnp.int32, (total, nx), 1)
    wide = lax.broadcasted_iota(jnp.int32, (stack, nx), 1)
    for field in range(FIELDS + 1):
        cells = out_ref[field, :total]
        line_ref[field, :total] = cells
        line_ref[field, total : 2 * total] = jnp.where(
            lane == nx - 1, cells, pltpu.roll(cells, nx - 1, 1)
        )
        if stack > 2 * total:
            line_ref[field, 2 * total :] = jnp.zeros((stack - 2 * total, nx), jnp.float32)
    cache = {}

    def window(field, k):
        if (field, k) not in cache:
            if k == 3:
                value = line_ref[field]
            elif k < 3:
                near = window(field, k + 1)
                value = jnp.where(wide == 0, near, pltpu.roll(near, 1, 1))
            else:
                near = window(field, k - 1)
                value = jnp.where(wide == nx - 1, near, pltpu.roll(near, nx - 1, 1))
            cache[field, k] = value
        return cache[field, k]

    for slot, flux in enumerate(face_fluxes(window, 0)):
        line_ref[slot] = flux
    for slot in range(8):
        lower = line_ref[slot, :total]
        upper = line_ref[slot, total : 2 * total]
        flux_ref[slot, :total] = (
            jnp.where(lane == nx - 1, upper, pltpu.roll(lower, nx - 1, 1)) - lower
        )
        flux_ref[slot, total:] = jnp.zeros((flux_ref.shape[1] - total, nx), jnp.float32)


def step_of(peak_ref):
    best = jnp.max(peak_ref[...], axis=0, keepdims=True)
    return COURANT / jnp.max(best, axis=1, keepdims=True)


def y_kernel(peak_ref, cells_ref, change_ref, out_ref, step_ref, line_ref, face_ref):
    copies, _, rows, nx = out_ref.shape
    step = step_of(peak_ref)
    step_ref[...] = jnp.broadcast_to(step, step_ref.shape)
    label = cells_ref[FIELDS]
    fields = [cells_ref[field] for field in range(FIELDS)]
    for slot, field in enumerate(changed_fields(0)):
        fields[field] = fields[field] - step * change_ref[slot]
    fields = plastic(fields, label)
    height = label.shape[0]
    for field in range(FIELDS):
        line_ref[field, :height] = fields[field]
    line_ref[FIELDS, :height] = label
    faces = face_ref.shape[1]
    for field in range(FIELDS + 1):
        if line_ref.shape[1] > height:
            line_ref[field, height:] = jnp.zeros((line_ref.shape[1] - height, nx), jnp.float32)
    fluxes = face_fluxes(lambda field, k: line_ref[field, k : k + faces], 1)
    for slot in range(8):
        face_ref[slot] = fluxes[slot]
    label = line_ref[FIELDS, REACH : REACH + rows]
    fields = [line_ref[field, REACH : REACH + rows] for field in range(FIELDS)]
    for slot, field in enumerate(changed_fields(1)):
        change = face_ref[slot, 1 : rows + 1] - face_ref[slot, :rows]
        fields[field] = fields[field] - step * change
    fields = plastic(fields, label) + [label]
    for copy in range(copies):
        for field in range(FIELDS + 1):
            out_ref[copy, field] = fields[field]


def z_kernel(centred, step_ref, lines_ref, out_ref, line_ref):
    rows = out_ref.shape[2]
    pos, count = lax.axis_index("ba"), lax.axis_size("ba")
    step = step_ref[:rows, :1]
    for k in range(2 * REACH + 1):
        where = jnp.clip(pos + k - REACH, 0, count - 1)
        if centred:
            where = where - pos + REACH
        for field in range(FIELDS + 1):
            line_ref[field, k * rows : (k + 1) * rows] = lines_ref[where, field]
    fluxes = face_fluxes(
        lambda field, k: line_ref[field, k * rows : (k + 2) * rows], 2
    )
    centre = slice(REACH * rows, (REACH + 1) * rows)
    label = line_ref[FIELDS, centre]
    fields = [line_ref[field, centre] for field in range(FIELDS)]
    for slot, field in enumerate(changed_fields(2)):
        fields[field] = fields[field] - step * (fluxes[slot][rows:] - fluxes[slot][:rows])
    fields = plastic(fields, label)
    for field in range(FIELDS):
        out_ref[field, 0] = fields[field]


CHANGED = 8


def columns_kernel(
    state_ref, label_ref, out_ref, both_ref, stage_ref
):
    rows, nx = label_ref.shape[1:]
    label = label_ref[0]
    held = FIELDS * rows
    stage_ref[:held] = state_ref[...]
    stage_ref[held : held + rows] = label
    fields = [state_ref[field * rows : (field + 1) * rows] for field in range(FIELDS)]
    density, velocity, dev, pressure, sound = primitives(fields, material(label))
    speed = sound + jnp.maximum(
        jnp.maximum(jnp.abs(velocity[0]), jnp.abs(velocity[1])), jnp.abs(velocity[2])
    )
    used = (FIELDS + 1 + CHANGED) * rows
    stage_ref[used:] = jnp.broadcast_to(
        jnp.max(speed, keepdims=True), (stage_ref.shape[0] - used, nx)
    )
    pairs = [state_ref[field * rows : (field + 2) * rows] for field in range(0, FIELDS, 2)]
    for slot, change in enumerate(line_changes(pairs, both_ref, label, nx, 1, 0)):
        start = (FIELDS + 1 + slot) * rows
        stage_ref[start : start + rows] = change
    tall = stage_ref.shape[0]
    out_ref[:, :tall] = stage_ref[...].T


def line_changes(pairs, both_ref, label, group, width, d):
    tall, nx = pairs[0].shape
    rows = tall // 2
    lane = lax.broadcasted_iota(jnp.int32, (tall, nx), 1)

    def within(low, high):
        hit = lane < 0
        for start in range(0, nx, group):
            hit = hit | ((lane >= start + low * width) & (lane < start + high * width))
        return hit

    cells = group // width
    first = {n: within(0, n) for n in (1, 2, 3)}
    last = {n: within(cells - n, cells) for n in (1, 2)}
    ends = None
    for p, own in enumerate(pairs):
        moved = {n: pltpu.roll(own, n * width, 1) for n in {1, 2, 3, p + 1, p + 2, p + 3}}
        ahead = [pltpu.roll(own, nx - n * width, 1) for n in (1, 2)]
        low1 = jnp.where(first[1], own, moved[1])
        low2 = jnp.where(first[2], low1, moved[2])
        low3 = jnp.where(first[3], low2, moved[3])
        high1 = jnp.where(last[1], own, ahead[0])
        high2 = jnp.where(last[2], high1, ahead[1])
        values = weno_pair([low3, low2, low1, own, high1, high2])
        for side in range(2):
            both_ref[side, 2 * p, :rows] = values[side][:rows]
            both_ref[side, 2 * p + 1, :rows] = values[side][rows:]
        mine = [moved[p + 1 + n] for n in range(3)]
        if ends is None:
            ends = mine
        else:
            slot = within(p, p + 1)
            ends = [jnp.where(slot, new, old) for new, old in zip(mine, ends)]
    values = weno_pair([ends[2], ends[1], ends[0], ends[0], ends[0], ends[0]])
    for p in range(len(pairs)):
        for side in range(2):
            value = values[side]
            value = pltpu.roll(value, nx - p * width, 1) if p else value
            both_ref[side, 2 * p, rows:] = value[:rows]
            both_ref[side, 2 * p + 1, rows:] = value[rows:]
    left = [both_ref[0, field] for field in range(FIELDS)]
    right = [both_ref[1, field] for field in range(FIELDS)]
    kinds = jnp.concatenate([label, label], axis=0)
    before = pltpu.roll(kinds, width, 1)
    upper = lax.broadcasted_iota(jnp.int32, (tall, nx), 0) >= rows
    left_kinds = jnp.where(first[1] & jnp.logical_not(upper), kinds, before)
    fluxes = riemann(left, right, left_kinds, jnp.where(upper, before, kinds), d)
    start = first[1][:rows]
    changes = []
    for flux in fluxes:
        faces = jnp.where(start, flux[rows:], flux[:rows])
        changes.append(pltpu.roll(faces, nx - width, 1) - flux[:rows])
    return changes


def sweeps_kernel(rows, count_a, count_b, in_ref, out_ref, stage_ref, line_ref, face_ref, deep_ref, pair_ref):
    nx = in_ref.shape[0]
    group = nx // count_a
    width = group // count_b
    tall = stage_ref.shape[0]
    stage_ref[...] = in_ref[:, :tall].T
    used = (FIELDS + 1 + CHANGED) * rows
    step = COURANT / jnp.max(in_ref[:, used : used + 1], axis=0, keepdims=True)

    def block(index):
        return stage_ref[index * rows : (index + 1) * rows, :]

    label = block(FIELDS)
    fields = [block(field) for field in range(FIELDS)]
    for slot, field in enumerate(changed_fields(0)):
        fields[field] = fields[field] - step * block(FIELDS + 1 + slot)

    lane = lax.broadcasted_iota(jnp.int32, (REACH, nx), 1)
    faces = rows + 1

    def lay(field, cells):
        low = pltpu.roll(cells, group, 1)[rows - REACH :]
        high = pltpu.roll(cells, nx - group, 1)[:REACH]
        line_ref[field, :REACH] = jnp.where(lane < group, cells[:1], low)
        line_ref[field, REACH : REACH + rows] = cells
        line_ref[field, REACH + rows : 2 * REACH + rows] = jnp.where(
            lane >= nx - group, cells[rows - 1 :], high
        )

    def window(field, k):
        return line_ref[field, k : k + faces]

    lay(FIELDS, label)
    fields = plastic(fields, label)
    for field in range(FIELDS):
        lay(field, fields[field])
    values = face_values(window, range(FIELDS))
    fluxes = face_fluxes(window, 1, values)
    for slot in range(CHANGED):
        face_ref[slot, :faces] = fluxes[slot]
    for slot, field in enumerate(changed_fields(1)):
        change = face_ref[slot, 1 : rows + 1] - face_ref[slot, :rows]
        fields[field] = fields[field] - step * change

    fields = plastic(fields, label)
    for field in range(FIELDS):
        pair_ref[field // 2, (field % 2) * rows : (field % 2 + 1) * rows] = fields[field]
    pairs = [pair_ref[p] for p in range(FIELDS // 2)]
    changes = line_changes(pairs, deep_ref, label, group, width, 2)
    for slot, field in enumerate(changed_fields(2)):
        fields[field] = fields[field] - step * changes[slot]
    fields = plastic(fields, label)
    for field in range(FIELDS):
        stage_ref[field * rows : (field + 1) * rows, :] = fields[field]
    tall = up8(FIELDS * rows)
    out_ref[:, :tall] = stage_ref[:tall].T


def home_kernel(in_ref, out_ref):
    held = out_ref.shape[0]
    out_ref[...] = in_ref[:, : up8(held)].T[:held]


def up8(size):
    return -(-size // 8) * 8


def call(kernel, outs, scratch, cost, name, space=pltpu.VMEM, fuse=None):
    vmem = pl.BlockSpec(memory_space=pltpu.VMEM)
    given = pl.BlockSpec(memory_space=space)
    shapes = [jax.ShapeDtypeStruct(shape, jnp.float32) for shape in outs]

    def run(*args):
        return pl.pallas_call(
            kernel,
            out_shape=shapes if len(shapes) > 1 else shapes[0],
            in_specs=[given] * len(args),
            out_specs=[vmem] * len(shapes) if len(shapes) > 1 else vmem,
            scratch_shapes=[
                pltpu.VMEM(shape, jnp.float32) if isinstance(shape, tuple) else shape
                for shape in scratch
            ],
            cost_estimate=pl.CostEstimate(flops=cost, bytes_accessed=cost // 4, transcendentals=0),
            name=name,
            compiler_params=pltpu.CompilerParams(vmem_limit_bytes=16 * 1024 * 1024, allow_input_fusion=fuse),
        )(*args)

    return run


def by_columns(state, labels):
    _, _, rows, nx = state.shape
    count_a, count_b = lax.axis_size("aa"), lax.axis_size("ba")
    devices = count_a * count_b
    used = (FIELDS + 1 + CHANGED) * rows + 1
    padded = -(-used // 128) * 128

    def swap(array):
        parts = array.reshape(devices, nx // devices, padded)
        return lax.all_to_all(parts, ("aa", "ba"), 0, 0, tiled=True).reshape(nx, padded)

    columns = call(
        columns_kernel,
        [(nx, padded)],
        [
            (2, FIELDS, 2 * rows, nx),
            (up8(used), nx),
        ],
        4_000_000,
        "columns",
        fuse=[False, True],
    )(state.reshape(FIELDS * rows, nx), labels.astype(jnp.float32))
    faces = up8(rows + 1)
    swept = call(
        functools.partial(sweeps_kernel, rows, count_a, count_b),
        [(nx, padded)],
        [
            (up8(used), nx),
            (FIELDS + 1, up8(2 * REACH + rows), nx),
            (CHANGED, faces, nx),
            (2, FIELDS, 2 * rows, nx),
            (FIELDS // 2, 2 * rows, nx),
        ],
        8_000_000,
        "sweeps",
    )(swap(columns))
    home = call(home_kernel, [(FIELDS * rows, nx)], [], 100_000, "home")
    return home(swap(swept)).reshape(state.shape)


def shards(state, labels):
    _, depth, rows, nx = state.shape
    assert depth == 1 and rows >= REACH and nx % 128 == 0
    count_a, count_b = lax.axis_size("aa"), lax.axis_size("ba")
    devices = count_a * count_b
    if nx % devices == 0 and count_b >= FIELDS // 2:
        return by_columns(state, labels)
    total = rows + 2 * REACH
    tall = up8(total)
    small = devices <= SMALL_GROUP
    peak, packed = call(
        peak_kernel,
        [(devices if small else 8, 128), (FIELDS + 1, rows, nx)],
        [],
        200_000,
        "peak",
    )(state, labels)
    ups = [(i, i + 1) for i in range(count_a - 1)]
    low = lax.ppermute(packed, "aa", ups)
    high = lax.ppermute(packed, "aa", [(j, i) for i, j in ups])
    if small:
        peaks = lax.all_to_all(peak, ("aa", "ba"), 0, 0, tiled=True)
    else:
        peaks = lax.pmax(peak, ("aa", "ba"))
    cells, change = call(
        x_kernel,
        [(FIELDS + 1, tall, nx), (8, tall, nx)],
        [(FIELDS + 1, up8(2 * total), nx)],
        4_000_000,
        "xflux",
    )(packed, low, high)
    exchange = count_b <= SMALL_AXIS
    faces = up8(rows + 1)
    after_y, step = call(
        y_kernel,
        [(count_b if exchange else 1, FIELDS + 1, rows, nx), (8, 128)],
        [(FIELDS + 1, max(tall, up8(2 * REACH - 1 + faces)), nx), (8, faces, nx)],
        4_000_000,
        "ysweep",
    )(peaks, cells, change)
    if exchange:
        lines = lax.all_to_all(after_y, "ba", 0, 0, tiled=True)
    else:
        near = []
        for shift in range(-REACH, REACH + 1):
            pairs = [(i, i - shift) for i in range(count_b) if 0 <= i - shift < count_b]
            near.append(lax.ppermute(after_y, "ba", pairs) if shift else after_y)
        lines = jnp.concatenate(near, axis=0)
    return call(
        functools.partial(z_kernel, not exchange),
        [(FIELDS, 1, rows, nx)],
        [(FIELDS + 1, (2 * REACH + 1) * rows, nx)],
        4_000_000,
        "zsweep",
    )(step, lines)


def solution(mesh):
    return jax.shard_map(
        shards,
        mesh=mesh,
        in_specs=(P(None, "ba", "aa", None), P("ba", "aa", None)),
        out_specs=P(None, "ba", "aa", None),
        check_vma=False,
    )
```

```python
import functools

import jax
import jax.numpy as jnp
from jax import lax
from jax.experimental import pallas as pl
from jax.experimental.pallas import tpu as pltpu
from jax.sharding import PartitionSpec as P

RETURN_ITERS = 2
REACH = 3
FIELDS = 14
DENSITY_FLOOR = 0.2
TRACTION_FLOOR = 0.1
COURANT = 0.4
WENO_EPSILON = 1e-06
TINY = 1e-36
SMALL_GROUP = 32
SMALL_AXIS = 8


def pick(label, sand, solid, void):
    return jnp.where(label == 0.0, sand, jnp.where(label == 1.0, solid, void))


def material(label):
    gamma = pick(label, 3.0, 4.0, 1.4)
    stiff = jnp.where(label == 1.0, 6.0, jnp.where(label == 0.0, 1.0, 0.0))
    shear = pick(label, 0.6, 3.0, 0.0)
    return gamma, stiff, shear


def deviator(grad):
    metric = {}
    for i in range(3):
        for j in range(i, 3):
            metric[i, j] = (
                grad[0][i] * grad[0][j] + grad[1][i] * grad[1][j] + grad[2][i] * grad[2][j]
            )
    third = (metric[0, 0] + metric[1, 1] + metric[2, 2]) * (1.0 / 3.0)
    for i in range(3):
        metric[i, i] = metric[i, i] - third
    return metric


def square_sum(dev):
    off = dev[0, 1] * dev[0, 1] + dev[0, 2] * dev[0, 2] + dev[1, 2] * dev[1, 2]
    diag = dev[0, 0] * dev[0, 0] + dev[1, 1] * dev[1, 1] + dev[2, 2] * dev[2, 2]
    return diag + (off + off)


def grad_of(fields):
    return [[fields[5 + 3 * row + col] for col in range(3)] for row in range(3)]


def pressure_of(fields, dev, mats):
    gamma, stiff, shear = mats
    density = jnp.maximum(fields[0], DENSITY_FLOOR)
    inverse = 1.0 / density
    velocity = [fields[1 + comp] * inverse for comp in range(3)]
    kinetic = 0.5 * (
        fields[1] * velocity[0] + fields[2] * velocity[1] + fields[3] * velocity[2]
    )
    energy = (0.25 * shear) * square_sum(dev)
    pressure = (gamma - 1.0) * (fields[4] - kinetic - energy) - gamma * stiff
    return density, inverse, velocity, pressure


def primitives(fields, mats):
    gamma, stiff, shear = mats
    dev = deviator(grad_of(fields))
    density, inverse, velocity, pressure = pressure_of(fields, dev, mats)
    square = (gamma * jnp.maximum(pressure + stiff, TRACTION_FLOOR) + (4.0 / 3.0) * shear) * inverse
    sound = square * lax.rsqrt(jnp.maximum(square, TINY))
    return density, velocity, dev, pressure, sound


def weno_pair(v):
    d = [v[i + 1] - v[i] for i in range(5)]
    b = [d[i + 1] - d[i] for i in range(4)]
    d1, d2, d3 = d[1] + d[1], d[2] + d[2], d[3] + d[3]
    bend = [4.0 * WENO_EPSILON + (13.0 / 3.0) * (x * x) for x in b]
    outer0, outer3 = (4.0 / 3.0) * b[0], (4.0 / 3.0) * b[3]
    inner1, inner2 = (2.0 / 3.0) * b[1], (2.0 / 3.0) * b[2]

    def shift(slopes, bends, steps):
        inv = [1.0 / (bends[i] + slopes[i] * slopes[i]) for i in range(3)]
        weight = [inv[0] * inv[0], 6.0 * (inv[1] * inv[1]), 3.0 * (inv[2] * inv[2])]
        total = weight[0] * steps[0] + weight[1] * steps[1] + weight[2] * steps[2]
        return 0.25 * (total / (weight[0] + weight[1] + weight[2]))

    left = v[2] + shift(
        (d1 + b[0], d1 + b[1], d2 - b[2]),
        (bend[0], bend[1], bend[2]),
        (d1 + outer0, d2 - inner1, d2 - inner2),
    )
    right = v[3] - shift(
        (d3 - b[3], d2 + b[2], d2 + b[1]),
        (bend[3], bend[2], bend[1]),
        (d3 - outer3, d2 + inner2, d2 + inner1),
    )
    return left, right


def riemann(lf, rf, left_label, right_label, d):
    left_mats, right_mats = material(left_label), material(right_label)
    l_rho, l_vel, l_dev, l_p, l_c = primitives(lf, left_mats)
    r_rho, r_vel, r_dev, r_p, r_c = primitives(rf, right_mats)

    def stress(dev, mats, i, j):
        return -mats[2] * dev[min(i, j), max(i, j)]

    l_s = [stress(l_dev, left_mats, k, d) for k in range(3)]
    r_s = [stress(r_dev, right_mats, k, d) for k in range(3)]
    l_u, r_u = l_vel[d], r_vel[d]
    slow = jnp.minimum(l_u - l_c, r_u - r_c)
    fast = jnp.maximum(l_u + l_c, r_u + r_c)
    l_t, r_t = l_p - l_s[d], r_p - r_s[d]
    l_gap, r_gap = slow - l_u, fast - r_u
    l_push, r_push = l_rho * l_gap, r_rho * r_gap
    contact = (r_t - l_t + l_push * l_u - r_push * r_u) / (l_push - r_push)
    width = fast - slow
    margin = 0.05 * width
    contact = jnp.minimum(jnp.maximum(contact, slow + margin), fast - margin)

    go_left = (slow >= 0.0) | (contact >= 0.0)
    plain = (slow >= 0.0) | (jnp.logical_not(contact >= 0.0) & jnp.logical_not(fast > 0.0))

    def side(a, b):
        return jnp.where(go_left, a, b)

    rho, gap, wave, trac = side(l_rho, r_rho), side(l_gap, r_gap), side(slow, fast), side(l_t, r_t)
    vel = [side(l_vel[k], r_vel[k]) for k in range(3)]
    mom = [side(lf[1 + k], rf[1 + k]) for k in range(3)]
    ener = side(lf[4], rf[4])
    u = vel[d]
    ratio = gap / (wave - contact)
    mass = rho * ratio
    star_e = ratio * (ener + (contact - u) * (rho * contact + trac / gap))
    result = [mom[d] + jnp.where(plain, 0.0, wave * (mass - rho))]
    for k in range(3):
        flux = mom[k] * u + trac if k == d else mom[k] * u
        star = mass * (contact if k == d else vel[k])
        result.append(flux + jnp.where(plain, 0.0, wave * (star - mom[k])))
    result.append((ener + trac) * u + jnp.where(plain, 0.0, wave * (star_e - ener)))
    for k in range(3):
        if k != d:
            result[1 + k] = result[1 + k] - 0.5 * (l_s[k] + r_s[k])
            result[4] = result[4] - 0.5 * (l_s[k] * l_vel[k] + r_s[k] * r_vel[k])
    inverse = 1.0 / width
    for row in range(3):
        base = 5 + 3 * row
        l_flow = lf[base] * l_vel[0] + lf[base + 1] * l_vel[1] + lf[base + 2] * l_vel[2]
        r_flow = rf[base] * r_vel[0] + rf[base + 1] * r_vel[1] + rf[base + 2] * r_vel[2]
        jump = rf[base + d] - lf[base + d]
        blend = (fast * l_flow - slow * r_flow + slow * fast * jump) * inverse
        result.append(jnp.where(slow >= 0.0, l_flow, jnp.where(fast <= 0.0, r_flow, blend)))
    return result


def changed_fields(d):
    return [0, 1, 2, 3, 4] + [5 + 3 * row + d for row in range(3)]


def face_values(window, fields):
    return [weno_pair([window(field, k) for k in range(6)]) for field in fields]


def face_fluxes(window, d, values=()):
    values = list(values) + face_values(window, range(len(values), FIELDS))
    left = [value[0] for value in values]
    right = [value[1] for value in values]
    return riemann(left, right, window(FIELDS, 2), window(FIELDS, 3), d)


def plastic(fields, label):
    mats = material(label)
    sandy = label == 0.0
    grad = grad_of(fields)
    dev = deviator(grad)
    third = (grad[0][0] + grad[1][1] + grad[2][2]) * (1.0 / 3.0)
    rest = [[grad[i][j] - third if i == j else grad[i][j] for j in range(3)] for i in range(3)]
    even = {(i, j): third * (rest[i][j] + rest[j][i]) for i, j in dev}
    pure = {key: dev[key] - even[key] for key in dev}
    pressure = pressure_of(fields, dev, mats)[3]
    radius = 0.025 + 0.2 * jnp.maximum(pressure, 0.0)
    product = None
    for turn in range(RETURN_ITERS):
        if turn:
            dev = {key: product * (product * pure[key] + even[key]) for key in dev}
        factor = 0.5 + jnp.minimum(radius * lax.rsqrt(0.36 * square_sum(dev)), 0.5)
        product = product * factor if turn else factor
    product = jnp.where(sandy, product, 1.0)
    less = product - 1.0
    return list(fields[:5]) + [
        grad[i][j] + less * rest[i][j] if i == j else product * grad[i][j]
        for i in range(3)
        for j in range(3)
    ]


def peak_kernel(state_ref, label_ref, peak_ref, packed_ref):
    rows = state_ref.shape[2]
    label = label_ref[0].astype(jnp.float32)
    fields = [state_ref[field, 0] for field in range(FIELDS)]
    for field in range(FIELDS):
        packed_ref[field] = fields[field]
    packed_ref[FIELDS] = label
    density, velocity, dev, pressure, sound = primitives(fields, material(label))
    speed = sound + jnp.maximum(
        jnp.maximum(jnp.abs(velocity[0]), jnp.abs(velocity[1])), jnp.abs(velocity[2])
    )
    best = speed[:, :128]
    for start in range(128, speed.shape[1], 128):
        best = jnp.maximum(best, speed[:, start : start + 128])
    best = jnp.max(best, axis=0, keepdims=True)
    peak_ref[...] = jnp.broadcast_to(best, peak_ref.shape)


def x_kernel(own_ref, low_ref, high_ref, out_ref, flux_ref, line_ref):
    rows, nx = own_ref.shape[1:]
    total = rows + 2 * REACH
    stack = line_ref.shape[1]
    pos, count = lax.axis_index("aa"), lax.axis_size("aa")
    first, last = pos == 0, pos == count - 1
    for field in range(FIELDS + 1):
        own = own_ref[field]
        low = jnp.where(first, own[:1], low_ref[field, rows - REACH :])
        high = jnp.where(last, own[rows - 1 :], high_ref[field, :REACH])
        out_ref[field, :REACH] = low
        out_ref[field, REACH : REACH + rows] = own
        out_ref[field, REACH + rows : total] = high
        out_ref[field, total:] = jnp.zeros((out_ref.shape[1] - total, nx), jnp.float32)
    lane = lax.broadcasted_iota(jnp.int32, (total, nx), 1)
    wide = lax.broadcasted_iota(jnp.int32, (stack, nx), 1)
    for field in range(FIELDS + 1):
        cells = out_ref[field, :total]
        line_ref[field, :total] = cells
        line_ref[field, total : 2 * total] = jnp.where(
            lane == nx - 1, cells, pltpu.roll(cells, nx - 1, 1)
        )
        if stack > 2 * total:
            line_ref[field, 2 * total :] = jnp.zeros((stack - 2 * total, nx), jnp.float32)
    cache = {}

    def window(field, k):
        if (field, k) not in cache:
            if k == 3:
                value = line_ref[field]
            elif k < 3:
                near = window(field, k + 1)
                value = jnp.where(wide == 0, near, pltpu.roll(near, 1, 1))
            else:
                near = window(field, k - 1)
                value = jnp.where(wide == nx - 1, near, pltpu.roll(near, nx - 1, 1))
            cache[field, k] = value
        return cache[field, k]

    for slot, flux in enumerate(face_fluxes(window, 0)):
        line_ref[slot] = flux
    for slot in range(8):
        lower = line_ref[slot, :total]
        upper = line_ref[slot, total : 2 * total]
        flux_ref[slot, :total] = (
            jnp.where(lane == nx - 1, upper, pltpu.roll(lower, nx - 1, 1)) - lower
        )
        flux_ref[slot, total:] = jnp.zeros((flux_ref.shape[1] - total, nx), jnp.float32)


def step_of(peak_ref):
    best = jnp.max(peak_ref[...], axis=0, keepdims=True)
    return COURANT / jnp.max(best, axis=1, keepdims=True)


def y_kernel(peak_ref, cells_ref, change_ref, out_ref, step_ref, line_ref, face_ref):
    copies, _, rows, nx = out_ref.shape
    step = step_of(peak_ref)
    step_ref[...] = jnp.broadcast_to(step, step_ref.shape)
    label = cells_ref[FIELDS]
    fields = [cells_ref[field] for field in range(FIELDS)]
    for slot, field in enumerate(changed_fields(0)):
        fields[field] = fields[field] - step * change_ref[slot]
    fields = plastic(fields, label)
    height = label.shape[0]
    for field in range(FIELDS):
        line_ref[field, :height] = fields[field]
    line_ref[FIELDS, :height] = label
    faces = face_ref.shape[1]
    for field in range(FIELDS + 1):
        if line_ref.shape[1] > height:
            line_ref[field, height:] = jnp.zeros((line_ref.shape[1] - height, nx), jnp.float32)
    fluxes = face_fluxes(lambda field, k: line_ref[field, k : k + faces], 1)
    for slot in range(8):
        face_ref[slot] = fluxes[slot]
    label = line_ref[FIELDS, REACH : REACH + rows]
    fields = [line_ref[field, REACH : REACH + rows] for field in range(FIELDS)]
    for slot, field in enumerate(changed_fields(1)):
        change = face_ref[slot, 1 : rows + 1] - face_ref[slot, :rows]
        fields[field] = fields[field] - step * change
    fields = plastic(fields, label) + [label]
    for copy in range(copies):
        for field in range(FIELDS + 1):
            out_ref[copy, field] = fields[field]


def z_kernel(centred, step_ref, lines_ref, out_ref, line_ref):
    rows = out_ref.shape[2]
    pos, count = lax.axis_index("ba"), lax.axis_size("ba")
    step = step_ref[:rows, :1]
    for k in range(2 * REACH + 1):
        where = jnp.clip(pos + k - REACH, 0, count - 1)
        if centred:
            where = where - pos + REACH
        for field in range(FIELDS + 1):
            line_ref[field, k * rows : (k + 1) * rows] = lines_ref[where, field]
    fluxes = face_fluxes(
        lambda field, k: line_ref[field, k * rows : (k + 2) * rows], 2
    )
    centre = slice(REACH * rows, (REACH + 1) * rows)
    label = line_ref[FIELDS, centre]
    fields = [line_ref[field, centre] for field in range(FIELDS)]
    for slot, field in enumerate(changed_fields(2)):
        fields[field] = fields[field] - step * (fluxes[slot][rows:] - fluxes[slot][:rows])
    fields = plastic(fields, label)
    for field in range(FIELDS):
        out_ref[field, 0] = fields[field]


CHANGED = 8


def columns_kernel(
    state_ref, label_ref, out_ref, both_ref, stage_ref
):
    rows, nx = label_ref.shape[1:]
    label = label_ref[0]
    held = FIELDS * rows
    stage_ref[:held] = state_ref[...]
    stage_ref[held : held + rows] = label
    fields = [state_ref[field * rows : (field + 1) * rows] for field in range(FIELDS)]
    density, velocity, dev, pressure, sound = primitives(fields, material(label))
    speed = sound + jnp.maximum(
        jnp.maximum(jnp.abs(velocity[0]), jnp.abs(velocity[1])), jnp.abs(velocity[2])
    )
    used = (FIELDS + 1 + CHANGED) * rows
    stage_ref[used:] = jnp.broadcast_to(
        jnp.max(speed, keepdims=True), (stage_ref.shape[0] - used, nx)
    )
    pairs = [state_ref[field * rows : (field + 2) * rows] for field in range(0, FIELDS, 2)]
    for slot, change in enumerate(line_changes(pairs, both_ref, label, nx, 1, 0)):
        start = (FIELDS + 1 + slot) * rows
        stage_ref[start : start + rows] = change
    tall = stage_ref.shape[0]
    out_ref[:, :tall] = stage_ref[...].T


def line_changes(pairs, both_ref, label, group, width, d):
    tall, nx = pairs[0].shape
    rows = tall // 2
    lane = lax.broadcasted_iota(jnp.int32, (tall, nx), 1)

    def within(low, high):
        hit = lane < 0
        for start in range(0, nx, group):
            hit = hit | ((lane >= start + low * width) & (lane < start + high * width))
        return hit

    cells = group // width
    first = {n: within(0, n) for n in (1, 2, 3)}
    last = {n: within(cells - n, cells) for n in (1, 2)}
    ends = None
    for p, own in enumerate(pairs):
        moved = {n: pltpu.roll(own, n * width, 1) for n in {1, 2, 3, p + 1, p + 2, p + 3}}
        ahead = [pltpu.roll(own, nx - n * width, 1) for n in (1, 2)]
        low1 = jnp.where(first[1], own, moved[1])
        low2 = jnp.where(first[2], low1, moved[2])
        low3 = jnp.where(first[3], low2, moved[3])
        high1 = jnp.where(last[1], own, ahead[0])
        high2 = jnp.where(last[2], high1, ahead[1])
        values = weno_pair([low3, low2, low1, own, high1, high2])
        for side in range(2):
            both_ref[side, 2 * p, :rows] = values[side][:rows]
            both_ref[side, 2 * p + 1, :rows] = values[side][rows:]
        mine = [moved[p + 1 + n] for n in range(3)]
        if ends is None:
            ends = mine
        else:
            slot = within(p, p + 1)
            ends = [jnp.where(slot, new, old) for new, old in zip(mine, ends)]
    values = weno_pair([ends[2], ends[1], ends[0], ends[0], ends[0], ends[0]])
    for p in range(len(pairs)):
        for side in range(2):
            value = values[side]
            value = pltpu.roll(value, nx - p * width, 1) if p else value
            both_ref[side, 2 * p, rows:] = value[:rows]
            both_ref[side, 2 * p + 1, rows:] = value[rows:]
    left = [both_ref[0, field] for field in range(FIELDS)]
    right = [both_ref[1, field] for field in range(FIELDS)]
    kinds = jnp.concatenate([label, label], axis=0)
    before = pltpu.roll(kinds, width, 1)
    upper = lax.broadcasted_iota(jnp.int32, (tall, nx), 0) >= rows
    left_kinds = jnp.where(first[1] & jnp.logical_not(upper), kinds, before)
    fluxes = riemann(left, right, left_kinds, jnp.where(upper, before, kinds), d)
    start = first[1][:rows]
    changes = []
    for flux in fluxes:
        faces = jnp.where(start, flux[rows:], flux[:rows])
        changes.append(pltpu.roll(faces, nx - width, 1) - flux[:rows])
    return changes


def sweeps_kernel(rows, count_a, count_b, in_ref, out_ref, stage_ref, line_ref, face_ref, deep_ref, pair_ref):
    nx = in_ref.shape[0]
    group = nx // count_a
    width = group // count_b
    tall = stage_ref.shape[0]
    stage_ref[...] = in_ref[:, :tall].T
    used = (FIELDS + 1 + CHANGED) * rows
    step = COURANT / jnp.max(in_ref[:, used : used + 1], axis=0, keepdims=True)

    def block(index):
        return stage_ref[index * rows : (index + 1) * rows, :]

    label = block(FIELDS)
    fields = [block(field) for field in range(FIELDS)]
    for slot, field in enumerate(changed_fields(0)):
        fields[field] = fields[field] - step * block(FIELDS + 1 + slot)

    lane = lax.broadcasted_iota(jnp.int32, (REACH, nx), 1)
    faces = rows + 1

    def lay(field, cells, before, after):
        line_ref[field, :REACH] = jnp.where(lane < group, cells[:1], before[rows - REACH :])
        line_ref[field, REACH : REACH + rows] = cells
        line_ref[field, REACH + rows : 2 * REACH + rows] = jnp.where(
            lane >= nx - group, cells[rows - 1 :], after[:REACH]
        )

    def window(field, k):
        return line_ref[field, k : k + faces]

    lay(FIELDS, label, pltpu.roll(label, group, 1), pltpu.roll(label, nx - group, 1))
    fields = plastic(fields, label)
    for field in range(FIELDS):
        pair_ref[field // 2, (field % 2) * rows : (field % 2 + 1) * rows] = fields[field]
    for p in range(FIELDS // 2):
        before = pltpu.roll(pair_ref[p], group, 1)
        after = pltpu.roll(pair_ref[p], nx - group, 1)
        for half in range(2):
            part = slice(half * rows, (half + 1) * rows)
            lay(2 * p + half, fields[2 * p + half], before[part], after[part])
    values = face_values(window, range(FIELDS))
    fluxes = face_fluxes(window, 1, values)
    for slot in range(CHANGED):
        face_ref[slot, :faces] = fluxes[slot]
    for slot, field in enumerate(changed_fields(1)):
        change = face_ref[slot, 1 : rows + 1] - face_ref[slot, :rows]
        fields[field] = fields[field] - step * change

    fields = plastic(fields, label)
    for field in range(FIELDS):
        pair_ref[field // 2, (field % 2) * rows : (field % 2 + 1) * rows] = fields[field]
    pairs = [pair_ref[p] for p in range(FIELDS // 2)]
    changes = line_changes(pairs, deep_ref, label, group, width, 2)
    for slot, field in enumerate(changed_fields(2)):
        fields[field] = fields[field] - step * changes[slot]
    fields = plastic(fields, label)
    for field in range(FIELDS):
        stage_ref[field * rows : (field + 1) * rows, :] = fields[field]
    tall = up8(FIELDS * rows)
    out_ref[:, :tall] = stage_ref[:tall].T


def home_kernel(in_ref, out_ref):
    held = out_ref.shape[0]
    out_ref[...] = in_ref[:, : up8(held)].T[:held]


def up8(size):
    return -(-size // 8) * 8


def call(kernel, outs, scratch, cost, name, space=pltpu.VMEM, fuse=None):
    vmem = pl.BlockSpec(memory_space=pltpu.VMEM)
    given = pl.BlockSpec(memory_space=space)
    shapes = [jax.ShapeDtypeStruct(shape, jnp.float32) for shape in outs]

    def run(*args):
        return pl.pallas_call(
            kernel,
            out_shape=shapes if len(shapes) > 1 else shapes[0],
            in_specs=[given] * len(args),
            out_specs=[vmem] * len(shapes) if len(shapes) > 1 else vmem,
            scratch_shapes=[
                pltpu.VMEM(shape, jnp.float32) if isinstance(shape, tuple) else shape
                for shape in scratch
            ],
            cost_estimate=pl.CostEstimate(flops=cost, bytes_accessed=cost // 4, transcendentals=0),
            name=name,
            compiler_params=pltpu.CompilerParams(vmem_limit_bytes=16 * 1024 * 1024, allow_input_fusion=fuse),
        )(*args)

    return run


def by_columns(state, labels):
    _, _, rows, nx = state.shape
    count_a, count_b = lax.axis_size("aa"), lax.axis_size("ba")
    devices = count_a * count_b
    used = (FIELDS + 1 + CHANGED) * rows + 1
    padded = -(-used // 128) * 128

    def swap(array):
        parts = array.reshape(devices, nx // devices, padded)
        return lax.all_to_all(parts, ("aa", "ba"), 0, 0, tiled=True).reshape(nx, padded)

    columns = call(
        columns_kernel,
        [(nx, padded)],
        [
            (2, FIELDS, 2 * rows, nx),
            (up8(used), nx),
        ],
        4_000_000,
        "columns",
        fuse=[False, True],
    )(state.reshape(FIELDS * rows, nx), labels.astype(jnp.float32))
    faces = up8(rows + 1)
    swept = call(
        functools.partial(sweeps_kernel, rows, count_a, count_b),
        [(nx, padded)],
        [
            (up8(used), nx),
            (FIELDS + 1, up8(2 * REACH + rows), nx),
            (CHANGED, faces, nx),
            (2, FIELDS, 2 * rows, nx),
            (FIELDS // 2, 2 * rows, nx),
        ],
        8_000_000,
        "sweeps",
    )(swap(columns))
    home = call(home_kernel, [(FIELDS * rows, nx)], [], 100_000, "home")
    return home(swap(swept)).reshape(state.shape)


def shards(state, labels):
    _, depth, rows, nx = state.shape
    assert depth == 1 and rows >= REACH and nx % 128 == 0
    count_a, count_b = lax.axis_size("aa"), lax.axis_size("ba")
    devices = count_a * count_b
    if nx % devices == 0 and count_b >= FIELDS // 2:
        return by_columns(state, labels)
    total = rows + 2 * REACH
    tall = up8(total)
    small = devices <= SMALL_GROUP
    peak, packed = call(
        peak_kernel,
        [(devices if small else 8, 128), (FIELDS + 1, rows, nx)],
        [],
        200_000,
        "peak",
    )(state, labels)
    ups = [(i, i + 1) for i in range(count_a - 1)]
    low = lax.ppermute(packed, "aa", ups)
    high = lax.ppermute(packed, "aa", [(j, i) for i, j in ups])
    if small:
        peaks = lax.all_to_all(peak, ("aa", "ba"), 0, 0, tiled=True)
    else:
        peaks = lax.pmax(peak, ("aa", "ba"))
    cells, change = call(
        x_kernel,
        [(FIELDS + 1, tall, nx), (8, tall, nx)],
        [(FIELDS + 1, up8(2 * total), nx)],
        4_000_000,
        "xflux",
    )(packed, low, high)
    exchange = count_b <= SMALL_AXIS
    faces = up8(rows + 1)
    after_y, step = call(
        y_kernel,
        [(count_b if exchange else 1, FIELDS + 1, rows, nx), (8, 128)],
        [(FIELDS + 1, max(tall, up8(2 * REACH - 1 + faces)), nx), (8, faces, nx)],
        4_000_000,
        "ysweep",
    )(peaks, cells, change)
    if exchange:
        lines = lax.all_to_all(after_y, "ba", 0, 0, tiled=True)
    else:
        near = []
        for shift in range(-REACH, REACH + 1):
            pairs = [(i, i - shift) for i in range(count_b) if 0 <= i - shift < count_b]
            near.append(lax.ppermute(after_y, "ba", pairs) if shift else after_y)
        lines = jnp.concatenate(near, axis=0)
    return call(
        functools.partial(z_kernel, not exchange),
        [(FIELDS, 1, rows, nx)],
        [(FIELDS + 1, (2 * REACH + 1) * rows, nx)],
        4_000_000,
        "zsweep",
    )(step, lines)


def solution(mesh):
    return jax.shard_map(
        shards,
        mesh=mesh,
        in_specs=(P(None, "ba", "aa", None), P("ba", "aa", None)),
        out_specs=P(None, "ba", "aa", None),
        check_vma=False,
    )
```

```python
import functools

import jax
import jax.numpy as jnp
from jax import lax
from jax.experimental import pallas as pl
from jax.experimental.pallas import tpu as pltpu
from jax.sharding import PartitionSpec as P

RETURN_ITERS = 2
REACH = 3
FIELDS = 14
DENSITY_FLOOR = 0.2
TRACTION_FLOOR = 0.1
COURANT = 0.4
WENO_EPSILON = 1e-06
TINY = 1e-36
SMALL_GROUP = 32
SMALL_AXIS = 8


def pick(label, sand, solid, void):
    return jnp.where(label == 0.0, sand, jnp.where(label == 1.0, solid, void))


def material(label):
    gamma = pick(label, 3.0, 4.0, 1.4)
    stiff = jnp.where(label == 1.0, 6.0, jnp.where(label == 0.0, 1.0, 0.0))
    shear = pick(label, 0.6, 3.0, 0.0)
    return gamma, stiff, shear


def deviator(grad):
    metric = {}
    for i in range(3):
        for j in range(i, 3):
            metric[i, j] = (
                grad[0][i] * grad[0][j] + grad[1][i] * grad[1][j] + grad[2][i] * grad[2][j]
            )
    third = (metric[0, 0] + metric[1, 1] + metric[2, 2]) * (1.0 / 3.0)
    for i in range(3):
        metric[i, i] = metric[i, i] - third
    return metric


def square_sum(dev):
    off = dev[0, 1] * dev[0, 1] + dev[0, 2] * dev[0, 2] + dev[1, 2] * dev[1, 2]
    diag = dev[0, 0] * dev[0, 0] + dev[1, 1] * dev[1, 1] + dev[2, 2] * dev[2, 2]
    return diag + (off + off)


def grad_of(fields):
    return [[fields[5 + 3 * row + col] for col in range(3)] for row in range(3)]


def pressure_of(fields, dev, mats):
    gamma, stiff, shear = mats
    density = jnp.maximum(fields[0], DENSITY_FLOOR)
    inverse = 1.0 / density
    velocity = [fields[1 + comp] * inverse for comp in range(3)]
    kinetic = 0.5 * (
        fields[1] * velocity[0] + fields[2] * velocity[1] + fields[3] * velocity[2]
    )
    energy = (0.25 * shear) * square_sum(dev)
    pressure = (gamma - 1.0) * (fields[4] - kinetic - energy) - gamma * stiff
    return density, inverse, velocity, pressure


def primitives(fields, mats):
    gamma, stiff, shear = mats
    dev = deviator(grad_of(fields))
    density, inverse, velocity, pressure = pressure_of(fields, dev, mats)
    square = (gamma * jnp.maximum(pressure + stiff, TRACTION_FLOOR) + (4.0 / 3.0) * shear) * inverse
    sound = square * lax.rsqrt(jnp.maximum(square, TINY))
    return density, velocity, dev, pressure, sound


def weno_pair(v):
    d = [v[i + 1] - v[i] for i in range(5)]
    b = [d[i + 1] - d[i] for i in range(4)]
    d1, d2, d3 = d[1] + d[1], d[2] + d[2], d[3] + d[3]
    bend = [4.0 * WENO_EPSILON + (13.0 / 3.0) * (x * x) for x in b]
    outer0, outer3 = (4.0 / 3.0) * b[0], (4.0 / 3.0) * b[3]
    inner1, inner2 = (2.0 / 3.0) * b[1], (2.0 / 3.0) * b[2]

    def shift(slopes, bends, steps):
        inv = [1.0 / (bends[i] + slopes[i] * slopes[i]) for i in range(3)]
        weight = [inv[0] * inv[0], 6.0 * (inv[1] * inv[1]), 3.0 * (inv[2] * inv[2])]
        total = weight[0] * steps[0] + weight[1] * steps[1] + weight[2] * steps[2]
        return 0.25 * (total / (weight[0] + weight[1] + weight[2]))

    left = v[2] + shift(
        (d1 + b[0], d1 + b[1], d2 - b[2]),
        (bend[0], bend[1], bend[2]),
        (d1 + outer0, d2 - inner1, d2 - inner2),
    )
    right = v[3] - shift(
        (d3 - b[3], d2 + b[2], d2 + b[1]),
        (bend[3], bend[2], bend[1]),
        (d3 - outer3, d2 + inner2, d2 + inner1),
    )
    return left, right


def riemann(lf, rf, left_label, right_label, d):
    left_mats, right_mats = material(left_label), material(right_label)
    l_rho, l_vel, l_dev, l_p, l_c = primitives(lf, left_mats)
    r_rho, r_vel, r_dev, r_p, r_c = primitives(rf, right_mats)

    def stress(dev, mats, i, j):
        return -mats[2] * dev[min(i, j), max(i, j)]

    l_s = [stress(l_dev, left_mats, k, d) for k in range(3)]
    r_s = [stress(r_dev, right_mats, k, d) for k in range(3)]
    l_u, r_u = l_vel[d], r_vel[d]
    slow = jnp.minimum(l_u - l_c, r_u - r_c)
    fast = jnp.maximum(l_u + l_c, r_u + r_c)
    l_t, r_t = l_p - l_s[d], r_p - r_s[d]
    l_gap, r_gap = slow - l_u, fast - r_u
    l_push, r_push = l_rho * l_gap, r_rho * r_gap
    contact = (r_t - l_t + l_push * l_u - r_push * r_u) / (l_push - r_push)
    width = fast - slow
    margin = 0.05 * width
    contact = jnp.minimum(jnp.maximum(contact, slow + margin), fast - margin)

    go_left = (slow >= 0.0) | (contact >= 0.0)
    plain = (slow >= 0.0) | (jnp.logical_not(contact >= 0.0) & jnp.logical_not(fast > 0.0))

    def side(a, b):
        return jnp.where(go_left, a, b)

    rho, gap, wave, trac = side(l_rho, r_rho), side(l_gap, r_gap), side(slow, fast), side(l_t, r_t)
    vel = [side(l_vel[k], r_vel[k]) for k in range(3)]
    mom = [side(lf[1 + k], rf[1 + k]) for k in range(3)]
    ener = side(lf[4], rf[4])
    u = vel[d]
    ratio = gap / (wave - contact)
    mass = rho * ratio
    star_e = ratio * (ener + (contact - u) * (rho * contact + trac / gap))
    result = [mom[d] + jnp.where(plain, 0.0, wave * (mass - rho))]
    for k in range(3):
        flux = mom[k] * u + trac if k == d else mom[k] * u
        star = mass * (contact if k == d else vel[k])
        result.append(flux + jnp.where(plain, 0.0, wave * (star - mom[k])))
    result.append((ener + trac) * u + jnp.where(plain, 0.0, wave * (star_e - ener)))
    for k in range(3):
        if k != d:
            result[1 + k] = result[1 + k] - 0.5 * (l_s[k] + r_s[k])
            result[4] = result[4] - 0.5 * (l_s[k] * l_vel[k] + r_s[k] * r_vel[k])
    inverse = 1.0 / width
    for row in range(3):
        base = 5 + 3 * row
        l_flow = lf[base] * l_vel[0] + lf[base + 1] * l_vel[1] + lf[base + 2] * l_vel[2]
        r_flow = rf[base] * r_vel[0] + rf[base + 1] * r_vel[1] + rf[base + 2] * r_vel[2]
        jump = rf[base + d] - lf[base + d]
        blend = (fast * l_flow - slow * r_flow + slow * fast * jump) * inverse
        result.append(jnp.where(slow >= 0.0, l_flow, jnp.where(fast <= 0.0, r_flow, blend)))
    return result


def changed_fields(d):
    return [0, 1, 2, 3, 4] + [5 + 3 * row + d for row in range(3)]


def face_values(window, fields):
    return [weno_pair([window(field, k) for k in range(6)]) for field in fields]


def face_fluxes(window, d, values=()):
    values = list(values) + face_values(window, range(len(values), FIELDS))
    left = [value[0] for value in values]
    right = [value[1] for value in values]
    return riemann(left, right, window(FIELDS, 2), window(FIELDS, 3), d)


def plastic(fields, label):
    mats = material(label)
    sandy = label == 0.0
    grad = grad_of(fields)
    dev = deviator(grad)
    third = (grad[0][0] + grad[1][1] + grad[2][2]) * (1.0 / 3.0)
    rest = [[grad[i][j] - third if i == j else grad[i][j] for j in range(3)] for i in range(3)]
    even = {(i, j): third * (rest[i][j] + rest[j][i]) for i, j in dev}
    pure = {key: dev[key] - even[key] for key in dev}
    pressure = pressure_of(fields, dev, mats)[3]
    radius = 0.025 + 0.2 * jnp.maximum(pressure, 0.0)
    product = None
    for turn in range(RETURN_ITERS):
        if turn:
            dev = {key: product * (product * pure[key] + even[key]) for key in dev}
        factor = 0.5 + jnp.minimum(radius * lax.rsqrt(0.36 * square_sum(dev)), 0.5)
        product = product * factor if turn else factor
    product = jnp.where(sandy, product, 1.0)
    less = product - 1.0
    return list(fields[:5]) + [
        grad[i][j] + less * rest[i][j] if i == j else product * grad[i][j]
        for i in range(3)
        for j in range(3)
    ]


def peak_kernel(state_ref, label_ref, peak_ref, packed_ref):
    rows = state_ref.shape[2]
    label = label_ref[0].astype(jnp.float32)
    fields = [state_ref[field, 0] for field in range(FIELDS)]
    for field in range(FIELDS):
        packed_ref[field] = fields[field]
    packed_ref[FIELDS] = label
    density, velocity, dev, pressure, sound = primitives(fields, material(label))
    speed = sound + jnp.maximum(
        jnp.maximum(jnp.abs(velocity[0]), jnp.abs(velocity[1])), jnp.abs(velocity[2])
    )
    best = speed[:, :128]
    for start in range(128, speed.shape[1], 128):
        best = jnp.maximum(best, speed[:, start : start + 128])
    best = jnp.max(best, axis=0, keepdims=True)
    peak_ref[...] = jnp.broadcast_to(best, peak_ref.shape)


def x_kernel(own_ref, low_ref, high_ref, out_ref, flux_ref, line_ref):
    rows, nx = own_ref.shape[1:]
    total = rows + 2 * REACH
    stack = line_ref.shape[1]
    pos, count = lax.axis_index("aa"), lax.axis_size("aa")
    first, last = pos == 0, pos == count - 1
    for field in range(FIELDS + 1):
        own = own_ref[field]
        low = jnp.where(first, own[:1], low_ref[field, rows - REACH :])
        high = jnp.where(last, own[rows - 1 :], high_ref[field, :REACH])
        out_ref[field, :REACH] = low
        out_ref[field, REACH : REACH + rows] = own
        out_ref[field, REACH + rows : total] = high
        out_ref[field, total:] = jnp.zeros((out_ref.shape[1] - total, nx), jnp.float32)
    lane = lax.broadcasted_iota(jnp.int32, (total, nx), 1)
    wide = lax.broadcasted_iota(jnp.int32, (stack, nx), 1)
    for field in range(FIELDS + 1):
        cells = out_ref[field, :total]
        line_ref[field, :total] = cells
        line_ref[field, total : 2 * total] = jnp.where(
            lane == nx - 1, cells, pltpu.roll(cells, nx - 1, 1)
        )
        if stack > 2 * total:
            line_ref[field, 2 * total :] = jnp.zeros((stack - 2 * total, nx), jnp.float32)
    cache = {}

    def window(field, k):
        if (field, k) not in cache:
            if k == 3:
                value = line_ref[field]
            elif k < 3:
                near = window(field, k + 1)
                value = jnp.where(wide == 0, near, pltpu.roll(near, 1, 1))
            else:
                near = window(field, k - 1)
                value = jnp.where(wide == nx - 1, near, pltpu.roll(near, nx - 1, 1))
            cache[field, k] = value
        return cache[field, k]

    for slot, flux in enumerate(face_fluxes(window, 0)):
        line_ref[slot] = flux
    for slot in range(8):
        lower = line_ref[slot, :total]
        upper = line_ref[slot, total : 2 * total]
        flux_ref[slot, :total] = (
            jnp.where(lane == nx - 1, upper, pltpu.roll(lower, nx - 1, 1)) - lower
        )
        flux_ref[slot, total:] = jnp.zeros((flux_ref.shape[1] - total, nx), jnp.float32)


def step_of(peak_ref):
    best = jnp.max(peak_ref[...], axis=0, keepdims=True)
    return COURANT / jnp.max(best, axis=1, keepdims=True)


def y_kernel(peak_ref, cells_ref, change_ref, out_ref, step_ref, line_ref, face_ref):
    copies, _, rows, nx = out_ref.shape
    step = step_of(peak_ref)
    step_ref[...] = jnp.broadcast_to(step, step_ref.shape)
    label = cells_ref[FIELDS]
    fields = [cells_ref[field] for field in range(FIELDS)]
    for slot, field in enumerate(changed_fields(0)):
        fields[field] = fields[field] - step * change_ref[slot]
    fields = plastic(fields, label)
    height = label.shape[0]
    for field in range(FIELDS):
        line_ref[field, :height] = fields[field]
    line_ref[FIELDS, :height] = label
    faces = face_ref.shape[1]
    for field in range(FIELDS + 1):
        if line_ref.shape[1] > height:
            line_ref[field, height:] = jnp.zeros((line_ref.shape[1] - height, nx), jnp.float32)
    fluxes = face_fluxes(lambda field, k: line_ref[field, k : k + faces], 1)
    for slot in range(8):
        face_ref[slot] = fluxes[slot]
    label = line_ref[FIELDS, REACH : REACH + rows]
    fields = [line_ref[field, REACH : REACH + rows] for field in range(FIELDS)]
    for slot, field in enumerate(changed_fields(1)):
        change = face_ref[slot, 1 : rows + 1] - face_ref[slot, :rows]
        fields[field] = fields[field] - step * change
    fields = plastic(fields, label) + [label]
    for copy in range(copies):
        for field in range(FIELDS + 1):
            out_ref[copy, field] = fields[field]


def z_kernel(centred, step_ref, lines_ref, out_ref, line_ref):
    rows = out_ref.shape[2]
    pos, count = lax.axis_index("ba"), lax.axis_size("ba")
    step = step_ref[:rows, :1]
    for k in range(2 * REACH + 1):
        where = jnp.clip(pos + k - REACH, 0, count - 1)
        if centred:
            where = where - pos + REACH
        for field in range(FIELDS + 1):
            line_ref[field, k * rows : (k + 1) * rows] = lines_ref[where, field]
    fluxes = face_fluxes(
        lambda field, k: line_ref[field, k * rows : (k + 2) * rows], 2
    )
    centre = slice(REACH * rows, (REACH + 1) * rows)
    label = line_ref[FIELDS, centre]
    fields = [line_ref[field, centre] for field in range(FIELDS)]
    for slot, field in enumerate(changed_fields(2)):
        fields[field] = fields[field] - step * (fluxes[slot][rows:] - fluxes[slot][:rows])
    fields = plastic(fields, label)
    for field in range(FIELDS):
        out_ref[field, 0] = fields[field]


CHANGED = 8


def columns_kernel(
    state_ref, label_ref, out_ref, both_ref, stage_ref
):
    rows, nx = label_ref.shape[1:]
    label = label_ref[0]
    held = FIELDS * rows
    stage_ref[:held] = state_ref[...]
    stage_ref[held : held + rows] = label
    fields = [state_ref[field * rows : (field + 1) * rows] for field in range(FIELDS)]
    density, velocity, dev, pressure, sound = primitives(fields, material(label))
    speed = sound + jnp.maximum(
        jnp.maximum(jnp.abs(velocity[0]), jnp.abs(velocity[1])), jnp.abs(velocity[2])
    )
    used = (FIELDS + 1 + CHANGED) * rows
    stage_ref[used:] = jnp.broadcast_to(
        jnp.max(speed, keepdims=True), (stage_ref.shape[0] - used, nx)
    )
    pairs = [state_ref[field * rows : (field + 2) * rows] for field in range(0, FIELDS, 2)]
    for slot, change in enumerate(line_changes(pairs, both_ref, label, nx, 1, 0)):
        start = (FIELDS + 1 + slot) * rows
        stage_ref[start : start + rows] = change
    tall = stage_ref.shape[0]
    out_ref[:, :tall] = stage_ref[...].T


def line_changes(pairs, both_ref, label, group, width, d):
    tall, nx = pairs[0].shape
    rows = tall // 2
    lane = lax.broadcasted_iota(jnp.int32, (tall, nx), 1)

    def within(low, high):
        hit = lane < 0
        for start in range(0, nx, group):
            hit = hit | ((lane >= start + low * width) & (lane < start + high * width))
        return hit

    cells = group // width
    first = {n: within(0, n) for n in (1, 2, 3)}
    last = {n: within(cells - n, cells) for n in (1, 2)}
    ends = None
    for p, own in enumerate(pairs):
        moved = {n: pltpu.roll(own, n * width, 1) for n in {1, 2, 3, p + 1, p + 2, p + 3}}
        ahead = [pltpu.roll(own, nx - n * width, 1) for n in (1, 2)]
        low1 = jnp.where(first[1], own, moved[1])
        low2 = jnp.where(first[2], low1, moved[2])
        low3 = jnp.where(first[3], low2, moved[3])
        high1 = jnp.where(last[1], own, ahead[0])
        high2 = jnp.where(last[2], high1, ahead[1])
        values = weno_pair([low3, low2, low1, own, high1, high2])
        for side in range(2):
            both_ref[side, 2 * p, :rows] = values[side][:rows]
            both_ref[side, 2 * p + 1, :rows] = values[side][rows:]
        mine = [moved[p + 1 + n] for n in range(3)]
        if ends is None:
            ends = mine
        else:
            slot = within(p, p + 1)
            ends = [jnp.where(slot, new, old) for new, old in zip(mine, ends)]
    values = weno_pair([ends[2], ends[1], ends[0], ends[0], ends[0], ends[0]])
    for p in range(len(pairs)):
        for side in range(2):
            value = values[side]
            value = pltpu.roll(value, nx - p * width, 1) if p else value
            both_ref[side, 2 * p, rows:] = value[:rows]
            both_ref[side, 2 * p + 1, rows:] = value[rows:]
    left = [both_ref[0, field] for field in range(FIELDS)]
    right = [both_ref[1, field] for field in range(FIELDS)]
    kinds = jnp.concatenate([label, label], axis=0)
    before = pltpu.roll(kinds, width, 1)
    upper = lax.broadcasted_iota(jnp.int32, (tall, nx), 0) >= rows
    left_kinds = jnp.where(first[1] & jnp.logical_not(upper), kinds, before)
    fluxes = riemann(left, right, left_kinds, jnp.where(upper, before, kinds), d)
    start = first[1][:rows]
    changes = []
    for flux in fluxes:
        faces = jnp.where(start, flux[rows:], flux[:rows])
        changes.append(pltpu.roll(faces, nx - width, 1) - flux[:rows])
    return changes


def sweeps_kernel(rows, count_a, count_b, in_ref, out_ref, stage_ref, line_ref, face_ref, deep_ref, pack_ref, both_ref, pair_ref):
    nx = in_ref.shape[0]
    group = nx // count_a
    width = group // count_b
    tall = stage_ref.shape[0]
    stage_ref[...] = in_ref[:, :tall].T
    used = (FIELDS + 1 + CHANGED) * rows
    step = COURANT / jnp.max(in_ref[:, used : used + 1], axis=0, keepdims=True)

    def block(index):
        return stage_ref[index * rows : (index + 1) * rows, :]

    label = block(FIELDS)
    fields = [block(field) for field in range(FIELDS)]
    for slot, field in enumerate(changed_fields(0)):
        fields[field] = fields[field] - step * block(FIELDS + 1 + slot)

    lane = lax.broadcasted_iota(jnp.int32, (REACH, nx), 1)
    faces = rows + 1

    def lay(field, cells):
        low = pltpu.roll(cells, group, 1)[rows - REACH :]
        high = pltpu.roll(cells, nx - group, 1)[:REACH]
        line_ref[field, :REACH] = jnp.where(lane < group, cells[:1], low)
        line_ref[field, REACH : REACH + rows] = cells
        line_ref[field, REACH + rows : 2 * REACH + rows] = jnp.where(
            lane >= nx - group, cells[rows - 1 :], high
        )

    def window(field, k):
        return line_ref[field, k : k + faces]

    def pack(field):
        for k in range(6):
            pack_ref[k, field * faces : (field + 1) * faces] = window(field, k)

    lay(FIELDS, label)
    fields = plastic(fields, label)
    for field in range(FIELDS):
        lay(field, fields[field])
        pack(field)
    used = FIELDS * faces
    left, right = weno_pair([pack_ref[k, :used] for k in range(6)])
    both_ref[0, :used] = left
    both_ref[1, :used] = right
    values = [
        [both_ref[side, field * faces : (field + 1) * faces] for side in range(2)]
        for field in range(FIELDS)
    ]
    fluxes = face_fluxes(window, 1, values)
    for slot in range(CHANGED):
        face_ref[slot, :faces] = fluxes[slot]
    for slot, field in enumerate(changed_fields(1)):
        change = face_ref[slot, 1 : rows + 1] - face_ref[slot, :rows]
        fields[field] = fields[field] - step * change

    fields = plastic(fields, label)
    for field in range(FIELDS):
        pair_ref[field // 2, (field % 2) * rows : (field % 2 + 1) * rows] = fields[field]
    pairs = [pair_ref[p] for p in range(FIELDS // 2)]
    changes = line_changes(pairs, deep_ref, label, group, width, 2)
    for slot, field in enumerate(changed_fields(2)):
        fields[field] = fields[field] - step * changes[slot]
    fields = plastic(fields, label)
    for field in range(FIELDS):
        stage_ref[field * rows : (field + 1) * rows, :] = fields[field]
    tall = up8(FIELDS * rows)
    out_ref[:, :tall] = stage_ref[:tall].T


def home_kernel(in_ref, out_ref):
    held = out_ref.shape[0]
    out_ref[...] = in_ref[:, : up8(held)].T[:held]


def up8(size):
    return -(-size // 8) * 8


def call(kernel, outs, scratch, cost, name, space=pltpu.VMEM, fuse=None):
    vmem = pl.BlockSpec(memory_space=pltpu.VMEM)
    given = pl.BlockSpec(memory_space=space)
    shapes = [jax.ShapeDtypeStruct(shape, jnp.float32) for shape in outs]

    def run(*args):
        return pl.pallas_call(
            kernel,
            out_shape=shapes if len(shapes) > 1 else shapes[0],
            in_specs=[given] * len(args),
            out_specs=[vmem] * len(shapes) if len(shapes) > 1 else vmem,
            scratch_shapes=[
                pltpu.VMEM(shape, jnp.float32) if isinstance(shape, tuple) else shape
                for shape in scratch
            ],
            cost_estimate=pl.CostEstimate(flops=cost, bytes_accessed=cost // 4, transcendentals=0),
            name=name,
            compiler_params=pltpu.CompilerParams(vmem_limit_bytes=16 * 1024 * 1024, allow_input_fusion=fuse),
        )(*args)

    return run


def by_columns(state, labels):
    _, _, rows, nx = state.shape
    count_a, count_b = lax.axis_size("aa"), lax.axis_size("ba")
    devices = count_a * count_b
    used = (FIELDS + 1 + CHANGED) * rows + 1
    padded = -(-used // 128) * 128

    def swap(array):
        parts = array.reshape(devices, nx // devices, padded)
        return lax.all_to_all(parts, ("aa", "ba"), 0, 0, tiled=True).reshape(nx, padded)

    columns = call(
        columns_kernel,
        [(nx, padded)],
        [
            (2, FIELDS, 2 * rows, nx),
            (up8(used), nx),
        ],
        4_000_000,
        "columns",
        fuse=[False, True],
    )(state.reshape(FIELDS * rows, nx), labels.astype(jnp.float32))
    faces = up8(rows + 1)
    swept = call(
        functools.partial(sweeps_kernel, rows, count_a, count_b),
        [(nx, padded)],
        [
            (up8(used), nx),
            (FIELDS + 1, up8(2 * REACH + rows), nx),
            (CHANGED, faces, nx),
            (2, FIELDS, 2 * rows, nx),
            (6, up8(FIELDS * (rows + 1)), nx),
            (2, up8(FIELDS * (rows + 1)), nx),
            (FIELDS // 2, 2 * rows, nx),
        ],
        8_000_000,
        "sweeps",
    )(swap(columns))
    home = call(home_kernel, [(FIELDS * rows, nx)], [], 100_000, "home")
    return home(swap(swept)).reshape(state.shape)


def shards(state, labels):
    _, depth, rows, nx = state.shape
    assert depth == 1 and rows >= REACH and nx % 128 == 0
    count_a, count_b = lax.axis_size("aa"), lax.axis_size("ba")
    devices = count_a * count_b
    if nx % devices == 0 and count_b >= FIELDS // 2:
        return by_columns(state, labels)
    total = rows + 2 * REACH
    tall = up8(total)
    small = devices <= SMALL_GROUP
    peak, packed = call(
        peak_kernel,
        [(devices if small else 8, 128), (FIELDS + 1, rows, nx)],
        [],
        200_000,
        "peak",
    )(state, labels)
    ups = [(i, i + 1) for i in range(count_a - 1)]
    low = lax.ppermute(packed, "aa", ups)
    high = lax.ppermute(packed, "aa", [(j, i) for i, j in ups])
    if small:
        peaks = lax.all_to_all(peak, ("aa", "ba"), 0, 0, tiled=True)
    else:
        peaks = lax.pmax(peak, ("aa", "ba"))
    cells, change = call(
        x_kernel,
        [(FIELDS + 1, tall, nx), (8, tall, nx)],
        [(FIELDS + 1, up8(2 * total), nx)],
        4_000_000,
        "xflux",
    )(packed, low, high)
    exchange = count_b <= SMALL_AXIS
    faces = up8(rows + 1)
    after_y, step = call(
        y_kernel,
        [(count_b if exchange else 1, FIELDS + 1, rows, nx), (8, 128)],
        [(FIELDS + 1, max(tall, up8(2 * REACH - 1 + faces)), nx), (8, faces, nx)],
        4_000_000,
        "ysweep",
    )(peaks, cells, change)
    if exchange:
        lines = lax.all_to_all(after_y, "ba", 0, 0, tiled=True)
    else:
        near = []
        for shift in range(-REACH, REACH + 1):
            pairs = [(i, i - shift) for i in range(count_b) if 0 <= i - shift < count_b]
            near.append(lax.ppermute(after_y, "ba", pairs) if shift else after_y)
        lines = jnp.concatenate(near, axis=0)
    return call(
        functools.partial(z_kernel, not exchange),
        [(FIELDS, 1, rows, nx)],
        [(FIELDS + 1, (2 * REACH + 1) * rows, nx)],
        4_000_000,
        "zsweep",
    )(step, lines)


def solution(mesh):
    return jax.shard_map(
        shards,
        mesh=mesh,
        in_specs=(P(None, "ba", "aa", None), P("ba", "aa", None)),
        out_specs=P(None, "ba", "aa", None),
        check_vma=False,
    )
```
